32 devices in a mesh: gx: 8 (over y, x, core), gy: 4 (over z).
Axes of the slice: x: 2, y: 2, z: 4, core: 2. Of those that a mesh axis runs over, the one named last changes fastest.
Arguments:
- features: bfloat16 [128, 64, 8, 64], P('gx', 'gy'), may hold values from -6 to 6
- cotangent: bfloat16 [128, 64, 8, 64], P('gx', 'gy'), may hold values from -6 to 6
- spectral_weight: bfloat16 [32, 32, 4, 2, 64, 64], P('gx', 'gy'), may hold values from -0.75 to 0.75
- conv_weight: bfloat16 [64, 64], replicated, may hold values from -0.75 to 0.75
- modes_x: int32 [32], replicated, may hold values from 0 to 127, as said below
- modes_y: int32 [32], replicated, may hold values from 0 to 63, as said below
- modes_z: int32 [4], replicated, may hold values from 0 to 7, as said below
Outputs:
- activation: bfloat16 [128, 64, 8, 64], P('gx', 'gy')
- grad_features: bfloat16 [128, 64, 8, 64], P('gx', 'gy')
- grad_spectral: float32 [32, 32, 4, 2, 64, 64], P('gx', 'gy')
- grad_conv: float32 [64, 64], replicated
The draws below stay inside these ranges and needn't reach their ends.
Inputs may be any that keep to these rules, and one draw needn't show every extreme that they name: `modes_x`: 32 distinct frequencies. `modes_y`: 32 distinct frequencies. `modes_z`: 4 distinct frequencies.
All inputs are finite; a program needn't handle non-finite values.
Results may differ from the reference program's by a relative error of at most 0.0049.
Values may be sent and summed in bfloat16 or wider, within the bound.
No kernel may reach another device: no remote copies, remote signals or barrier semaphores. Data moves between devices by JAX's collectives and lax.ppermute only.
A program may use at most 64 MiB of HBM per device.

```python
import math
import jax
import jax.numpy as jnp
from jax import lax

C = 64
NZ = 8
MX = 32
MY = 32
MZ = 4
NX = 128
NY = 64


def pick_distinct(key, length, count):
    middle = jax.random.permutation(key, length - 2)[:count - 2].astype(jnp.int32) + 1
    ends = jnp.array([0, length - 1], dtype=jnp.int32)
    return jnp.concatenate([ends, middle])


def draw_modes_x(key, part):
    return pick_distinct(key, NX, MX)


def draw_modes_y(key, part):
    return pick_distinct(key, NY, MY)


def draw_modes_z(key, part):
    return pick_distinct(key, NZ, MZ)


def shard_levels(stream_key, shape, cuts, low, high):
    gain, own = 1.0, jax.random.fold_in(stream_key, 6)
    for position, parts in cuts:
        heights = jnp.exp(jax.random.uniform(jax.random.fold_in(own, position), (parts,), jnp.float32, low / len(cuts), high / len(cuts)))
        gain = gain * jnp.repeat(heights, shape[position] // parts).reshape([-1 if axis == position else 1 for axis in range(len(shape))])
    return gain


def normal_values(own_key, dims, scale, most, cuts=(), kind=jnp.bfloat16):
    values = scale * jax.random.normal(own_key, dims, jnp.float32)
    if cuts:
        values = values * shard_levels(own_key, dims, cuts, -0.22, 0.18)
    return jnp.clip(values, -most, most).astype(kind)


def setup_inputs(seed: int = 0) -> dict:
    key_list = jax.random.split(jax.random.key(seed), 8)
    features = normal_values(key_list[0], (NX, NY, NZ, C), 1.0, 6.0, ((0, 8), (1, 4)))
    cotangent = normal_values(key_list[1], (NX, NY, NZ, C), 1.0, 6.0, ((0, 8), (1, 4)))
    spectral_weight = normal_values(key_list[2], (MX, MY, MZ, 2, C, C), C ** -0.5, 0.75, ((0, 8), (1, 4)))
    conv_weight = normal_values(key_list[3], (C, C), C ** -0.5, 0.75)
    modes_x = draw_modes_x(jax.random.fold_in(key_list[7], 71), 0)
    modes_y = draw_modes_y(jax.random.fold_in(key_list[7], 71), 0)
    modes_z = draw_modes_z(jax.random.fold_in(key_list[7], 71), 0)
    return {"features": features, "cotangent": cotangent, "spectral_weight": spectral_weight, "conv_weight": conv_weight, "modes_x": modes_x, "modes_y": modes_y, "modes_z": modes_z}


HIGH = lax.Precision.HIGHEST

def phase_tables(freqs, places, length):
    product = freqs[:, None] * places[None, :] % length
    angles = product.astype(jnp.float32) * (2.0 * math.pi / length)
    return (jnp.cos(angles), jnp.sin(angles))

def to_modes(values, factor, modes_x, modes_y, modes_z):
    size_x, size_y, size_z, chans = values.shape
    cos_z, sin_z = phase_tables(modes_z, jnp.arange(size_z, dtype=jnp.int32), size_z)
    wide = values.astype(jnp.float32)
    plane_real = (factor * jnp.einsum('xyzc,kz->xykc', wide, cos_z, precision=HIGH)).reshape(size_x, size_y, -1)
    plane_imag = (-factor * jnp.einsum('xyzc,kz->xykc', wide, sin_z, precision=HIGH)).reshape(size_x, size_y, -1)
    cos_x, sin_x = phase_tables(modes_x, jnp.arange(size_x, dtype=jnp.int32), size_x)
    line_real = jnp.einsum('kx,xyq->kyq', cos_x, plane_real, precision=HIGH) + jnp.einsum('kx,xyq->kyq', sin_x, plane_imag, precision=HIGH)
    line_imag = jnp.einsum('kx,xyq->kyq', cos_x, plane_imag, precision=HIGH) - jnp.einsum('kx,xyq->kyq', sin_x, plane_real, precision=HIGH)
    cos_y, sin_y = phase_tables(modes_y, jnp.arange(size_y, dtype=jnp.int32), size_y)
    mode_real = jnp.einsum('ly,kyq->lkq', cos_y, line_real, precision=HIGH) + jnp.einsum('ly,kyq->lkq', sin_y, line_imag, precision=HIGH)
    mode_imag = jnp.einsum('ly,kyq->lkq', cos_y, line_imag, precision=HIGH) - jnp.einsum('ly,kyq->lkq', sin_y, line_real, precision=HIGH)
    return (mode_real, mode_imag)

def to_cells(mode_real, mode_imag, factor, size_x, size_y, size_z, modes_x, modes_y, modes_z):
    cos_y, sin_y = phase_tables(modes_y, jnp.arange(size_y, dtype=jnp.int32), size_y)
    line_real = jnp.einsum('ly,lkq->kyq', cos_y, mode_real, precision=HIGH) - jnp.einsum('ly,lkq->kyq', sin_y, mode_imag, precision=HIGH)
    line_imag = jnp.einsum('ly,lkq->kyq', cos_y, mode_imag, precision=HIGH) + jnp.einsum('ly,lkq->kyq', sin_y, mode_real, precision=HIGH)
    cos_x, sin_x = phase_tables(modes_x, jnp.arange(size_x, dtype=jnp.int32), size_x)
    plane_real = jnp.einsum('kx,kyq->xyq', cos_x, line_real, precision=HIGH) - jnp.einsum('kx,kyq->xyq', sin_x, line_imag, precision=HIGH)
    plane_imag = jnp.einsum('kx,kyq->xyq', cos_x, line_imag, precision=HIGH) + jnp.einsum('kx,kyq->xyq', sin_x, line_real, precision=HIGH)
    count_z = modes_z.shape[0]
    plane_real = plane_real.reshape(size_x, size_y, count_z, -1)
    plane_imag = plane_imag.reshape(size_x, size_y, count_z, -1)
    cos_z, sin_z = phase_tables(modes_z, jnp.arange(size_z, dtype=jnp.int32), size_z)
    return factor * (jnp.einsum('xykc,kz->xyzc', plane_real, cos_z, precision=HIGH) - jnp.einsum('xykc,kz->xyzc', plane_imag, sin_z, precision=HIGH))

def normal_cdf(values):
    return 0.5 * (1.0 + jax.scipy.special.erf(values * (1.0 / math.sqrt(2.0))))

def normal_pdf(values):
    return jnp.exp(-0.5 * values * values) * (1.0 / math.sqrt(2.0 * math.pi))

def reference(features, cotangent, spectral_weight, conv_weight, modes_x, modes_y, modes_z):
    size_x, size_y, size_z, chans = features.shape
    count_x, count_y, count_z = (modes_x.shape[0], modes_y.shape[0], modes_z.shape[0])
    first = 1.0 / math.sqrt(size_x * size_y * size_z)
    second = 1.0 / math.sqrt(count_x * count_y * count_z)
    spec_real, spec_imag = to_modes(features, first, modes_x, modes_y, modes_z)
    spec_real = spec_real.reshape(count_y, count_x, count_z, chans)
    spec_imag = spec_imag.reshape(count_y, count_x, count_z, chans)
    weight = spectral_weight.astype(jnp.float32)
    real_w = weight[:, :, :, 0]
    imag_w = weight[:, :, :, 1]
    form = 'abzoi,bazi->bazo'
    mixed_real = jnp.einsum(form, real_w, spec_real, precision=HIGH) - jnp.einsum(form, imag_w, spec_imag, precision=HIGH)
    mixed_imag = jnp.einsum(form, real_w, spec_imag, precision=HIGH) + jnp.einsum(form, imag_w, spec_real, precision=HIGH)
    spectral = to_cells(mixed_real.reshape(count_y, count_x, -1), mixed_imag.reshape(count_y, count_x, -1), second, size_x, size_y, size_z, modes_x, modes_y, modes_z)
    flat = features.reshape(-1, chans)
    conv = jnp.dot(flat, conv_weight, preferred_element_type=jnp.float32).reshape(spectral.shape)
    pre = spectral + conv
    cdf = normal_cdf(pre)
    activation = (pre * cdf).astype(jnp.bfloat16)
    slope = (cotangent.astype(jnp.float32) * (cdf + pre * normal_pdf(pre))).astype(jnp.bfloat16)
    back_real, back_imag = to_modes(slope, second, modes_x, modes_y, modes_z)
    back_real = back_real.reshape(count_y, count_x, count_z, chans)
    back_imag = back_imag.reshape(count_y, count_x, count_z, chans)
    outer = 'bazo,bazi->abzoi'
    grad_real = jnp.einsum(outer, back_real, spec_real, precision=HIGH) + jnp.einsum(outer, back_imag, spec_imag, precision=HIGH)
    grad_imag = jnp.einsum(outer, back_imag, spec_real, precision=HIGH) - jnp.einsum(outer, back_real, spec_imag, precision=HIGH)
    grad_spectral = jnp.stack([grad_real, grad_imag], axis=3)
    adjoint = 'abzoi,bazo->bazi'
    modes_real = jnp.einsum(adjoint, real_w, back_real, precision=HIGH) + jnp.einsum(adjoint, imag_w, back_imag, precision=HIGH)
    modes_imag = jnp.einsum(adjoint, real_w, back_imag, precision=HIGH) - jnp.einsum(adjoint, imag_w, back_real, precision=HIGH)
    spectral_back = to_cells(modes_real.reshape(count_y, count_x, -1), modes_imag.reshape(count_y, count_x, -1), first, size_x, size_y, size_z, modes_x, modes_y, modes_z)
    slope_flat = slope.reshape(-1, chans)
    conv_back = jnp.dot(slope_flat, conv_weight.T, preferred_element_type=jnp.float32).reshape(spectral.shape)
    grad_features = (spectral_back + conv_back).astype(jnp.bfloat16)
    grad_conv = first * jnp.dot(flat.T, slope_flat, preferred_element_type=jnp.float32)
    return (activation, grad_features, grad_spectral, grad_conv)
```

```python
import math

import jax
import jax.numpy as jnp
from jax import lax
from jax.experimental import pallas as pl
from jax.experimental.pallas import tpu as pltpu
from jax.sharding import PartitionSpec as P

HIGH = lax.Precision.HIGHEST
BF = jnp.bfloat16
F32 = jnp.float32
LANES = 128
EXTRA = 16
WIDE = 1024


def steps_of(parts):
    return list(range(0, parts, 2)) + list(range(1, parts, 2))


def cosine(turns, length):
    half = length // 2
    place = ((turns + length // 4) & (length - 1)) - half
    place = jnp.minimum(jnp.maximum(place, -half - place), half - place)
    angle = place.astype(F32) * (-2.0 * math.pi / length)
    square = angle * angle
    series = 1.0 / 362880.0 - square * (1.0 / 39916800.0)
    series = square * series - 1.0 / 5040.0
    series = square * series + 1.0 / 120.0
    series = square * series - 1.0 / 6.0
    return angle + angle * (square * series)


def pick(ref, index, places):
    out = jnp.zeros(index.shape, jnp.int32)
    for k, place in enumerate(places):
        out = jnp.where(index == k, ref[place], out)
    return out


def store_halves(ref, row, value):
    high = value.astype(BF)
    tall = ref.shape[0] // 2
    ref[row : row + value.shape[0]] = high
    ref[tall + row : tall + row + value.shape[0]] = (value - high.astype(F32)).astype(BF)


def grid_of(rows, cols):
    return (
        lax.broadcasted_iota(jnp.int32, (rows, cols), 0),
        lax.broadcasted_iota(jnp.int32, (rows, cols), 1),
    )


def table_kernel(size_z, *refs):
    sources, outs, places, sems = refs[:4], refs[5:11], refs[11:15], refs[15]
    line_ref, column_ref, cback_ref, lback_ref, pair_ref, turn_ref = outs
    copies = [
        pltpu.make_async_copy(source, place, sems.at[k])
        for k, (source, place) in enumerate(zip(sources, places))
    ]
    for copy in copies:
        copy.start()
    for copy in copies:
        copy.wait()
    mx_ref, my_ref, mz_ref, conv_ref = places
    parts_x, parts_y = lax.axis_size("gx"), lax.axis_size("gy")
    me_x, me_y = lax.axis_index("gx"), lax.axis_index("gy")
    count_x, count_y, count_z = mx_ref.shape[0], my_ref.shape[0], mz_ref.shape[0]
    local_x, local_y = count_x // parts_x, count_y // parts_y
    chans = conv_ref.shape[0]
    block = chans // parts_x
    length_x = line_ref.shape[1] // size_z
    whole = line_ref.shape[1]
    tile = 16

    row, col = grid_of(tile, whole)
    per = tile // count_z
    x, z = col // size_z, col % size_z
    base = pick(mz_ref, row % count_z, range(count_z)) * z * length_x
    x = x * size_z
    inner = row // count_z
    for part in range(2):
        for start in range(0, count_x, per):
            turns = pick(mx_ref, inner, range(start, start + per)) * x + base
            at = part * count_x * count_z + start * count_z
            store_halves(line_ref, at, cosine(turns + part * (whole // 4), whole))

    rows_y = column_ref.shape[0] // 4 // block
    length_y = rows_y * parts_y
    row, col = grid_of(tile, column_ref.shape[1])
    per = tile // block
    wide = local_y * block
    freq = pick(my_ref, col // (2 * wide) * local_y + col // block % local_y, range(count_y))
    shift = col // wide % 2 * (length_y // 4)
    same = row % block == col % block
    inner = row // block + me_y * rows_y
    for part in range(2):
        for start in range(0, rows_y, per):
            turns = freq * (inner + start) + shift - part * (length_y // 4)
            value = jnp.where(same, cosine(turns, length_y), 0.0)
            store_halves(column_ref, part * rows_y * block + start * block, value)

    row, col = grid_of(2 * rows_y, cback_ref.shape[1])
    places = [
        (me_y + parts_y - step) % parts_y * local_y + k for step in range(parts_y) for k in range(local_y)
    ]
    freq = pick(my_ref, col // (2 * local_y) * local_y + col % local_y, places)
    shift = (col // local_y % 2 - row // rows_y) * (length_y // 4)
    store_halves(cback_ref, 0, cosine(freq * (row % rows_y + me_y * rows_y) + shift, length_y))

    row, col = grid_of(tile, lback_ref.shape[1])
    modes = local_x * count_z
    kx = col // (2 * modes) * local_x + col // count_z % local_x
    places = [(me_x ^ step) * local_x + k for step in steps_of(parts_x) for k in range(local_x)]
    freq = pick(mx_ref, kx, places) * size_z
    base = pick(mz_ref, col % count_z, range(count_z)) * (row % size_z) * length_x
    base = base + col // modes % 2 * (whole // 4)
    rows_x = length_x // parts_x
    inner = row // size_z + me_x * rows_x
    per = tile // size_z
    for start in range(0, rows_x, per):
        store_halves(lback_ref, start * size_z, cosine(freq * (inner + start) + base, whole))

    conv = conv_ref[...].astype(F32)
    none = jnp.zeros_like(conv)
    for ref, value in ((pair_ref, conv), (turn_ref, conv.T)):
        ref[:chans] = jnp.concatenate([value, none], axis=1).astype(BF)
        ref[chans:] = jnp.concatenate([none, value], axis=1).astype(BF)


def dot(a, b, dims=((1,), (0,))):
    return lax.dot_general(a, b, (dims, ((), ())), preferred_element_type=F32)


def pairs_of(ref):
    size_x, size_y, size_z, chans = ref.shape
    out = []
    for y in range(size_y // 2):
        low = ref[:, y, :, :].astype(F32).reshape(size_x * size_z, chans)
        high = ref[:, y + size_y // 2, :, :].astype(F32).reshape(size_x * size_z, chans)
        out.append(jnp.concatenate([low, high], axis=1))
    return out


def block_transpose(arrays, block):
    count = len(arrays)
    arrays = list(arrays)
    lanes = arrays[0].shape[1]
    index = lax.broadcasted_iota(jnp.int32, arrays[0].shape, 1) // block % count
    step = 1
    while step < count:
        upper = (index & step) != 0
        for p in range(count):
            if p & step:
                continue
            a, b = arrays[p], arrays[p | step]
            arrays[p] = jnp.where(upper, pltpu.roll(b, step * block, 1), a)
            arrays[p | step] = jnp.where(upper, b, pltpu.roll(a, lanes - step * block, 1))
        step *= 2
    return arrays


def split_rows(value):
    high = value.astype(BF)
    return jnp.concatenate([high, (value - high.astype(F32)).astype(BF)], axis=0)


def normal_cdf(values):
    return 0.5 * (1.0 + lax.erf(values * (1.0 / math.sqrt(2.0))))


def normal_pdf(values):
    return jnp.exp(-0.5 * values * values) * (1.0 / math.sqrt(2.0 * math.pi))


def spread_kernel(field_ref, send_ref, pairs_ref):
    size_x, _, size_z, chans = field_ref.shape
    step = 4
    for x in range(0, size_x, step):
        rows = slice(x * size_z, (x + step) * size_z)
        pairs = pairs_of(field_ref.at[pl.ds(x, step)])
        for p, pair in enumerate(pairs):
            pairs_ref[p, rows] = pair.astype(BF)
        for b, chunk in enumerate(block_transpose(pairs, chans // len(pairs))):
            send_ref[b, rows] = chunk.astype(BF)


def pairs_kernel(field_ref, pairs_ref):
    for p, pair in enumerate(pairs_of(field_ref)):
        pairs_ref[p] = pair.astype(BF)


def joined(value):
    chans = value.shape[1] // 2
    return value[:, :chans].astype(F32) + value[:, chans:].astype(F32)


def parted(value):
    high = value.astype(BF).astype(F32)
    both = jnp.concatenate([high, value - high], axis=1)
    rest = jnp.zeros((EXTRA - both.shape[0], both.shape[1]), F32)
    return jnp.concatenate([both, rest], axis=0).astype(BF)


def transform_kernel(scale, parts_y, line_ref, column_ref, recv_ref, send_ref, *extra):
    parts_x, tall_in, lanes = recv_ref.shape
    rows = line_ref.shape[1] // parts_x
    if extra:
        total = joined(recv_ref[0, rows:, :])
        for gx in range(1, parts_x):
            total = total + joined(recv_ref[gx, rows:, :])
        extra[0][...] = parted(total[: lanes // 2 // parts_x])
    data = recv_ref[:, :rows, :].reshape(parts_x * rows, lanes)
    lines = dot(line_ref[...], data)
    half = lines.shape[0] // 2
    lines = lines[:half] + lines[half:]
    count = half // 2
    both = jnp.concatenate([lines[:count], lines[count:]], axis=1)
    depth = both.shape[1]
    high = both.astype(BF)
    low = (both - high.astype(F32)).astype(BF)
    modes = dot(split_rows(both), column_ref[:depth, :])
    modes = modes[:count] + modes[count:] + dot(high, column_ref[depth:, :])
    modes = modes * scale
    tall = count // parts_x
    for gx in range(parts_x):
        for gy in range(parts_y):
            send_ref[gx * parts_y + gy] = modes[
                gx * tall : (gx + 1) * tall, gy * LANES : (gy + 1) * LANES
            ].astype(BF)


def sum_parts(recv_ref, parts_y):
    parts = recv_ref.shape[0] // parts_y
    out = []
    for b in range(parts):
        total = recv_ref[b * parts_y].astype(F32)
        for gy in range(1, parts_y):
            total = total + recv_ref[b * parts_y + gy].astype(F32)
        out.append(total)
    return out


def lay_modes(scratch, send_ref, count_y, rows):
    chans = 64
    for m in range(0, rows, 2):
        parts = []
        for part in range(2):
            first = scratch[pl.ds(part * rows + m, count_y, stride=2 * rows), :chans]
            second = scratch[pl.ds(part * rows + m + 1, count_y, stride=2 * rows), :chans]
            parts.append(jnp.concatenate([first, second], axis=1))
        send_ref[:, m * chans : (m + 2) * chans] = jnp.concatenate(parts, axis=0)


def mix_kernel(forward, parts_y, recv_ref, weight_ref, *refs):
    send_ref, spec_ref, scratch = refs[-3:]
    if len(refs) == 4:
        send_ref[:, WIDE:] = refs[0][...].astype(F32)
    size_x, size_y, size_z, _, chans, _ = weight_ref.shape
    rows = size_x * size_z
    spectra = block_transpose(sum_parts(recv_ref, parts_y), chans // size_y)
    for ky in range(size_y):
        spec = spectra[ky]
        spec_ref[ky] = spec
        turned = pltpu.roll(spec, chans, 1)
        if forward:
            both = jnp.concatenate([spec, turned], axis=0)[:, :chans].T
            high = both.astype(BF)
            both = jnp.concatenate([high, (both - high.astype(F32)).astype(BF)], axis=1)
        else:
            first = lax.broadcasted_iota(jnp.int32, spec.shape, 1) < chans
            both = split_rows(jnp.concatenate([spec, jnp.where(first, turned, -turned)], axis=0))
        mode = lax.broadcasted_iota(jnp.int32, both.shape, 1 if forward else 0) % rows
        total = jnp.zeros((2 * chans, 4 * rows) if forward else (4 * rows, chans), F32)
        for m in range(rows):
            weight = weight_ref[m // size_z, ky, m % size_z].reshape(2 * chans, chans)
            own = jnp.where(mode == m, both, jnp.zeros_like(both))
            total = total + (dot(weight, own) if forward else dot(own, weight))
        if forward:
            total = total.T
        total = total[: 2 * rows] + total[2 * rows :]
        if forward:
            real, imag = total[:rows], total[rows:]
            mixed = jnp.concatenate(
                [
                    real[:, :chans] - imag[:, chans:],
                    imag[:, :chans] + real[:, chans:],
                ],
                axis=0,
            )
        else:
            mixed = total
        scratch[ky * 2 * rows : (ky + 1) * 2 * rows, :chans] = mixed
    lay_modes(scratch, send_ref, size_y, rows)


def column_kernel(table_ref, *refs):
    steps = len(refs) - 2
    send_ref, scratch = refs[steps], refs[steps + 1]
    chans = 64
    if refs[0].shape[1] > WIDE:
        total = joined(refs[0][:, WIDE:])
        for s in range(1, steps):
            total = total + joined(refs[s][:, WIDE:])
        send_ref[:EXTRA, WIDE:] = parted(total[: EXTRA // 2])
        send_ref[EXTRA:, WIDE:] = jnp.zeros((send_ref.shape[0] - EXTRA, LANES), BF)
    data = jnp.concatenate([refs[s][:, :WIDE] for s in range(steps)], axis=0)
    high = data.astype(BF)
    low = (data - high.astype(F32)).astype(BF)
    lines = dot(table_ref[...], high)
    half = lines.shape[0] // 2
    lines = lines[:half] + lines[half:] + dot(table_ref[:half, :], low)
    size_y = half // 2
    count = WIDE // chans
    for m in range(0, count, 2):
        pair = lines[:, m * chans : (m + 2) * chans]
        scratch[m * half : (m + 1) * half, :] = pair
        scratch[(m + 1) * half : (m + 2) * half, :] = pltpu.roll(pair, chans, 1)
    for part in range(2):
        for y in range(size_y // 2):
            first = scratch[pl.ds(part * size_y + y, count, stride=half), :chans]
            second = scratch[pl.ds(part * size_y + y + size_y // 2, count, stride=half), :chans]
            send_ref[part * count : (part + 1) * count, y * 2 * chans : (y + 1) * 2 * chans] = (
                jnp.concatenate([first, second], axis=1).astype(BF)
            )


def cells_of(table_ref, recv_refs, scale):
    data = jnp.concatenate([ref[:, :WIDE] for ref in recv_refs], axis=0)
    cells = dot(table_ref[...], data)
    half = cells.shape[0] // 2
    return (cells[:half] + cells[half:]) * scale


def store_pair(out_ref, p, value):
    size_x, size_y, size_z, chans = out_ref.shape
    out_ref[:, p, :, :] = value[:, :chans].reshape(size_x, size_z, chans).astype(out_ref.dtype)
    out_ref[:, p + size_y // 2, :, :] = (
        value[:, chans:].reshape(size_x, size_z, chans).astype(out_ref.dtype)
    )


def point_kernel(scale, table_ref, *refs):
    conv_ref, field_ref, cot_ref, act_ref, slope_ref, send_ref = refs[-6:]
    cells = cells_of(table_ref, refs[:-6], scale)
    count = field_ref.shape[0]
    slopes = []
    grad = jnp.zeros((LANES, LANES), F32)
    for p in range(count):
        field = field_ref[p]
        pre = cells[:, p * LANES : (p + 1) * LANES] + dot(field, conv_ref[...])
        cdf = normal_cdf(pre)
        store_pair(act_ref, p, pre * cdf)
        slope = cot_ref[p].astype(F32) * (cdf + pre * normal_pdf(pre))
        narrow = slope.astype(BF)
        slope_ref[p] = narrow
        slopes.append(narrow.astype(F32))
        grad = grad + dot(field, narrow, ((0,), (0,)))
    rows = slopes[0].shape[0]
    chans = LANES // 2
    grad = grad[:chans, :chans] + grad[chans:, chans:]
    block = chans // count
    for b, chunk in enumerate(block_transpose(slopes, block)):
        send_ref[b, :rows, :] = chunk.astype(BF)
        send_ref[b, rows:, :] = parted(grad[b * block : (b + 1) * block])


def last_kernel(scale, table_ref, *refs):
    conv_ref, slope_ref, out_ref, grad_ref = refs[-4:]
    recv_refs = refs[:-4]
    block = grad_ref.shape[0] // len(recv_refs)
    me = lax.axis_index("gx")
    for step, ref in zip(steps_of(len(recv_refs)), recv_refs):
        total = joined(ref[:EXTRA, WIDE:])
        grad_ref[pl.ds(pl.multiple_of((me ^ step) * block, block), block), :] = total[:block] * scale
    cells = cells_of(table_ref, recv_refs, scale)
    for p in range(slope_ref.shape[0]):
        store_pair(out_ref, p, cells[:, p * LANES : (p + 1) * LANES] + dot(slope_ref[p], conv_ref[...]))


def outer_kernel(spec_ref, back_ref, out_ref):
    size_x, size_y, size_z, _, chans, _ = out_ref.shape
    rows = size_x * size_z
    first = lax.broadcasted_iota(jnp.int32, back_ref.shape[1:], 1) < chans
    mode = lax.broadcasted_iota(jnp.int32, (6 * rows, chans), 0) % rows
    for ky in range(size_y):
        back, spec = back_ref[ky], spec_ref[ky]
        turned = pltpu.roll(back, chans, 1)
        left = jnp.concatenate([back, jnp.where(first, turned, -turned)], axis=0).T
        right = jnp.concatenate([spec, pltpu.roll(spec, chans, 1)], axis=0)[:, :chans]
        left_high, right_high = left.astype(BF), right.astype(BF)
        left_low = (left - left_high.astype(F32)).astype(BF)
        right_low = (right - right_high.astype(F32)).astype(BF)
        lefts = jnp.concatenate([left_high, left_high, left_low], axis=1)
        rights = jnp.concatenate([right_high, right_low, right_high], axis=0)
        for m in range(rows):
            own = jnp.where(mode == m, rights, jnp.zeros_like(rights))
            out_ref[m // size_z, ky, m % size_z] = dot(lefts, own).reshape(2, chans, chans)


def call(kernel, outs, *args, scratch=()):
    params = pltpu.CompilerParams(vmem_limit_bytes=16 * 2**20)
    return pl.pallas_call(kernel, out_shape=outs, scratch_shapes=list(scratch), compiler_params=params)(*args)


def bind(kernel, *static):
    def bound(*refs):
        return kernel(*static, *refs)

    return bound


def sds(shape, dtype):
    return jax.ShapeDtypeStruct(shape, dtype)


def fast(features, cotangent, spectral_weight, conv_weight, modes_x, modes_y, modes_z):
    rows_x, rows_y, size_z, chans = features.shape
    local_x, local_y, count_z = spectral_weight.shape[:3]
    parts_x, parts_y = lax.axis_size("gx"), lax.axis_size("gy")
    length_x, length_y = rows_x * parts_x, rows_y * parts_y
    block = chans // parts_x
    cells = rows_x * size_z
    modes = local_x * count_z
    half_y = rows_y // 2
    first = 1.0 / math.sqrt(length_x * length_y * size_z)
    second = 1.0 / math.sqrt(modes_x.shape[0] * modes_y.shape[0] * count_z)

    send, field = call(
        spread_kernel,
        (sds((parts_x, cells, LANES), BF), sds((half_y, cells, LANES), BF)),
        features,
    )
    cot = call(pairs_kernel, sds((half_y, cells, LANES), BF), cotangent)
    outside = pl.BlockSpec(memory_space=pltpu.HBM)
    inside = pl.BlockSpec(memory_space=pltpu.VMEM)
    line_table, column_table, column_back, line_back, conv_pair, conv_turn = pl.pallas_call(
        bind(table_kernel, size_z),
        in_specs=[outside] * 4 + [inside],
        out_shape=(
            sds((4 * modes_x.shape[0] * count_z, length_x * size_z), BF),
            sds((4 * LANES, 4 * LANES), BF),
            sds((4 * rows_y, 2 * modes_y.shape[0]), BF),
            sds((2 * cells, 2 * modes_x.shape[0] * count_z), BF),
            sds((LANES, LANES), BF),
            sds((LANES, LANES), BF),
        ),
        scratch_shapes=[
            pltpu.SMEM(modes_x.shape, jnp.int32),
            pltpu.SMEM(modes_y.shape, jnp.int32),
            pltpu.SMEM(modes_z.shape, jnp.int32),
            pltpu.VMEM(conv_weight.shape, BF),
            pltpu.SemaphoreType.DMA((4,)),
        ],
        compiler_params=pltpu.CompilerParams(vmem_limit_bytes=16 * 2**20),
    )(*(pltpu.with_memory_space_constraint(x, pltpu.HBM) for x in (modes_x, modes_y, modes_z, conv_weight)), spectral_weight)

    def to_modes(send, factor, extra):
        recv = lax.all_to_all(send, "gx", 0, 0, tiled=True)
        outs = [sds((parts_x * parts_y, modes, LANES), BF)]
        if extra:
            outs.append(sds((EXTRA, LANES), BF))
        send, *rest = call(bind(transform_kernel, factor, parts_y), outs, line_table, column_table, recv)
        return lax.all_to_all(send, ("gx", "gy"), 0, 0, tiled=True), rest

    def mix(recv, forward, rest):
        return call(
            bind(mix_kernel, forward, parts_y),
            (
                sds((2 * local_y, WIDE + len(rest) * LANES), F32),
                sds((local_y, modes, LANES), F32),
            ),
            recv,
            spectral_weight,
            *rest,
            scratch=[pltpu.VMEM((local_y * 2 * modes, LANES), F32)],
        )

    def to_lines(send, beside=None):
        pieces = [send]
        for step in range(1, parts_y):
            ring = [(i, (i + step) % parts_y) for i in range(parts_y)]
            pieces.append(lax.ppermute(send, "gy", ring))
        if beside is not None:
            pieces[-1], beside = lax.optimization_barrier((pieces[-1], beside))
        lines = call(
            column_kernel,
            sds((2 * modes, send.shape[1]), BF),
            column_back,
            *pieces,
            scratch=[pltpu.VMEM((modes * 2 * rows_y, LANES), F32)],
        )
        pieces = [lines]
        for step in range(2, parts_x, 2):
            pieces.append(lax.ppermute(lines, "gx", [(i, i ^ step) for i in range(parts_x)]))
        swap = [(i, i ^ 1) for i in range(parts_x)]
        return pieces + [lax.ppermute(piece, "gx", swap) for piece in pieces], beside

    recv, _ = to_modes(send, first, False)
    send, spec = mix(recv, True, [])
    pieces, _ = to_lines(send)
    activation, slope, send = call(
        bind(point_kernel, second),
        (
            sds(features.shape, BF),
            sds((half_y, cells, LANES), BF),
            sds((parts_x, cells + EXTRA, LANES), BF),
        ),
        line_back,
        *pieces,
        conv_pair,
        field,
        cot,
    )
    recv, rest = to_modes(send, second, True)
    send, back = mix(recv, False, rest)
    grad_spectral = call(outer_kernel, sds(spectral_weight.shape, F32), spec, back)
    pieces, grad_spectral = to_lines(send, grad_spectral)
    grad_features, grad_conv = call(
        bind(last_kernel, first),
        (sds(features.shape, BF), sds((chans, chans), F32)),
        line_back,
        *pieces,
        conv_turn,
        slope,
    )
    return activation, grad_features, grad_spectral, grad_conv


def phase_tables(freqs, places, length):
    product = freqs[:, None] * places[None, :] % length
    angles = product.astype(jnp.float32) * (2.0 * math.pi / length)
    return (jnp.cos(angles), jnp.sin(angles))


def plane_modes(values, factor, modes_z):
    size_x, size_y, size_z, chans = values.shape
    cos_z, sin_z = phase_tables(modes_z, jnp.arange(size_z, dtype=jnp.int32), size_z)
    wide = values.astype(jnp.float32)
    plane_real = (factor * jnp.einsum("xyzc,kz->xykc", wide, cos_z, precision=HIGH)).reshape(
        size_x, size_y, -1
    )
    plane_imag = (-factor * jnp.einsum("xyzc,kz->xykc", wide, sin_z, precision=HIGH)).reshape(
        size_x, size_y, -1
    )
    return (plane_real, plane_imag)


def line_modes(plane_real, plane_imag, freqs, places, length):
    cos_x, sin_x = phase_tables(freqs, places, length)
    line_real = jnp.einsum("kx,xyq->kyq", cos_x, plane_real, precision=HIGH) + jnp.einsum(
        "kx,xyq->kyq", sin_x, plane_imag, precision=HIGH
    )
    line_imag = jnp.einsum("kx,xyq->kyq", cos_x, plane_imag, precision=HIGH) - jnp.einsum(
        "kx,xyq->kyq", sin_x, plane_real, precision=HIGH
    )
    return jnp.stack([line_real, line_imag], axis=1)


def to_modes(values, factor, modes_x, modes_y, modes_z):
    rows_x, rows_y = (values.shape[0], values.shape[1])
    parts_x = lax.axis_size("gx")
    parts_y = lax.axis_size("gy")
    length_x = rows_x * parts_x
    length_y = rows_y * parts_y
    pencil = lax.all_to_all(values, "gx", split_axis=1, concat_axis=0, tiled=True)
    plane_real, plane_imag = plane_modes(pencil, factor, modes_z)
    whole = line_modes(
        plane_real, plane_imag, modes_x, jnp.arange(length_x, dtype=jnp.int32), length_x
    )
    spectrum = lax.all_to_all(whole, "gx", split_axis=0, concat_axis=2, tiled=True)
    places_y = lax.axis_index("gy") * rows_y + jnp.arange(rows_y, dtype=jnp.int32)
    cos_y, sin_y = phase_tables(modes_y, places_y, length_y)
    mode_real = jnp.einsum("ly,kyq->lkq", cos_y, spectrum[:, 0], precision=HIGH) + jnp.einsum(
        "ly,kyq->lkq", sin_y, spectrum[:, 1], precision=HIGH
    )
    mode_imag = jnp.einsum("ly,kyq->lkq", cos_y, spectrum[:, 1], precision=HIGH) - jnp.einsum(
        "ly,kyq->lkq", sin_y, spectrum[:, 0], precision=HIGH
    )
    return lax.psum_scatter(
        jnp.stack([mode_real, mode_imag], axis=2), "gy", scatter_dimension=0, tiled=True
    )


def to_cells(spectrum, factor, rows_x, rows_y, size_z, modes_x, modes_y, modes_z):
    length_x = rows_x * lax.axis_size("gx")
    length_y = rows_y * lax.axis_size("gy")
    places_y = lax.axis_index("gy") * rows_y + jnp.arange(rows_y, dtype=jnp.int32)
    places_x = lax.axis_index("gx") * rows_x + jnp.arange(rows_x, dtype=jnp.int32)
    piece = lax.all_gather(spectrum, "gy", axis=0, tiled=True)
    freqs = modes_y
    cos_y, sin_y = phase_tables(freqs, places_y, length_y)
    line_real = jnp.einsum("ly,lkq->kyq", cos_y, piece[:, :, 0], precision=HIGH) - jnp.einsum(
        "ly,lkq->kyq", sin_y, piece[:, :, 1], precision=HIGH
    )
    line_imag = jnp.einsum("ly,lkq->kyq", cos_y, piece[:, :, 1], precision=HIGH) + jnp.einsum(
        "ly,lkq->kyq", sin_y, piece[:, :, 0], precision=HIGH
    )
    line_real, line_imag = (line_real, line_imag)
    lines = jnp.stack([line_real, line_imag], axis=1)
    piece = lax.all_gather(lines, "gx", axis=0, tiled=True)
    freqs = modes_x
    cos_x, sin_x = phase_tables(freqs, places_x, length_x)
    plane_real = jnp.einsum("kx,kyq->xyq", cos_x, piece[:, 0], precision=HIGH) - jnp.einsum(
        "kx,kyq->xyq", sin_x, piece[:, 1], precision=HIGH
    )
    plane_imag = jnp.einsum("kx,kyq->xyq", cos_x, piece[:, 1], precision=HIGH) + jnp.einsum(
        "kx,kyq->xyq", sin_x, piece[:, 0], precision=HIGH
    )
    plane_real, plane_imag = (plane_real, plane_imag)
    count_z = modes_z.shape[0]
    plane_real = plane_real.reshape(rows_x, rows_y, count_z, -1)
    plane_imag = plane_imag.reshape(rows_x, rows_y, count_z, -1)
    cos_z, sin_z = phase_tables(modes_z, jnp.arange(size_z, dtype=jnp.int32), size_z)
    return factor * (
        jnp.einsum("xykc,kz->xyzc", plane_real, cos_z, precision=HIGH)
        - jnp.einsum("xykc,kz->xyzc", plane_imag, sin_z, precision=HIGH)
    )


def plain(features, cotangent, spectral_weight, conv_weight, modes_x, modes_y, modes_z):
    rows_x, rows_y, size_z, chans = features.shape
    count_x, count_y, count_z = (modes_x.shape[0], modes_y.shape[0], modes_z.shape[0])
    length_x = rows_x * lax.axis_size("gx")
    length_y = rows_y * lax.axis_size("gy")
    first = 1.0 / math.sqrt(length_x * length_y * size_z)
    second = 1.0 / math.sqrt(count_x * count_y * count_z)
    spectrum = to_modes(features, first, modes_x, modes_y, modes_z)
    local_y, local_x = (spectrum.shape[0], spectrum.shape[1])
    spec_real = spectrum[:, :, 0].reshape(local_y, local_x, count_z, chans)
    spec_imag = spectrum[:, :, 1].reshape(local_y, local_x, count_z, chans)
    weight = spectral_weight.astype(jnp.float32)
    real_w = weight[:, :, :, 0]
    imag_w = weight[:, :, :, 1]
    form = "abzoi,bazi->bazo"
    mixed_real = jnp.einsum(form, real_w, spec_real, precision=HIGH) - jnp.einsum(
        form, imag_w, spec_imag, precision=HIGH
    )
    mixed_imag = jnp.einsum(form, real_w, spec_imag, precision=HIGH) + jnp.einsum(
        form, imag_w, spec_real, precision=HIGH
    )
    mixed = jnp.stack(
        [mixed_real.reshape(local_y, local_x, -1), mixed_imag.reshape(local_y, local_x, -1)], axis=2
    )
    spectral = to_cells(mixed, second, rows_x, rows_y, size_z, modes_x, modes_y, modes_z)
    flat = features.reshape(-1, chans)
    conv = jnp.dot(flat, conv_weight, preferred_element_type=jnp.float32).reshape(spectral.shape)
    pre = spectral + conv
    cdf = normal_cdf(pre)
    activation = (pre * cdf).astype(jnp.bfloat16)
    slope = (cotangent.astype(jnp.float32) * (cdf + pre * normal_pdf(pre))).astype(jnp.bfloat16)
    back = to_modes(slope, second, modes_x, modes_y, modes_z)
    back_real = back[:, :, 0].reshape(local_y, local_x, count_z, chans)
    back_imag = back[:, :, 1].reshape(local_y, local_x, count_z, chans)
    outer = "bazo,bazi->abzoi"
    grad_real = jnp.einsum(outer, back_real, spec_real, precision=HIGH) + jnp.einsum(
        outer, back_imag, spec_imag, precision=HIGH
    )
    grad_imag = jnp.einsum(outer, back_imag, spec_real, precision=HIGH) - jnp.einsum(
        outer, back_real, spec_imag, precision=HIGH
    )
    grad_spectral = jnp.stack([grad_real, grad_imag], axis=3)
    adjoint = "abzoi,bazo->bazi"
    modes_real = jnp.einsum(adjoint, real_w, back_real, precision=HIGH) + jnp.einsum(
        adjoint, imag_w, back_imag, precision=HIGH
    )
    modes_imag = jnp.einsum(adjoint, real_w, back_imag, precision=HIGH) - jnp.einsum(
        adjoint, imag_w, back_real, precision=HIGH
    )
    back_modes = jnp.stack(
        [modes_real.reshape(local_y, local_x, -1), modes_imag.reshape(local_y, local_x, -1)], axis=2
    )
    spectral_back = to_cells(back_modes, first, rows_x, rows_y, size_z, modes_x, modes_y, modes_z)
    slope_flat = slope.reshape(-1, chans)
    conv_back = jnp.dot(slope_flat, conv_weight.T, preferred_element_type=jnp.float32).reshape(
        spectral.shape
    )
    grad_features = (spectral_back + conv_back).astype(jnp.bfloat16)
    local_conv = jnp.dot(flat.T, slope_flat, preferred_element_type=jnp.float32)
    grad_conv = first * lax.psum(local_conv, ("gx", "gy"))
    return (activation, grad_features, grad_spectral, grad_conv)


def fits(features, spectral_weight):
    rows_x, rows_y, size_z, chans = features.shape
    local_x, local_y, count_z = spectral_weight.shape[:3]
    parts_x, parts_y = lax.axis_size("gx"), lax.axis_size("gy")
    return (
        chans == 64
        and parts_x == 8
        and rows_y == 2 * parts_x
        and local_y == parts_x
        and rows_x * size_z == LANES
        and local_x * count_z == 2 * parts_x
        and parts_y == 4
        and all(n & (n - 1) == 0 for n in (rows_x * parts_x, rows_y * parts_y, size_z))
    )


def shards(features, cotangent, spectral_weight, *rest):
    run = fast if fits(features, spectral_weight) else plain
    return run(features, cotangent, spectral_weight, *rest)


def solution(mesh):
    placed = (
        P("gx", "gy", None, None),
        P("gx", "gy", None, None),
        P("gx", "gy", None, None, None, None),
        P(),
        P(),
        P(),
        P(),
    )
    return jax.shard_map(
        shards,
        mesh=mesh,
        in_specs=placed,
        out_specs=(
            P("gx", "gy", None, None),
            P("gx", "gy", None, None),
            P("gx", "gy", None, None, None, None),
            P(),
        ),
        check_vma=False,
    )
```

```python
import math

import jax
import jax.numpy as jnp
from jax import lax
from jax.experimental import pallas as pl
from jax.experimental.pallas import tpu as pltpu
from jax.sharding import PartitionSpec as P

HIGH = lax.Precision.HIGHEST
BF = jnp.bfloat16
F32 = jnp.float32
LANES = 128
EXTRA = 16
WIDE = 1024
SIDES = 4


def steps_of(parts):
    return list(range(0, parts, 2)) + list(range(1, parts, 2))


def cosine(turns, length):
    half = length // 2
    place = ((turns + length // 4) & (length - 1)) - half
    place = jnp.minimum(jnp.maximum(place, -half - place), half - place)
    angle = place.astype(F32) * (-2.0 * math.pi / length)
    square = angle * angle
    series = 1.0 / 362880.0 - square * (1.0 / 39916800.0)
    series = square * series - 1.0 / 5040.0
    series = square * series + 1.0 / 120.0
    series = square * series - 1.0 / 6.0
    return angle + angle * (square * series)


def pick(ref, index, places):
    out = jnp.zeros(index.shape, jnp.int32)
    for k, place in enumerate(places):
        out = jnp.where(index == k, ref[place], out)
    return out


def store_halves(ref, row, value):
    high = value.astype(BF)
    tall = ref.shape[0] // 2
    ref[row : row + value.shape[0]] = high
    ref[tall + row : tall + row + value.shape[0]] = (value - high.astype(F32)).astype(BF)


def grid_of(rows, cols):
    return (
        lax.broadcasted_iota(jnp.int32, (rows, cols), 0),
        lax.broadcasted_iota(jnp.int32, (rows, cols), 1),
    )


def table_kernel(size_z, *refs):
    sources, outs, places, sems = refs[:4], refs[5:11], refs[11:15], refs[15]
    line_ref, column_ref, cback_ref, lback_ref, pair_ref, turn_ref = outs
    copies = [
        pltpu.make_async_copy(source, place, sems.at[k])
        for k, (source, place) in enumerate(zip(sources, places))
    ]
    for copy in copies:
        copy.start()
    for copy in copies:
        copy.wait()
    mx_ref, my_ref, mz_ref, conv_ref = places
    parts_x, parts_y = lax.axis_size("gx"), lax.axis_size("gy")
    me_x, me_y = lax.axis_index("gx"), lax.axis_index("gy")
    count_x, count_y, count_z = mx_ref.shape[0], my_ref.shape[0], mz_ref.shape[0]
    local_x, local_y = count_x // parts_x, count_y // parts_y
    chans = conv_ref.shape[0]
    block = chans // parts_x
    length_x = line_ref.shape[1] // size_z
    whole = line_ref.shape[1]
    tile = 16

    rows_x = length_x // parts_x
    row, col = grid_of(tile, LANES)
    per = tile // count_z
    quarter = whole // 4
    base = pick(mz_ref, row % count_z, range(count_z)) * (col % size_z) * length_x
    inner = row // count_z
    offset = jnp.zeros(col.shape, jnp.int32)
    for k, step in enumerate(steps_of(parts_x)):
        offset = jnp.where(col == k, (me_x ^ step) * (rows_x * size_z), offset)
    modes = count_x * count_z
    for start in range(0, count_x, per):
        freq = pick(mx_ref, inner, range(start, start + per))
        turns = freq * (col // size_z * size_z) + base
        cos, sin = cosine(turns, whole), cosine(turns - quarter, whole)
        turns = freq * offset
        cos_step, sin_step = cosine(turns, whole), cosine(turns - quarter, whole)
        at = start * count_z
        for k in range(parts_x):
            cos_k = jnp.broadcast_to(cos_step[:, k : k + 1], cos.shape)
            sin_k = jnp.broadcast_to(sin_step[:, k : k + 1], cos.shape)
            columns = line_ref.at[:, k * LANES : (k + 1) * LANES]
            store_halves(columns, at, cos * cos_k - sin * sin_k)
            store_halves(columns, at + modes, -sin * cos_k - cos * sin_k)

    rows_y = column_ref.shape[0] // 4 // block
    length_y = rows_y * parts_y
    per = tile // block
    ky = col // block % local_y
    shift = col // (LANES // 2) * (length_y // 4)
    same = row % block == col % block
    low = col < LANES // 2
    inner = row // block + me_y * rows_y
    for gy in range(parts_y):
        freq = pick(my_ref, ky, range(gy * local_y, (gy + 1) * local_y))
        columns = column_ref.at[:, gy * LANES : (gy + 1) * LANES]
        for start in range(0, rows_y, per):
            value = jnp.where(same, cosine(freq * (inner + start) + shift, length_y), 0.0)
            store_halves(columns, start * block, value)
            turned = pltpu.roll(value, LANES // 2, 1)
            store_halves(columns, (rows_y + start) * block, jnp.where(low, -turned, turned))

    row, col = grid_of(2 * rows_y, cback_ref.shape[1])
    places = [
        (me_y + parts_y - step) % parts_y * local_y + k for step in range(parts_y) for k in range(local_y)
    ]
    freq = pick(my_ref, col // (2 * local_y) * local_y + col % local_y, places)
    shift = (col // local_y % 2 - row // rows_y) * (length_y // 4)
    store_halves(cback_ref, 0, cosine(freq * (row % rows_y + me_y * rows_y) + shift, length_y))

    row, col = grid_of(tile, lback_ref.shape[1])
    modes = local_x * count_z
    kx = col // (2 * modes) * local_x + col // count_z % local_x
    places = [(me_x ^ step) * local_x + k for step in steps_of(parts_x) for k in range(local_x)]
    freq = pick(mx_ref, kx, places) * size_z
    base = pick(mz_ref, col % count_z, range(count_z)) * (row % size_z) * length_x
    base = base + col // modes % 2 * (whole // 4)
    inner = row // size_z + me_x * rows_x
    per = tile // size_z
    for start in range(0, rows_x, per):
        store_halves(lback_ref, start * size_z, cosine(freq * (inner + start) + base, whole))

    conv = conv_ref[...].astype(F32)
    none = jnp.zeros_like(conv)
    for ref, value in ((pair_ref, conv), (turn_ref, conv.T)):
        ref[:chans] = jnp.concatenate([value, none], axis=1).astype(BF)
        ref[chans:] = jnp.concatenate([none, value], axis=1).astype(BF)


def dot(a, b, dims=((1,), (0,))):
    return lax.dot_general(a, b, (dims, ((), ())), preferred_element_type=F32)


def pairs_of(ref):
    size_x, size_y, size_z, chans = ref.shape
    out = []
    for y in range(size_y // 2):
        low = ref[:, y, :, :].astype(F32).reshape(size_x * size_z, chans)
        high = ref[:, y + size_y // 2, :, :].astype(F32).reshape(size_x * size_z, chans)
        out.append(jnp.concatenate([low, high], axis=1))
    return out


def block_transpose(arrays, block):
    count = len(arrays)
    arrays = list(arrays)
    lanes = arrays[0].shape[1]
    index = lax.broadcasted_iota(jnp.int32, arrays[0].shape, 1) // block % count
    step = 1
    while step < count:
        upper = (index & step) != 0
        for p in range(count):
            if p & step:
                continue
            a, b = arrays[p], arrays[p | step]
            arrays[p] = jnp.where(upper, pltpu.roll(b, step * block, 1), a)
            arrays[p | step] = jnp.where(upper, b, pltpu.roll(a, lanes - step * block, 1))
        step *= 2
    return arrays


def split_rows(value):
    high = value.astype(BF)
    return jnp.concatenate([high, (value - high.astype(F32)).astype(BF)], axis=0)


def normal_cdf(values):
    return 0.5 * (1.0 + lax.erf(values * (1.0 / math.sqrt(2.0))))


def normal_pdf(values):
    return jnp.exp(-0.5 * values * values) * (1.0 / math.sqrt(2.0 * math.pi))


def store_steps(chunk_ref, send_refs):
    me = lax.axis_index("gx")
    for t, ref in enumerate(send_refs):
        for r in range(2):
            ref[r] = chunk_ref[me ^ (2 * t + r)]


def spread_kernel(field_ref, *refs):
    send_refs, pairs_ref, chunk_ref = refs[:-2], refs[-2], refs[-1]
    pairs = pairs_of(field_ref)
    for p, pair in enumerate(pairs):
        pairs_ref[p] = pair.astype(BF)
    for b, chunk in enumerate(block_transpose(pairs, field_ref.shape[3] // len(pairs))):
        chunk_ref[b] = chunk.astype(BF)
    store_steps(chunk_ref, send_refs)


def pairs_kernel(field_ref, pairs_ref):
    for p, pair in enumerate(pairs_of(field_ref)):
        pairs_ref[p] = pair.astype(BF)


def joined(value):
    chans = value.shape[1] // 2
    return value[:, :chans].astype(F32) + value[:, chans:].astype(F32)


def parted(value):
    high = value.astype(BF).astype(F32)
    both = jnp.concatenate([high, value - high], axis=1)
    rest = jnp.zeros((EXTRA - both.shape[0], both.shape[1]), F32)
    return jnp.concatenate([both, rest], axis=0).astype(BF)


def transform_kernel(scale, parts_x, parts_y, line_ref, column_ref, *refs):
    recv_refs, send_ref, extra = refs[:parts_x], refs[parts_x], refs[parts_x + 1 :]
    rows = line_ref.shape[1] // parts_x
    own = [ref.at[k // (parts_x // 2)] for k, ref in enumerate(recv_refs)]
    if extra:
        total = joined(own[0][rows:, :])
        for ref in own[1:]:
            total = total + joined(ref[rows:, :])
        extra[0][...] = parted(total[: LANES // 2 // parts_x])
    data = jnp.concatenate([ref[:rows, :] for ref in own], axis=0)
    lines = dot(line_ref[...], data)
    half = lines.shape[0] // 2
    lines = lines[:half] + lines[half:]
    count = half // 2
    both = jnp.concatenate([lines[:count], lines[count:]], axis=1)
    depth = both.shape[1]
    high = both.astype(BF)
    low = (both - high.astype(F32)).astype(BF)
    modes = dot(split_rows(both), column_ref[:depth, :])
    modes = modes[:count] + modes[count:] + dot(high, column_ref[depth:, :])
    modes = modes * scale
    tall = count // parts_x
    for gx in range(parts_x):
        for gy in range(parts_y):
            send_ref[gx * parts_y + gy] = modes[
                gx * tall : (gx + 1) * tall, gy * LANES : (gy + 1) * LANES
            ].astype(BF)


def sum_parts(recv_ref, parts_y):
    parts = recv_ref.shape[0] // parts_y
    out = []
    for b in range(parts):
        total = recv_ref[b * parts_y].astype(F32)
        for gy in range(1, parts_y):
            total = total + recv_ref[b * parts_y + gy].astype(F32)
        out.append(total)
    return out


def lay_modes(scratch, send_ref, count_y, rows):
    chans = 64
    for m in range(0, rows, 2):
        parts = []
        for part in range(2):
            first = scratch[pl.ds(part * rows + m, count_y, stride=2 * rows), :chans]
            second = scratch[pl.ds(part * rows + m + 1, count_y, stride=2 * rows), :chans]
            parts.append(jnp.concatenate([first, second], axis=1))
        send_ref[:, m * chans : (m + 2) * chans] = jnp.concatenate(parts, axis=0).astype(send_ref.dtype)


def mix_kernel(forward, parts_y, recv_ref, weight_ref, *refs):
    send_ref, spec_ref, scratch = refs[-3:]
    if len(refs) == 4:
        send_ref[:, WIDE:] = refs[0][...]
    size_x, size_y, size_z, _, chans, _ = weight_ref.shape
    rows = size_x * size_z
    spectra = block_transpose(sum_parts(recv_ref, parts_y), chans // size_y)
    for ky in range(size_y):
        spec = spectra[ky]
        spec_ref[ky] = spec
        turned = pltpu.roll(spec, chans, 1)
        if forward:
            both = jnp.concatenate([spec, turned], axis=0)[:, :chans].T
            high = both.astype(BF)
            both = jnp.concatenate([high, (both - high.astype(F32)).astype(BF)], axis=1)
        else:
            first = lax.broadcasted_iota(jnp.int32, spec.shape, 1) < chans
            both = split_rows(jnp.concatenate([spec, jnp.where(first, turned, -turned)], axis=0))
        mode = lax.broadcasted_iota(jnp.int32, both.shape, 1 if forward else 0) % rows
        total = jnp.zeros((2 * chans, 4 * rows) if forward else (4 * rows, chans), F32)
        for m in range(rows):
            weight = weight_ref[m // size_z, ky, m % size_z].reshape(2 * chans, chans)
            own = jnp.where(mode == m, both, jnp.zeros_like(both))
            total = total + (dot(weight, own) if forward else dot(own, weight))
        if forward:
            total = total.T
        total = total[: 2 * rows] + total[2 * rows :]
        if forward:
            real, imag = total[:rows], total[rows:]
            mixed = jnp.concatenate(
                [
                    real[:, :chans] - imag[:, chans:],
                    imag[:, :chans] + real[:, chans:],
                ],
                axis=0,
            )
        else:
            mixed = total
        scratch[ky * 2 * rows : (ky + 1) * 2 * rows, :chans] = mixed
    lay_modes(scratch, send_ref, size_y, rows)


def column_kernel(table_ref, *refs):
    steps = len(refs) - 2
    send_ref, scratch = refs[steps], refs[steps + 1]
    chans = 64
    if refs[0].shape[1] > WIDE:
        total = joined(refs[0][:, WIDE:])
        for s in range(1, steps):
            total = total + joined(refs[s][:, WIDE:])
        send_ref[:EXTRA, WIDE:] = parted(total[: EXTRA // 2])
        send_ref[EXTRA:, WIDE:] = jnp.zeros((send_ref.shape[0] - EXTRA, LANES), BF)
    data = jnp.concatenate([refs[s][:, :WIDE] for s in range(steps)], axis=0)
    high = data.astype(BF)
    lines = dot(table_ref[...], high)
    half = lines.shape[0] // 2
    lines = lines[:half] + lines[half:]
    if data.dtype == F32:
        lines = lines + dot(table_ref[:half, :], (data - high.astype(F32)).astype(BF))
    size_y = half // 2
    count = WIDE // chans
    for m in range(0, count, 2):
        pair = lines[:, m * chans : (m + 2) * chans]
        scratch[m * half : (m + 1) * half, :] = pair
        scratch[(m + 1) * half : (m + 2) * half, :] = pltpu.roll(pair, chans, 1)
    for part in range(2):
        for y in range(size_y // 2):
            first = scratch[pl.ds(part * size_y + y, count, stride=half), :chans]
            second = scratch[pl.ds(part * size_y + y + size_y // 2, count, stride=half), :chans]
            send_ref[part * count : (part + 1) * count, y * 2 * chans : (y + 1) * 2 * chans] = (
                jnp.concatenate([first, second], axis=1).astype(BF)
            )


def cells_of(table_ref, recv_refs, scale):
    data = jnp.concatenate([ref[:, :WIDE] for ref in recv_refs], axis=0)
    cells = dot(table_ref[...], data)
    half = cells.shape[0] // 2
    return (cells[:half] + cells[half:]) * scale


def store_pair(out_ref, p, value):
    size_x, size_y, size_z, chans = out_ref.shape
    out_ref[:, p, :, :] = value[:, :chans].reshape(size_x, size_z, chans).astype(out_ref.dtype)
    out_ref[:, p + size_y // 2, :, :] = (
        value[:, chans:].reshape(size_x, size_z, chans).astype(out_ref.dtype)
    )


def point_kernel(scale, table_ref, *refs):
    recv_refs, refs = refs[: 2 * SIDES], refs[2 * SIDES :]
    conv_ref, field_ref, cot_ref, act_ref, slope_ref = refs[:5]
    send_refs, chunk_ref = refs[5:-1], refs[-1]
    cells = cells_of(table_ref, recv_refs, scale)
    count = field_ref.shape[0]
    slopes = []
    grad = jnp.zeros((LANES, LANES), F32)
    for p in range(count):
        field = field_ref[p]
        pre = cells[:, p * LANES : (p + 1) * LANES] + dot(field, conv_ref[...])
        cdf = normal_cdf(pre)
        store_pair(act_ref, p, pre * cdf)
        slope = cot_ref[p].astype(F32) * (cdf + pre * normal_pdf(pre))
        narrow = slope.astype(BF)
        slope_ref[p] = narrow
        slopes.append(narrow.astype(F32))
        grad = grad + dot(field, narrow, ((0,), (0,)))
    rows = slopes[0].shape[0]
    chans = LANES // 2
    grad = grad[:chans, :chans] + grad[chans:, chans:]
    block = chans // count
    for b, chunk in enumerate(block_transpose(slopes, block)):
        chunk_ref[b, :rows, :] = chunk.astype(BF)
        chunk_ref[b, rows:, :] = parted(grad[b * block : (b + 1) * block])
    store_steps(chunk_ref, send_refs)


def last_kernel(scale, table_ref, *refs):
    conv_ref, slope_ref, out_ref, grad_ref = refs[-4:]
    recv_refs = refs[:-4]
    block = grad_ref.shape[0] // len(recv_refs)
    me = lax.axis_index("gx")
    for step, ref in zip(steps_of(len(recv_refs)), recv_refs):
        total = joined(ref[:EXTRA, WIDE:])
        grad_ref[pl.ds(pl.multiple_of((me ^ step) * block, block), block), :] = total[:block] * scale
    cells = cells_of(table_ref, recv_refs, scale)
    for p in range(slope_ref.shape[0]):
        store_pair(out_ref, p, cells[:, p * LANES : (p + 1) * LANES] + dot(slope_ref[p], conv_ref[...]))


def outer_kernel(spec_ref, back_ref, out_ref):
    _, size_y, size_z, _, chans, _ = out_ref.shape
    rows = back_ref.shape[1]
    first = lax.broadcasted_iota(jnp.int32, back_ref.shape[1:], 1) < chans
    mode = lax.broadcasted_iota(jnp.int32, (6 * rows, chans), 0) % rows
    start = pl.program_id(0) * size_z
    for ky in range(size_y):
        back, spec = back_ref[ky], spec_ref[ky]
        turned = pltpu.roll(back, chans, 1)
        left = jnp.concatenate([back, jnp.where(first, turned, -turned)], axis=0).T
        right = jnp.concatenate([spec, pltpu.roll(spec, chans, 1)], axis=0)[:, :chans]
        left_high, right_high = left.astype(BF), right.astype(BF)
        left_low = (left - left_high.astype(F32)).astype(BF)
        right_low = (right - right_high.astype(F32)).astype(BF)
        lefts = jnp.concatenate([left_high, left_high, left_low], axis=1)
        rights = jnp.concatenate([right_high, right_low, right_high], axis=0)
        for m in range(size_z):
            own = jnp.where(mode == start + m, rights, jnp.zeros_like(rights))
            out_ref[0, ky, m] = dot(lefts, own).reshape(2, chans, chans)


def call(kernel, outs, *args, scratch=()):
    params = pltpu.CompilerParams(vmem_limit_bytes=16 * 2**20)
    return pl.pallas_call(kernel, out_shape=outs, scratch_shapes=list(scratch), compiler_params=params)(*args)


def bind(kernel, *static):
    def bound(*refs):
        return kernel(*static, *refs)

    return bound


def sds(shape, dtype):
    return jax.ShapeDtypeStruct(shape, dtype)


def fast(features, cotangent, spectral_weight, conv_weight, modes_x, modes_y, modes_z):
    rows_x, rows_y, size_z, chans = features.shape
    local_x, local_y, count_z = spectral_weight.shape[:3]
    parts_x, parts_y = lax.axis_size("gx"), lax.axis_size("gy")
    length_x, length_y = rows_x * parts_x, rows_y * parts_y
    block = chans // parts_x
    cells = rows_x * size_z
    modes = local_x * count_z
    half_y = rows_y // 2
    first = 1.0 / math.sqrt(length_x * length_y * size_z)
    second = 1.0 / math.sqrt(modes_x.shape[0] * modes_y.shape[0] * count_z)

    *send, field = call(
        spread_kernel,
        [sds((2, cells, LANES), BF)] * SIDES + [sds((half_y, cells, LANES), BF)],
        features,
        scratch=[pltpu.VMEM((parts_x, cells, LANES), BF)],
    )
    cot = call(pairs_kernel, sds((half_y, cells, LANES), BF), cotangent)
    outside = pl.BlockSpec(memory_space=pltpu.HBM)
    inside = pl.BlockSpec(memory_space=pltpu.VMEM)
    line_table, column_table, column_back, line_back, conv_pair, conv_turn = pl.pallas_call(
        bind(table_kernel, size_z),
        in_specs=[outside] * 4 + [inside],
        out_shape=(
            sds((4 * modes_x.shape[0] * count_z, length_x * size_z), BF),
            sds((4 * LANES, 4 * LANES), BF),
            sds((4 * rows_y, 2 * modes_y.shape[0]), BF),
            sds((2 * cells, 2 * modes_x.shape[0] * count_z), BF),
            sds((LANES, LANES), BF),
            sds((LANES, LANES), BF),
        ),
        scratch_shapes=[
            pltpu.SMEM(modes_x.shape, jnp.int32),
            pltpu.SMEM(modes_y.shape, jnp.int32),
            pltpu.SMEM(modes_z.shape, jnp.int32),
            pltpu.VMEM(conv_weight.shape, BF),
            pltpu.SemaphoreType.DMA((4,)),
        ],
        compiler_params=pltpu.CompilerParams(vmem_limit_bytes=16 * 2**20),
    )(*(pltpu.with_memory_space_constraint(x, pltpu.HBM) for x in (modes_x, modes_y, modes_z, conv_weight)), spectral_weight)

    def cross(pieces, beside=None):
        pieces = pieces[:1] + [
            lax.ppermute(piece, "gx", [(i, i ^ 2 * t) for i in range(parts_x)])
            for t, piece in enumerate(pieces)
            if t
        ]
        if beside is not None:
            pieces[-1], beside = lax.optimization_barrier((pieces[-1], beside))
        swap = [(i, i ^ 1) for i in range(parts_x)]
        pieces = pieces + [lax.ppermute(piece, "gx", swap) for piece in pieces]
        return pieces, beside

    def to_modes(send, factor, extra, tables):
        outs = [sds((parts_x * parts_y, modes, LANES), BF)]
        if extra:
            outs.append(sds((EXTRA, LANES), BF))
        kernel = bind(transform_kernel, factor, parts_x, parts_y)
        pieces, ready = cross(send, None if extra else tables)
        tables = tables if ready is None else ready
        send, *rest = call(kernel, outs, *tables, *pieces)
        return lax.all_to_all(send, ("gx", "gy"), 0, 0, tiled=True), rest, tables

    def mix(recv, forward, rest):
        return call(
            bind(mix_kernel, forward, parts_y),
            (
                sds((2 * local_y, WIDE + len(rest) * LANES), F32 if forward else BF),
                sds((local_y, modes, LANES), F32),
            ),
            recv,
            spectral_weight,
            *rest,
            scratch=[pltpu.VMEM((local_y * 2 * modes, LANES), F32)],
        )

    def to_lines(send, beside=None):
        pieces = [send]
        for step in range(1, parts_y):
            ring = [(i, (i + step) % parts_y) for i in range(parts_y)]
            pieces.append(lax.ppermute(send, "gy", ring))
        if beside is not None:
            pieces[-1], beside = lax.optimization_barrier((pieces[-1], beside))
        lines = call(
            column_kernel,
            sds((2 * modes, send.shape[1]), BF),
            column_back,
            *pieces,
            scratch=[pltpu.VMEM((modes * 2 * rows_y, LANES), F32)],
        )
        return cross([lines] * SIDES)[0], beside


    recv, _, tables = to_modes(send, first, False, (line_table, column_table))
    send, spec = mix(recv, True, [])
    pieces, _ = to_lines(send)
    activation, slope, *send = call(
        bind(point_kernel, second),
        (
            sds(features.shape, BF),
            sds((half_y, cells, LANES), BF),
        )
        + (sds((2, cells + EXTRA, LANES), BF),) * SIDES,
        line_back,
        *pieces,
        conv_pair,
        field,
        cot,
        scratch=[pltpu.VMEM((parts_x, cells + EXTRA, LANES), BF)],
    )
    recv, rest, _ = to_modes(send, second, True, tables)
    send, back = mix(recv, False, rest)
    grad_spectral = pl.pallas_call(
        outer_kernel,
        grid=(local_x,),
        in_specs=[pl.BlockSpec(spec.shape, lambda i: (0, 0, 0))] * 2,
        out_specs=pl.BlockSpec((1,) + spectral_weight.shape[1:], lambda i: (i, 0, 0, 0, 0, 0)),
        out_shape=sds(spectral_weight.shape, F32),
        compiler_params=pltpu.CompilerParams(vmem_limit_bytes=16 * 2**20),
    )(spec, back)
    pieces, grad_spectral = to_lines(send, grad_spectral)
    grad_features, grad_conv = call(
        bind(last_kernel, first),
        (sds(features.shape, BF), sds((chans, chans), F32)),
        line_back,
        *pieces,
        conv_turn,
        slope,
    )
    return activation, grad_features, grad_spectral, grad_conv


def phase_tables(freqs, places, length):
    product = freqs[:, None] * places[None, :] % length
    angles = product.astype(jnp.float32) * (2.0 * math.pi / length)
    return (jnp.cos(angles), jnp.sin(angles))


def plane_modes(values, factor, modes_z):
    size_x, size_y, size_z, chans = values.shape
    cos_z, sin_z = phase_tables(modes_z, jnp.arange(size_z, dtype=jnp.int32), size_z)
    wide = values.astype(jnp.float32)
    plane_real = (factor * jnp.einsum("xyzc,kz->xykc", wide, cos_z, precision=HIGH)).reshape(
        size_x, size_y, -1
    )
    plane_imag = (-factor * jnp.einsum("xyzc,kz->xykc", wide, sin_z, precision=HIGH)).reshape(
        size_x, size_y, -1
    )
    return (plane_real, plane_imag)


def line_modes(plane_real, plane_imag, freqs, places, length):
    cos_x, sin_x = phase_tables(freqs, places, length)
    line_real = jnp.einsum("kx,xyq->kyq", cos_x, plane_real, precision=HIGH) + jnp.einsum(
        "kx,xyq->kyq", sin_x, plane_imag, precision=HIGH
    )
    line_imag = jnp.einsum("kx,xyq->kyq", cos_x, plane_imag, precision=HIGH) - jnp.einsum(
        "kx,xyq->kyq", sin_x, plane_real, precision=HIGH
    )
    return jnp.stack([line_real, line_imag], axis=1)


def to_modes(values, factor, modes_x, modes_y, modes_z):
    rows_x, rows_y = (values.shape[0], values.shape[1])
    parts_x = lax.axis_size("gx")
    parts_y = lax.axis_size("gy")
    length_x = rows_x * parts_x
    length_y = rows_y * parts_y
    pencil = lax.all_to_all(values, "gx", split_axis=1, concat_axis=0, tiled=True)
    plane_real, plane_imag = plane_modes(pencil, factor, modes_z)
    whole = line_modes(
        plane_real, plane_imag, modes_x, jnp.arange(length_x, dtype=jnp.int32), length_x
    )
    spectrum = lax.all_to_all(whole, "gx", split_axis=0, concat_axis=2, tiled=True)
    places_y = lax.axis_index("gy") * rows_y + jnp.arange(rows_y, dtype=jnp.int32)
    cos_y, sin_y = phase_tables(modes_y, places_y, length_y)
    mode_real = jnp.einsum("ly,kyq->lkq", cos_y, spectrum[:, 0], precision=HIGH) + jnp.einsum(
        "ly,kyq->lkq", sin_y, spectrum[:, 1], precision=HIGH
    )
    mode_imag = jnp.einsum("ly,kyq->lkq", cos_y, spectrum[:, 1], precision=HIGH) - jnp.einsum(
        "ly,kyq->lkq", sin_y, spectrum[:, 0], precision=HIGH
    )
    return lax.psum_scatter(
        jnp.stack([mode_real, mode_imag], axis=2), "gy", scatter_dimension=0, tiled=True
    )


def to_cells(spectrum, factor, rows_x, rows_y, size_z, modes_x, modes_y, modes_z):
    length_x = rows_x * lax.axis_size("gx")
    length_y = rows_y * lax.axis_size("gy")
    places_y = lax.axis_index("gy") * rows_y + jnp.arange(rows_y, dtype=jnp.int32)
    places_x = lax.axis_index("gx") * rows_x + jnp.arange(rows_x, dtype=jnp.int32)
    piece = lax.all_gather(spectrum, "gy", axis=0, tiled=True)
    freqs = modes_y
    cos_y, sin_y = phase_tables(freqs, places_y, length_y)
    line_real = jnp.einsum("ly,lkq->kyq", cos_y, piece[:, :, 0], precision=HIGH) - jnp.einsum(
        "ly,lkq->kyq", sin_y, piece[:, :, 1], precision=HIGH
    )
    line_imag = jnp.einsum("ly,lkq->kyq", cos_y, piece[:, :, 1], precision=HIGH) + jnp.einsum(
        "ly,lkq->kyq", sin_y, piece[:, :, 0], precision=HIGH
    )
    line_real, line_imag = (line_real, line_imag)
    lines = jnp.stack([line_real, line_imag], axis=1)
    piece = lax.all_gather(lines, "gx", axis=0, tiled=True)
    freqs = modes_x
    cos_x, sin_x = phase_tables(freqs, places_x, length_x)
    plane_real = jnp.einsum("kx,kyq->xyq", cos_x, piece[:, 0], precision=HIGH) - jnp.einsum(
        "kx,kyq->xyq", sin_x, piece[:, 1], precision=HIGH
    )
    plane_imag = jnp.einsum("kx,kyq->xyq", cos_x, piece[:, 1], precision=HIGH) + jnp.einsum(
        "kx,kyq->xyq", sin_x, piece[:, 0], precision=HIGH
    )
    plane_real, plane_imag = (plane_real, plane_imag)
    count_z = modes_z.shape[0]
    plane_real = plane_real.reshape(rows_x, rows_y, count_z, -1)
    plane_imag = plane_imag.reshape(rows_x, rows_y, count_z, -1)
    cos_z, sin_z = phase_tables(modes_z, jnp.arange(size_z, dtype=jnp.int32), size_z)
    return factor * (
        jnp.einsum("xykc,kz->xyzc", plane_real, cos_z, precision=HIGH)
        - jnp.einsum("xykc,kz->xyzc", plane_imag, sin_z, precision=HIGH)
    )


def plain(features, cotangent, spectral_weight, conv_weight, modes_x, modes_y, modes_z):
    rows_x, rows_y, size_z, chans = features.shape
    count_x, count_y, count_z = (modes_x.shape[0], modes_y.shape[0], modes_z.shape[0])
    length_x = rows_x * lax.axis_size("gx")
    length_y = rows_y * lax.axis_size("gy")
    first = 1.0 / math.sqrt(length_x * length_y * size_z)
    second = 1.0 / math.sqrt(count_x * count_y * count_z)
    spectrum = to_modes(features, first, modes_x, modes_y, modes_z)
    local_y, local_x = (spectrum.shape[0], spectrum.shape[1])
    spec_real = spectrum[:, :, 0].reshape(local_y, local_x, count_z, chans)
    spec_imag = spectrum[:, :, 1].reshape(local_y, local_x, count_z, chans)
    weight = spectral_weight.astype(jnp.float32)
    real_w = weight[:, :, :, 0]
    imag_w = weight[:, :, :, 1]
    form = "abzoi,bazi->bazo"
    mixed_real = jnp.einsum(form, real_w, spec_real, precision=HIGH) - jnp.einsum(
        form, imag_w, spec_imag, precision=HIGH
    )
    mixed_imag = jnp.einsum(form, real_w, spec_imag, precision=HIGH) + jnp.einsum(
        form, imag_w, spec_real, precision=HIGH
    )
    mixed = jnp.stack(
        [mixed_real.reshape(local_y, local_x, -1), mixed_imag.reshape(local_y, local_x, -1)], axis=2
    )
    spectral = to_cells(mixed, second, rows_x, rows_y, size_z, modes_x, modes_y, modes_z)
    flat = features.reshape(-1, chans)
    conv = jnp.dot(flat, conv_weight, preferred_element_type=jnp.float32).reshape(spectral.shape)
    pre = spectral + conv
    cdf = normal_cdf(pre)
    activation = (pre * cdf).astype(jnp.bfloat16)
    slope = (cotangent.astype(jnp.float32) * (cdf + pre * normal_pdf(pre))).astype(jnp.bfloat16)
    back = to_modes(slope, second, modes_x, modes_y, modes_z)
    back_real = back[:, :, 0].reshape(local_y, local_x, count_z, chans)
    back_imag = back[:, :, 1].reshape(local_y, local_x, count_z, chans)
    outer = "bazo,bazi->abzoi"
    grad_real = jnp.einsum(outer, back_real, spec_real, precision=HIGH) + jnp.einsum(
        outer, back_imag, spec_imag, precision=HIGH
    )
    grad_imag = jnp.einsum(outer, back_imag, spec_real, precision=HIGH) - jnp.einsum(
        outer, back_real, spec_imag, precision=HIGH
    )
    grad_spectral = jnp.stack([grad_real, grad_imag], axis=3)
    adjoint = "abzoi,bazo->bazi"
    modes_real = jnp.einsum(adjoint, real_w, back_real, precision=HIGH) + jnp.einsum(
        adjoint, imag_w, back_imag, precision=HIGH
    )
    modes_imag = jnp.einsum(adjoint, real_w, back_imag, precision=HIGH) - jnp.einsum(
        adjoint, imag_w, back_real, precision=HIGH
    )
    back_modes = jnp.stack(
        [modes_real.reshape(local_y, local_x, -1), modes_imag.reshape(local_y, local_x, -1)], axis=2
    )
    spectral_back = to_cells(back_modes, first, rows_x, rows_y, size_z, modes_x, modes_y, modes_z)
    slope_flat = slope.reshape(-1, chans)
    conv_back = jnp.dot(slope_flat, conv_weight.T, preferred_element_type=jnp.float32).reshape(
        spectral.shape
    )
    grad_features = (spectral_back + conv_back).astype(jnp.bfloat16)
    local_conv = jnp.dot(flat.T, slope_flat, preferred_element_type=jnp.float32)
    grad_conv = first * lax.psum(local_conv, ("gx", "gy"))
    return (activation, grad_features, grad_spectral, grad_conv)


def fits(features, spectral_weight):
    rows_x, rows_y, size_z, chans = features.shape
    local_x, local_y, count_z = spectral_weight.shape[:3]
    parts_x, parts_y = lax.axis_size("gx"), lax.axis_size("gy")
    return (
        chans == 64
        and parts_x == 8
        and rows_y == 2 * parts_x
        and local_y == parts_x
        and rows_x * size_z == LANES
        and local_x * count_z == 2 * parts_x
        and parts_y == 4
        and all(n & (n - 1) == 0 for n in (rows_x * parts_x, rows_y * parts_y, size_z))
    )


def shards(features, cotangent, spectral_weight, *rest):
    run = fast if fits(features, spectral_weight) else plain
    return run(features, cotangent, spectral_weight, *rest)


def solution(mesh):
    placed = (
        P("gx", "gy", None, None),
        P("gx", "gy", None, None),
        P("gx", "gy", None, None, None, None),
        P(),
        P(),
        P(),
        P(),
    )
    return jax.shard_map(
        shards,
        mesh=mesh,
        in_specs=placed,
        out_specs=(
            P("gx", "gy", None, None),
            P("gx", "gy", None, None),
            P("gx", "gy", None, None, None, None),
            P(),
        ),
        check_vma=False,
    )
```

```python
import math

import jax
import jax.numpy as jnp
from jax import lax
from jax.experimental import pallas as pl
from jax.experimental.pallas import tpu as pltpu
from jax.sharding import PartitionSpec as P

HIGH = lax.Precision.HIGHEST
BF = jnp.bfloat16
F32 = jnp.float32
LANES = 128
EXTRA = 16
WIDE = 1024
SIDES = 4


def steps_of(parts):
    return list(range(0, parts, 2)) + list(range(1, parts, 2))


def cosine(turns, length):
    half = length // 2
    place = ((turns + length // 4) & (length - 1)) - half
    place = jnp.minimum(jnp.maximum(place, -half - place), half - place)
    angle = place.astype(F32) * (-2.0 * math.pi / length)
    square = angle * angle
    series = 1.0 / 362880.0 - square * (1.0 / 39916800.0)
    series = square * series - 1.0 / 5040.0
    series = square * series + 1.0 / 120.0
    series = square * series - 1.0 / 6.0
    return angle + angle * (square * series)


def pick(ref, index, places):
    out = jnp.zeros(index.shape, jnp.int32)
    for k, place in enumerate(places):
        out = jnp.where(index == k, ref[place], out)
    return out


def store_halves(ref, row, value):
    high = value.astype(BF)
    tall = ref.shape[0] // 2
    ref[row : row + value.shape[0]] = high
    ref[tall + row : tall + row + value.shape[0]] = (value - high.astype(F32)).astype(BF)


def grid_of(rows, cols):
    return (
        lax.broadcasted_iota(jnp.int32, (rows, cols), 0),
        lax.broadcasted_iota(jnp.int32, (rows, cols), 1),
    )


def table_kernel(size_z, *refs):
    sources, outs, places, sems = refs[:4], refs[5:11], refs[11:15], refs[15]
    line_ref, column_ref, cback_ref, lback_ref, pair_ref, turn_ref = outs
    copies = [
        pltpu.make_async_copy(source, place, sems.at[k])
        for k, (source, place) in enumerate(zip(sources, places))
    ]
    for copy in copies:
        copy.start()
    for copy in copies:
        copy.wait()
    mx_ref, my_ref, mz_ref, conv_ref = places
    parts_x, parts_y = lax.axis_size("gx"), lax.axis_size("gy")
    me_x, me_y = lax.axis_index("gx"), lax.axis_index("gy")
    count_x, count_y, count_z = mx_ref.shape[0], my_ref.shape[0], mz_ref.shape[0]
    local_x, local_y = count_x // parts_x, count_y // parts_y
    chans = conv_ref.shape[0]
    block = chans // parts_x
    length_x = line_ref.shape[1] // size_z
    whole = line_ref.shape[1]
    tile = 16

    rows_x = length_x // parts_x
    row, col = grid_of(tile, LANES)
    per = tile // count_z
    quarter = whole // 4
    base = pick(mz_ref, row % count_z, range(count_z)) * (col % size_z) * length_x
    inner = row // count_z
    offset = jnp.zeros(col.shape, jnp.int32)
    for k, step in enumerate(steps_of(parts_x)):
        offset = jnp.where(col == k, (me_x ^ step) * (rows_x * size_z), offset)
    modes = count_x * count_z
    for start in range(0, count_x, per):
        freq = pick(mx_ref, inner, range(start, start + per))
        turns = freq * (col // size_z * size_z) + base
        cos, sin = cosine(turns, whole), cosine(turns - quarter, whole)
        turns = freq * offset
        cos_step, sin_step = cosine(turns, whole), cosine(turns - quarter, whole)
        at = start * count_z
        for k in range(parts_x):
            cos_k = jnp.broadcast_to(cos_step[:, k : k + 1], cos.shape)
            sin_k = jnp.broadcast_to(sin_step[:, k : k + 1], cos.shape)
            columns = line_ref.at[:, k * LANES : (k + 1) * LANES]
            store_halves(columns, at, cos * cos_k - sin * sin_k)
            store_halves(columns, at + modes, -sin * cos_k - cos * sin_k)

    rows_y = column_ref.shape[0] // 4 // block
    length_y = rows_y * parts_y
    per = tile // block
    ky = col // block % local_y
    shift = col // (LANES // 2) * (length_y // 4)
    same = row % block == col % block
    low = col < LANES // 2
    inner = row // block + me_y * rows_y
    for gy in range(parts_y):
        freq = pick(my_ref, ky, range(gy * local_y, (gy + 1) * local_y))
        columns = column_ref.at[:, gy * LANES : (gy + 1) * LANES]
        for start in range(0, rows_y, per):
            value = jnp.where(same, cosine(freq * (inner + start) + shift, length_y), 0.0)
            store_halves(columns, start * block, value)
            turned = pltpu.roll(value, LANES // 2, 1)
            store_halves(columns, (rows_y + start) * block, jnp.where(low, -turned, turned))

    row, col = grid_of(2 * rows_y, cback_ref.shape[1])
    places = [
        (me_y + parts_y - step) % parts_y * local_y + k for step in range(parts_y) for k in range(local_y)
    ]
    freq = pick(my_ref, col // (2 * local_y) * local_y + col % local_y, places)
    shift = (col // local_y % 2 - row // rows_y) * (length_y // 4)
    store_halves(cback_ref, 0, cosine(freq * (row % rows_y + me_y * rows_y) + shift, length_y))

    row, col = grid_of(tile, lback_ref.shape[1])
    modes = local_x * count_z
    kx = col // (2 * modes) * local_x + col // count_z % local_x
    places = [(me_x ^ step) * local_x + k for step in steps_of(parts_x) for k in range(local_x)]
    freq = pick(mx_ref, kx, places) * size_z
    base = pick(mz_ref, col % count_z, range(count_z)) * (row % size_z) * length_x
    base = base + col // modes % 2 * (whole // 4)
    inner = row // size_z + me_x * rows_x
    per = tile // size_z
    for start in range(0, rows_x, per):
        store_halves(lback_ref, start * size_z, cosine(freq * (inner + start) + base, whole))

    conv = conv_ref[...].astype(F32)
    none = jnp.zeros_like(conv)
    for ref, value in ((pair_ref, conv), (turn_ref, conv.T)):
        ref[:chans] = jnp.concatenate([value, none], axis=1).astype(BF)
        ref[chans:] = jnp.concatenate([none, value], axis=1).astype(BF)


def dot(a, b, dims=((1,), (0,))):
    return lax.dot_general(a, b, (dims, ((), ())), preferred_element_type=F32)


def pairs_of(ref):
    size_x, size_y, size_z, chans = ref.shape
    out = []
    for y in range(size_y // 2):
        low = ref[:, y, :, :].astype(F32).reshape(size_x * size_z, chans)
        high = ref[:, y + size_y // 2, :, :].astype(F32).reshape(size_x * size_z, chans)
        out.append(jnp.concatenate([low, high], axis=1))
    return out


def block_transpose(arrays, block):
    count = len(arrays)
    arrays = list(arrays)
    lanes = arrays[0].shape[1]
    index = lax.broadcasted_iota(jnp.int32, arrays[0].shape, 1) // block % count
    step = 1
    while step < count:
        upper = (index & step) != 0
        for p in range(count):
            if p & step:
                continue
            a, b = arrays[p], arrays[p | step]
            arrays[p] = jnp.where(upper, pltpu.roll(b, step * block, 1), a)
            arrays[p | step] = jnp.where(upper, b, pltpu.roll(a, lanes - step * block, 1))
        step *= 2
    return arrays


def split_rows(value):
    high = value.astype(BF)
    return jnp.concatenate([high, (value - high.astype(F32)).astype(BF)], axis=0)


def normal_cdf(values):
    return 0.5 * (1.0 + lax.erf(values * (1.0 / math.sqrt(2.0))))


def normal_pdf(values):
    return jnp.exp(-0.5 * values * values) * (1.0 / math.sqrt(2.0 * math.pi))


def store_steps(chunk_ref, send_refs):
    me = lax.axis_index("gx")
    for t, ref in enumerate(send_refs):
        for r in range(2):
            ref[r] = chunk_ref[me ^ (2 * t + r)]


def spread_kernel(field_ref, *refs):
    send_refs, pairs_ref, chunk_ref = refs[:-2], refs[-2], refs[-1]
    pairs = pairs_of(field_ref)
    for p, pair in enumerate(pairs):
        pairs_ref[p] = pair.astype(BF)
    for b, chunk in enumerate(block_transpose(pairs, field_ref.shape[3] // len(pairs))):
        chunk_ref[b] = chunk.astype(BF)
    store_steps(chunk_ref, send_refs)


def pairs_kernel(field_ref, pairs_ref):
    for p, pair in enumerate(pairs_of(field_ref)):
        pairs_ref[p] = pair.astype(BF)


def joined(value):
    chans = value.shape[1] // 2
    return value[:, :chans].astype(F32) + value[:, chans:].astype(F32)


def parted(value):
    high = value.astype(BF).astype(F32)
    both = jnp.concatenate([high, value - high], axis=1)
    rest = jnp.zeros((EXTRA - both.shape[0], both.shape[1]), F32)
    return jnp.concatenate([both, rest], axis=0).astype(BF)


def transform_kernel(scale, parts_x, parts_y, line_ref, column_ref, *refs):
    recv_refs, send_ref, extra = refs[:parts_x], refs[parts_x], refs[parts_x + 1 :]
    rows = line_ref.shape[1] // parts_x
    own = [ref.at[k // (parts_x // 2)] for k, ref in enumerate(recv_refs)]
    if extra:
        total = joined(own[0][rows:, :])
        for ref in own[1:]:
            total = total + joined(ref[rows:, :])
        extra[0][...] = parted(total[: LANES // 2 // parts_x])
    data = jnp.concatenate([ref[:rows, :] for ref in own], axis=0)
    lines = dot(line_ref[...], data)
    half = lines.shape[0] // 2
    lines = lines[:half] + lines[half:]
    count = half // 2
    both = jnp.concatenate([lines[:count], lines[count:]], axis=1)
    depth = both.shape[1]
    high = both.astype(BF)
    low = (both - high.astype(F32)).astype(BF)
    modes = dot(split_rows(both), column_ref[:depth, :])
    modes = modes[:count] + modes[count:] + dot(high, column_ref[depth:, :])
    modes = modes * scale
    tall = count // parts_x
    for gx in range(parts_x):
        for gy in range(parts_y):
            send_ref[gx * parts_y + gy] = modes[
                gx * tall : (gx + 1) * tall, gy * LANES : (gy + 1) * LANES
            ].astype(BF)


def sum_parts(recv_ref, parts_y):
    parts = recv_ref.shape[0] // parts_y
    out = []
    for b in range(parts):
        total = recv_ref[b * parts_y].astype(F32)
        for gy in range(1, parts_y):
            total = total + recv_ref[b * parts_y + gy].astype(F32)
        out.append(total)
    return out


def lay_modes(scratch, send_ref, count_y, rows):
    chans = 64
    for m in range(0, rows, 2):
        parts = []
        for part in range(2):
            first = scratch[pl.ds(part * rows + m, count_y, stride=2 * rows), :chans]
            second = scratch[pl.ds(part * rows + m + 1, count_y, stride=2 * rows), :chans]
            parts.append(jnp.concatenate([first, second], axis=1))
        send_ref[:, m * chans : (m + 2) * chans] = jnp.concatenate(parts, axis=0).astype(send_ref.dtype)


def mix_kernel(forward, parts_y, recv_ref, weight_ref, *refs):
    send_ref, spec_ref, scratch = refs[-3:]
    if len(refs) == 4:
        send_ref[:, WIDE:] = refs[0][...]
    size_x, size_y, size_z, _, chans, _ = weight_ref.shape
    rows = size_x * size_z
    spectra = block_transpose(sum_parts(recv_ref, parts_y), chans // size_y)
    for ky in range(size_y):
        spec = spectra[ky]
        spec_ref[ky] = spec
        turned = pltpu.roll(spec, chans, 1)
        if forward:
            both = jnp.concatenate([spec, turned], axis=0)[:, :chans].T
            high = both.astype(BF)
            both = jnp.concatenate([high, (both - high.astype(F32)).astype(BF)], axis=1)
        else:
            first = lax.broadcasted_iota(jnp.int32, spec.shape, 1) < chans
            both = split_rows(jnp.concatenate([spec, jnp.where(first, turned, -turned)], axis=0))
        mode = lax.broadcasted_iota(jnp.int32, both.shape, 1 if forward else 0) % rows
        total = jnp.zeros((2 * chans, 4 * rows) if forward else (4 * rows, chans), F32)
        for m in range(rows):
            weight = weight_ref[m // size_z, ky, m % size_z].reshape(2 * chans, chans)
            own = jnp.where(mode == m, both, jnp.zeros_like(both))
            total = total + (dot(weight, own) if forward else dot(own, weight))
        if forward:
            total = total.T
        total = total[: 2 * rows] + total[2 * rows :]
        if forward:
            real, imag = total[:rows], total[rows:]
            mixed = jnp.concatenate(
                [
                    real[:, :chans] - imag[:, chans:],
                    imag[:, :chans] + real[:, chans:],
                ],
                axis=0,
            )
        else:
            mixed = total
        scratch[ky * 2 * rows : (ky + 1) * 2 * rows, :chans] = mixed
    lay_modes(scratch, send_ref, size_y, rows)


def column_kernel(table_ref, *refs):
    steps = len(refs) - 2
    send_ref, scratch = refs[steps], refs[steps + 1]
    chans = 64
    if refs[0].shape[1] > WIDE:
        total = joined(refs[0][:, WIDE:])
        for s in range(1, steps):
            total = total + joined(refs[s][:, WIDE:])
        send_ref[:EXTRA, WIDE:] = parted(total[: EXTRA // 2])
        send_ref[EXTRA:, WIDE:] = jnp.zeros((send_ref.shape[0] - EXTRA, LANES), BF)
    data = jnp.concatenate([refs[s][:, :WIDE] for s in range(steps)], axis=0)
    high = data.astype(BF)
    lines = dot(table_ref[...], high)
    half = lines.shape[0] // 2
    lines = lines[:half] + lines[half:]
    if data.dtype == F32:
        lines = lines + dot(table_ref[:half, :], (data - high.astype(F32)).astype(BF))
    size_y = half // 2
    count = WIDE // chans
    for m in range(0, count, 2):
        pair = lines[:, m * chans : (m + 2) * chans]
        scratch[m * half : (m + 1) * half, :] = pair
        scratch[(m + 1) * half : (m + 2) * half, :] = pltpu.roll(pair, chans, 1)
    for part in range(2):
        for y in range(size_y // 2):
            first = scratch[pl.ds(part * size_y + y, count, stride=half), :chans]
            second = scratch[pl.ds(part * size_y + y + size_y // 2, count, stride=half), :chans]
            send_ref[part * count : (part + 1) * count, y * 2 * chans : (y + 1) * 2 * chans] = (
                jnp.concatenate([first, second], axis=1).astype(BF)
            )


def cells_of(table_ref, recv_refs, scale):
    data = jnp.concatenate([ref[:, :WIDE] for ref in recv_refs], axis=0)
    cells = dot(table_ref[...], data)
    half = cells.shape[0] // 2
    return (cells[:half] + cells[half:]) * scale


def store_pair(out_ref, p, value):
    size_x, size_y, size_z, chans = out_ref.shape
    out_ref[:, p, :, :] = value[:, :chans].reshape(size_x, size_z, chans).astype(out_ref.dtype)
    out_ref[:, p + size_y // 2, :, :] = (
        value[:, chans:].reshape(size_x, size_z, chans).astype(out_ref.dtype)
    )


def point_kernel(scale, table_ref, *refs):
    recv_refs, refs = refs[: 2 * SIDES], refs[2 * SIDES :]
    conv_ref, field_ref, cot_ref, act_ref, slope_ref = refs[:5]
    send_refs, chunk_ref = refs[5:-1], refs[-1]
    cells = cells_of(table_ref, recv_refs, scale)
    count = field_ref.shape[0]
    slopes = []
    grad = jnp.zeros((LANES, LANES), F32)
    for p in range(count):
        field = field_ref[p]
        pre = cells[:, p * LANES : (p + 1) * LANES] + dot(field, conv_ref[...])
        cdf = normal_cdf(pre)
        store_pair(act_ref, p, pre * cdf)
        slope = cot_ref[p].astype(F32) * (cdf + pre * normal_pdf(pre))
        narrow = slope.astype(BF)
        slope_ref[p] = narrow
        slopes.append(narrow.astype(F32))
        grad = grad + dot(field, narrow, ((0,), (0,)))
    rows = slopes[0].shape[0]
    chans = LANES // 2
    grad = grad[:chans, :chans] + grad[chans:, chans:]
    block = chans // count
    for b, chunk in enumerate(block_transpose(slopes, block)):
        chunk_ref[b, :rows, :] = chunk.astype(BF)
        chunk_ref[b, rows:, :] = parted(grad[b * block : (b + 1) * block])
    store_steps(chunk_ref, send_refs)


def last_kernel(scale, table_ref, *refs):
    conv_ref, slope_ref, out_ref, grad_ref = refs[-4:]
    recv_refs = refs[:-4]
    block = grad_ref.shape[0] // len(recv_refs)
    me = lax.axis_index("gx")
    for step, ref in zip(steps_of(len(recv_refs)), recv_refs):
        total = joined(ref[:EXTRA, WIDE:])
        grad_ref[pl.ds(pl.multiple_of((me ^ step) * block, block), block), :] = total[:block] * scale
    cells = cells_of(table_ref, recv_refs, scale)
    for p in range(slope_ref.shape[0]):
        store_pair(out_ref, p, cells[:, p * LANES : (p + 1) * LANES] + dot(slope_ref[p], conv_ref[...]))


def outer_kernel(spec_ref, back_ref, out_ref, held_ref, sems):
    size_x, size_y, size_z, _, chans, _ = held_ref.shape
    rows = size_x * size_z
    first = lax.broadcasted_iota(jnp.int32, back_ref.shape[1:], 1) < chans
    mode = lax.broadcasted_iota(jnp.int32, (6 * rows, chans), 0) % rows
    copies = []
    for ky in range(size_y):
        back, spec = back_ref[ky], spec_ref[ky]
        turned = pltpu.roll(back, chans, 1)
        left = jnp.concatenate([back, jnp.where(first, turned, -turned)], axis=0).T
        right = jnp.concatenate([spec, pltpu.roll(spec, chans, 1)], axis=0)[:, :chans]
        left_high, right_high = left.astype(BF), right.astype(BF)
        left_low = (left - left_high.astype(F32)).astype(BF)
        right_low = (right - right_high.astype(F32)).astype(BF)
        lefts = jnp.concatenate([left_high, left_high, left_low], axis=1)
        rights = jnp.concatenate([right_high, right_low, right_high], axis=0)
        for m in range(rows):
            own = jnp.where(mode == m, rights, jnp.zeros_like(rights))
            held_ref[m // size_z, ky, m % size_z] = dot(lefts, own).reshape(2, chans, chans)
        copy = pltpu.make_async_copy(held_ref.at[:, ky], out_ref.at[:, ky], sems.at[ky])
        copy.start()
        copies.append(copy)
    for copy in copies:
        copy.wait()


def call(kernel, outs, *args, scratch=()):
    params = pltpu.CompilerParams(vmem_limit_bytes=16 * 2**20)
    return pl.pallas_call(kernel, out_shape=outs, scratch_shapes=list(scratch), compiler_params=params)(*args)


def bind(kernel, *static):
    def bound(*refs):
        return kernel(*static, *refs)

    return bound


def sds(shape, dtype):
    return jax.ShapeDtypeStruct(shape, dtype)


def fast(features, cotangent, spectral_weight, conv_weight, modes_x, modes_y, modes_z):
    rows_x, rows_y, size_z, chans = features.shape
    local_x, local_y, count_z = spectral_weight.shape[:3]
    parts_x, parts_y = lax.axis_size("gx"), lax.axis_size("gy")
    length_x, length_y = rows_x * parts_x, rows_y * parts_y
    block = chans // parts_x
    cells = rows_x * size_z
    modes = local_x * count_z
    half_y = rows_y // 2
    first = 1.0 / math.sqrt(length_x * length_y * size_z)
    second = 1.0 / math.sqrt(modes_x.shape[0] * modes_y.shape[0] * count_z)

    *send, field = call(
        spread_kernel,
        [sds((2, cells, LANES), BF)] * SIDES + [sds((half_y, cells, LANES), BF)],
        features,
        scratch=[pltpu.VMEM((parts_x, cells, LANES), BF)],
    )
    cot = call(pairs_kernel, sds((half_y, cells, LANES), BF), cotangent)
    outside = pl.BlockSpec(memory_space=pltpu.HBM)
    inside = pl.BlockSpec(memory_space=pltpu.VMEM)
    line_table, column_table, column_back, line_back, conv_pair, conv_turn = pl.pallas_call(
        bind(table_kernel, size_z),
        in_specs=[outside] * 5,
        out_shape=(
            sds((4 * modes_x.shape[0] * count_z, length_x * size_z), BF),
            sds((4 * LANES, 4 * LANES), BF),
            sds((4 * rows_y, 2 * modes_y.shape[0]), BF),
            sds((2 * cells, 2 * modes_x.shape[0] * count_z), BF),
            sds((LANES, LANES), BF),
            sds((LANES, LANES), BF),
        ),
        scratch_shapes=[
            pltpu.SMEM(modes_x.shape, jnp.int32),
            pltpu.SMEM(modes_y.shape, jnp.int32),
            pltpu.SMEM(modes_z.shape, jnp.int32),
            pltpu.VMEM(conv_weight.shape, BF),
            pltpu.SemaphoreType.DMA((4,)),
        ],
        compiler_params=pltpu.CompilerParams(vmem_limit_bytes=16 * 2**20),
    )(*(pltpu.with_memory_space_constraint(x, pltpu.HBM) for x in (modes_x, modes_y, modes_z, conv_weight, spectral_weight)))

    def cross(pieces, beside=None):
        pieces = pieces[:1] + [
            lax.ppermute(piece, "gx", [(i, i ^ 2 * t) for i in range(parts_x)])
            for t, piece in enumerate(pieces)
            if t
        ]
        if beside is not None:
            pieces[-1], beside = lax.optimization_barrier((pieces[-1], beside))
        swap = [(i, i ^ 1) for i in range(parts_x)]
        pieces = pieces + [lax.ppermute(piece, "gx", swap) for piece in pieces]
        return pieces, beside

    def to_modes(send, factor, extra, tables):
        outs = [sds((parts_x * parts_y, modes, LANES), BF)]
        if extra:
            outs.append(sds((EXTRA, LANES), BF))
        kernel = bind(transform_kernel, factor, parts_x, parts_y)
        pieces, ready = cross(send, None if extra else tables)
        tables = tables if ready is None else ready
        send, *rest = call(kernel, outs, *tables, *pieces)
        return lax.all_to_all(send, ("gx", "gy"), 0, 0, tiled=True), rest, tables

    def mix(recv, forward, rest):
        return call(
            bind(mix_kernel, forward, parts_y),
            (
                sds((2 * local_y, WIDE + len(rest) * LANES), F32 if forward else BF),
                sds((local_y, modes, LANES), F32),
            ),
            recv,
            spectral_weight,
            *rest,
            scratch=[pltpu.VMEM((local_y * 2 * modes, LANES), F32)],
        )

    def to_lines(send, beside=None):
        pieces = [send]
        for step in range(1, parts_y):
            ring = [(i, (i + step) % parts_y) for i in range(parts_y)]
            pieces.append(lax.ppermute(send, "gy", ring))
        if beside is not None:
            pieces[-1], beside = lax.optimization_barrier((pieces[-1], beside))
        lines = call(
            column_kernel,
            sds((2 * modes, send.shape[1]), BF),
            column_back,
            *pieces,
            scratch=[pltpu.VMEM((modes * 2 * rows_y, LANES), F32)],
        )
        return cross([lines] * SIDES)[0], beside


    recv, _, tables = to_modes(send, first, False, (line_table, column_table))
    send, spec = mix(recv, True, [])
    pieces, _ = to_lines(send)
    activation, slope, *send = call(
        bind(point_kernel, second),
        (
            sds(features.shape, BF),
            sds((half_y, cells, LANES), BF),
        )
        + (sds((2, cells + EXTRA, LANES), BF),) * SIDES,
        line_back,
        *pieces,
        conv_pair,
        field,
        cot,
        scratch=[pltpu.VMEM((parts_x, cells + EXTRA, LANES), BF)],
    )
    recv, rest, _ = to_modes(send, second, True, tables)
    send, back = mix(recv, False, rest)
    grad_spectral = pl.pallas_call(
        outer_kernel,
        in_specs=[inside] * 2,
        out_specs=outside,
        out_shape=sds(spectral_weight.shape, F32),
        scratch_shapes=[pltpu.VMEM(spectral_weight.shape, F32), pltpu.SemaphoreType.DMA((local_y,))],
        compiler_params=pltpu.CompilerParams(vmem_limit_bytes=16 * 2**20),
    )(spec, back)
    pieces, grad_spectral = to_lines(send, grad_spectral)
    grad_features, grad_conv = call(
        bind(last_kernel, first),
        (sds(features.shape, BF), sds((chans, chans), F32)),
        line_back,
        *pieces,
        conv_turn,
        slope,
    )
    return activation, grad_features, grad_spectral, grad_conv


def phase_tables(freqs, places, length):
    product = freqs[:, None] * places[None, :] % length
    angles = product.astype(jnp.float32) * (2.0 * math.pi / length)
    return (jnp.cos(angles), jnp.sin(angles))


def plane_modes(values, factor, modes_z):
    size_x, size_y, size_z, chans = values.shape
    cos_z, sin_z = phase_tables(modes_z, jnp.arange(size_z, dtype=jnp.int32), size_z)
    wide = values.astype(jnp.float32)
    plane_real = (factor * jnp.einsum("xyzc,kz->xykc", wide, cos_z, precision=HIGH)).reshape(
        size_x, size_y, -1
    )
    plane_imag = (-factor * jnp.einsum("xyzc,kz->xykc", wide, sin_z, precision=HIGH)).reshape(
        size_x, size_y, -1
    )
    return (plane_real, plane_imag)


def line_modes(plane_real, plane_imag, freqs, places, length):
    cos_x, sin_x = phase_tables(freqs, places, length)
    line_real = jnp.einsum("kx,xyq->kyq", cos_x, plane_real, precision=HIGH) + jnp.einsum(
        "kx,xyq->kyq", sin_x, plane_imag, precision=HIGH
    )
    line_imag = jnp.einsum("kx,xyq->kyq", cos_x, plane_imag, precision=HIGH) - jnp.einsum(
        "kx,xyq->kyq", sin_x, plane_real, precision=HIGH
    )
    return jnp.stack([line_real, line_imag], axis=1)


def to_modes(values, factor, modes_x, modes_y, modes_z):
    rows_x, rows_y = (values.shape[0], values.shape[1])
    parts_x = lax.axis_size("gx")
    parts_y = lax.axis_size("gy")
    length_x = rows_x * parts_x
    length_y = rows_y * parts_y
    pencil = lax.all_to_all(values, "gx", split_axis=1, concat_axis=0, tiled=True)
    plane_real, plane_imag = plane_modes(pencil, factor, modes_z)
    whole = line_modes(
        plane_real, plane_imag, modes_x, jnp.arange(length_x, dtype=jnp.int32), length_x
    )
    spectrum = lax.all_to_all(whole, "gx", split_axis=0, concat_axis=2, tiled=True)
    places_y = lax.axis_index("gy") * rows_y + jnp.arange(rows_y, dtype=jnp.int32)
    cos_y, sin_y = phase_tables(modes_y, places_y, length_y)
    mode_real = jnp.einsum("ly,kyq->lkq", cos_y, spectrum[:, 0], precision=HIGH) + jnp.einsum(
        "ly,kyq->lkq", sin_y, spectrum[:, 1], precision=HIGH
    )
    mode_imag = jnp.einsum("ly,kyq->lkq", cos_y, spectrum[:, 1], precision=HIGH) - jnp.einsum(
        "ly,kyq->lkq", sin_y, spectrum[:, 0], precision=HIGH
    )
    return lax.psum_scatter(
        jnp.stack([mode_real, mode_imag], axis=2), "gy", scatter_dimension=0, tiled=True
    )


def to_cells(spectrum, factor, rows_x, rows_y, size_z, modes_x, modes_y, modes_z):
    length_x = rows_x * lax.axis_size("gx")
    length_y = rows_y * lax.axis_size("gy")
    places_y = lax.axis_index("gy") * rows_y + jnp.arange(rows_y, dtype=jnp.int32)
    places_x = lax.axis_index("gx") * rows_x + jnp.arange(rows_x, dtype=jnp.int32)
    piece = lax.all_gather(spectrum, "gy", axis=0, tiled=True)
    freqs = modes_y
    cos_y, sin_y = phase_tables(freqs, places_y, length_y)
    line_real = jnp.einsum("ly,lkq->kyq", cos_y, piece[:, :, 0], precision=HIGH) - jnp.einsum(
        "ly,lkq->kyq", sin_y, piece[:, :, 1], precision=HIGH
    )
    line_imag = jnp.einsum("ly,lkq->kyq", cos_y, piece[:, :, 1], precision=HIGH) + jnp.einsum(
        "ly,lkq->kyq", sin_y, piece[:, :, 0], precision=HIGH
    )
    line_real, line_imag = (line_real, line_imag)
    lines = jnp.stack([line_real, line_imag], axis=1)
    piece = lax.all_gather(lines, "gx", axis=0, tiled=True)
    freqs = modes_x
    cos_x, sin_x = phase_tables(freqs, places_x, length_x)
    plane_real = jnp.einsum("kx,kyq->xyq", cos_x, piece[:, 0], precision=HIGH) - jnp.einsum(
        "kx,kyq->xyq", sin_x, piece[:, 1], precision=HIGH
    )
    plane_imag = jnp.einsum("kx,kyq->xyq", cos_x, piece[:, 1], precision=HIGH) + jnp.einsum(
        "kx,kyq->xyq", sin_x, piece[:, 0], precision=HIGH
    )
    plane_real, plane_imag = (plane_real, plane_imag)
    count_z = modes_z.shape[0]
    plane_real = plane_real.reshape(rows_x, rows_y, count_z, -1)
    plane_imag = plane_imag.reshape(rows_x, rows_y, count_z, -1)
    cos_z, sin_z = phase_tables(modes_z, jnp.arange(size_z, dtype=jnp.int32), size_z)
    return factor * (
        jnp.einsum("xykc,kz->xyzc", plane_real, cos_z, precision=HIGH)
        - jnp.einsum("xykc,kz->xyzc", plane_imag, sin_z, precision=HIGH)
    )


def plain(features, cotangent, spectral_weight, conv_weight, modes_x, modes_y, modes_z):
    rows_x, rows_y, size_z, chans = features.shape
    count_x, count_y, count_z = (modes_x.shape[0], modes_y.shape[0], modes_z.shape[0])
    length_x = rows_x * lax.axis_size("gx")
    length_y = rows_y * lax.axis_size("gy")
    first = 1.0 / math.sqrt(length_x * length_y * size_z)
    second = 1.0 / math.sqrt(count_x * count_y * count_z)
    spectrum = to_modes(features, first, modes_x, modes_y, modes_z)
    local_y, local_x = (spectrum.shape[0], spectrum.shape[1])
    spec_real = spectrum[:, :, 0].reshape(local_y, local_x, count_z, chans)
    spec_imag = spectrum[:, :, 1].reshape(local_y, local_x, count_z, chans)
    weight = spectral_weight.astype(jnp.float32)
    real_w = weight[:, :, :, 0]
    imag_w = weight[:, :, :, 1]
    form = "abzoi,bazi->bazo"
    mixed_real = jnp.einsum(form, real_w, spec_real, precision=HIGH) - jnp.einsum(
        form, imag_w, spec_imag, precision=HIGH
    )
    mixed_imag = jnp.einsum(form, real_w, spec_imag, precision=HIGH) + jnp.einsum(
        form, imag_w, spec_real, precision=HIGH
    )
    mixed = jnp.stack(
        [mixed_real.reshape(local_y, local_x, -1), mixed_imag.reshape(local_y, local_x, -1)], axis=2
    )
    spectral = to_cells(mixed, second, rows_x, rows_y, size_z, modes_x, modes_y, modes_z)
    flat = features.reshape(-1, chans)
    conv = jnp.dot(flat, conv_weight, preferred_element_type=jnp.float32).reshape(spectral.shape)
    pre = spectral + conv
    cdf = normal_cdf(pre)
    activation = (pre * cdf).astype(jnp.bfloat16)
    slope = (cotangent.astype(jnp.float32) * (cdf + pre * normal_pdf(pre))).astype(jnp.bfloat16)
    back = to_modes(slope, second, modes_x, modes_y, modes_z)
    back_real = back[:, :, 0].reshape(local_y, local_x, count_z, chans)
    back_imag = back[:, :, 1].reshape(local_y, local_x, count_z, chans)
    outer = "bazo,bazi->abzoi"
    grad_real = jnp.einsum(outer, back_real, spec_real, precision=HIGH) + jnp.einsum(
        outer, back_imag, spec_imag, precision=HIGH
    )
    grad_imag = jnp.einsum(outer, back_imag, spec_real, precision=HIGH) - jnp.einsum(
        outer, back_real, spec_imag, precision=HIGH
    )
    grad_spectral = jnp.stack([grad_real, grad_imag], axis=3)
    adjoint = "abzoi,bazo->bazi"
    modes_real = jnp.einsum(adjoint, real_w, back_real, precision=HIGH) + jnp.einsum(
        adjoint, imag_w, back_imag, precision=HIGH
    )
    modes_imag = jnp.einsum(adjoint, real_w, back_imag, precision=HIGH) - jnp.einsum(
        adjoint, imag_w, back_real, precision=HIGH
    )
    back_modes = jnp.stack(
        [modes_real.reshape(local_y, local_x, -1), modes_imag.reshape(local_y, local_x, -1)], axis=2
    )
    spectral_back = to_cells(back_modes, first, rows_x, rows_y, size_z, modes_x, modes_y, modes_z)
    slope_flat = slope.reshape(-1, chans)
    conv_back = jnp.dot(slope_flat, conv_weight.T, preferred_element_type=jnp.float32).reshape(
        spectral.shape
    )
    grad_features = (spectral_back + conv_back).astype(jnp.bfloat16)
    local_conv = jnp.dot(flat.T, slope_flat, preferred_element_type=jnp.float32)
    grad_conv = first * lax.psum(local_conv, ("gx", "gy"))
    return (activation, grad_features, grad_spectral, grad_conv)


def fits(features, spectral_weight):
    rows_x, rows_y, size_z, chans = features.shape
    local_x, local_y, count_z = spectral_weight.shape[:3]
    parts_x, parts_y = lax.axis_size("gx"), lax.axis_size("gy")
    return (
        chans == 64
        and parts_x == 8
        and rows_y == 2 * parts_x
        and local_y == parts_x
        and rows_x * size_z == LANES
        and local_x * count_z == 2 * parts_x
        and parts_y == 4
        and all(n & (n - 1) == 0 for n in (rows_x * parts_x, rows_y * parts_y, size_z))
    )


def shards(features, cotangent, spectral_weight, *rest):
    run = fast if fits(features, spectral_weight) else plain
    return run(features, cotangent, spectral_weight, *rest)


def solution(mesh):
    placed = (
        P("gx", "gy", None, None),
        P("gx", "gy", None, None),
        P("gx", "gy", None, None, None, None),
        P(),
        P(),
        P(),
        P(),
    )
    return jax.shard_map(
        shards,
        mesh=mesh,
        in_specs=placed,
        out_specs=(
            P("gx", "gy", None, None),
            P("gx", "gy", None, None),
            P("gx", "gy", None, None, None, None),
            P(),
        ),
        check_vma=False,
    )
```

```python
import math

import jax
import jax.numpy as jnp
from jax import lax
from jax.experimental import pallas as pl
from jax.experimental.pallas import tpu as pltpu
from jax.sharding import PartitionSpec as P

HIGH = lax.Precision.HIGHEST
BF = jnp.bfloat16
F32 = jnp.float32
LANES = 128
EXTRA = 16
WIDE = 1024
SIDES = 4


def steps_of(parts):
    return list(range(0, parts, 2)) + list(range(1, parts, 2))


def cosine(turns, length):
    half = length // 2
    place = ((turns + length // 4) & (length - 1)) - half
    place = jnp.minimum(jnp.maximum(place, -half - place), half - place)
    angle = place.astype(F32) * (-2.0 * math.pi / length)
    square = angle * angle
    series = 1.0 / 362880.0 - square * (1.0 / 39916800.0)
    series = square * series - 1.0 / 5040.0
    series = square * series + 1.0 / 120.0
    series = square * series - 1.0 / 6.0
    return angle + angle * (square * series)


def pick(ref, index, places):
    out = jnp.zeros(index.shape, jnp.int32)
    for k, place in enumerate(places):
        out = jnp.where(index == k, ref[place], out)
    return out


def store_halves(ref, row, value):
    high = value.astype(BF)
    tall = ref.shape[0] // 2
    ref[row : row + value.shape[0]] = high
    ref[tall + row : tall + row + value.shape[0]] = (value - high.astype(F32)).astype(BF)


def grid_of(rows, cols):
    return (
        lax.broadcasted_iota(jnp.int32, (rows, cols), 0),
        lax.broadcasted_iota(jnp.int32, (rows, cols), 1),
    )


def table_kernel(size_z, *refs):
    sources, outs, places, sems = refs[:4], refs[5:11], refs[11:15], refs[15]
    line_ref, column_ref, cback_ref, lback_ref, pair_ref, turn_ref = outs
    copies = [
        pltpu.make_async_copy(source, place, sems.at[k])
        for k, (source, place) in enumerate(zip(sources, places))
    ]
    for copy in copies:
        copy.start()
    for copy in copies:
        copy.wait()
    mx_ref, my_ref, mz_ref, conv_ref = places
    parts_x, parts_y = lax.axis_size("gx"), lax.axis_size("gy")
    me_x, me_y = lax.axis_index("gx"), lax.axis_index("gy")
    count_x, count_y, count_z = mx_ref.shape[0], my_ref.shape[0], mz_ref.shape[0]
    local_x, local_y = count_x // parts_x, count_y // parts_y
    chans = conv_ref.shape[0]
    block = chans // parts_x
    length_x = line_ref.shape[1] // size_z
    whole = line_ref.shape[1]
    tile = 16

    rows_x = length_x // parts_x
    row, col = grid_of(tile, LANES)
    per = tile // count_z
    quarter = whole // 4
    base = pick(mz_ref, row % count_z, range(count_z)) * (col % size_z) * length_x
    inner = row // count_z
    offset = jnp.zeros(col.shape, jnp.int32)
    for k, step in enumerate(steps_of(parts_x)):
        offset = jnp.where(col == k, (me_x ^ step) * (rows_x * size_z), offset)
    modes = count_x * count_z
    for start in range(0, count_x, per):
        freq = pick(mx_ref, inner, range(start, start + per))
        turns = freq * (col // size_z * size_z) + base
        cos, sin = cosine(turns, whole), cosine(turns - quarter, whole)
        turns = freq * offset
        cos_step, sin_step = cosine(turns, whole), cosine(turns - quarter, whole)
        at = start * count_z
        for k in range(parts_x):
            cos_k = jnp.broadcast_to(cos_step[:, k : k + 1], cos.shape)
            sin_k = jnp.broadcast_to(sin_step[:, k : k + 1], cos.shape)
            columns = line_ref.at[:, k * LANES : (k + 1) * LANES]
            store_halves(columns, at, cos * cos_k - sin * sin_k)
            store_halves(columns, at + modes, -sin * cos_k - cos * sin_k)

    rows_y = column_ref.shape[0] // 4 // block
    length_y = rows_y * parts_y
    per = tile // block
    ky = col // block % local_y
    shift = col // (LANES // 2) * (length_y // 4)
    same = row % block == col % block
    low = col < LANES // 2
    inner = row // block + me_y * rows_y
    for gy in range(parts_y):
        freq = pick(my_ref, ky, range(gy * local_y, (gy + 1) * local_y))
        columns = column_ref.at[:, gy * LANES : (gy + 1) * LANES]
        for start in range(0, rows_y, per):
            value = jnp.where(same, cosine(freq * (inner + start) + shift, length_y), 0.0)
            store_halves(columns, start * block, value)
            turned = pltpu.roll(value, LANES // 2, 1)
            store_halves(columns, (rows_y + start) * block, jnp.where(low, -turned, turned))

    row, col = grid_of(2 * rows_y, cback_ref.shape[1])
    places = [
        (me_y + parts_y - step) % parts_y * local_y + k for step in range(parts_y) for k in range(local_y)
    ]
    freq = pick(my_ref, col // (2 * local_y) * local_y + col % local_y, places)
    shift = (col // local_y % 2 - row // rows_y) * (length_y // 4)
    store_halves(cback_ref, 0, cosine(freq * (row % rows_y + me_y * rows_y) + shift, length_y))

    row, col = grid_of(tile, lback_ref.shape[1])
    modes = local_x * count_z
    kx = col // (2 * modes) * local_x + col // count_z % local_x
    places = [(me_x ^ step) * local_x + k for step in steps_of(parts_x) for k in range(local_x)]
    freq = pick(mx_ref, kx, places) * size_z
    base = pick(mz_ref, col % count_z, range(count_z)) * (row % size_z) * length_x
    base = base + col // modes % 2 * (whole // 4)
    inner = row // size_z + me_x * rows_x
    per = tile // size_z
    for start in range(0, rows_x, per):
        store_halves(lback_ref, start * size_z, cosine(freq * (inner + start) + base, whole))

    conv = conv_ref[...].astype(F32)
    none = jnp.zeros_like(conv)
    for ref, value in ((pair_ref, conv), (turn_ref, conv.T)):
        ref[:chans] = jnp.concatenate([value, none], axis=1).astype(BF)
        ref[chans:] = jnp.concatenate([none, value], axis=1).astype(BF)


def dot(a, b, dims=((1,), (0,))):
    return lax.dot_general(a, b, (dims, ((), ())), preferred_element_type=F32)


def pairs_of(ref):
    size_x, size_y, size_z, chans = ref.shape
    out = []
    for y in range(size_y // 2):
        low = ref[:, y, :, :].astype(F32).reshape(size_x * size_z, chans)
        high = ref[:, y + size_y // 2, :, :].astype(F32).reshape(size_x * size_z, chans)
        out.append(jnp.concatenate([low, high], axis=1))
    return out


def block_transpose(arrays, block):
    count = len(arrays)
    arrays = list(arrays)
    lanes = arrays[0].shape[1]
    index = lax.broadcasted_iota(jnp.int32, arrays[0].shape, 1) // block % count
    step = 1
    while step < count:
        upper = (index & step) != 0
        for p in range(count):
            if p & step:
                continue
            a, b = arrays[p], arrays[p | step]
            arrays[p] = jnp.where(upper, pltpu.roll(b, step * block, 1), a)
            arrays[p | step] = jnp.where(upper, b, pltpu.roll(a, lanes - step * block, 1))
        step *= 2
    return arrays


def split_rows(value):
    high = value.astype(BF)
    return jnp.concatenate([high, (value - high.astype(F32)).astype(BF)], axis=0)


def normal_cdf(values):
    return 0.5 * (1.0 + lax.erf(values * (1.0 / math.sqrt(2.0))))


def normal_pdf(values):
    return jnp.exp(-0.5 * values * values) * (1.0 / math.sqrt(2.0 * math.pi))


def store_steps(chunk_ref, send_refs):
    me = lax.axis_index("gx")
    for t, ref in enumerate(send_refs):
        for r in range(2):
            ref[r] = chunk_ref[me ^ (2 * t + r)]


def spread_kernel(field_ref, *refs):
    send_refs, pairs_ref, chunk_ref = refs[:-2], refs[-2], refs[-1]
    pairs = pairs_of(field_ref)
    for p, pair in enumerate(pairs):
        pairs_ref[p] = pair.astype(BF)
    for b, chunk in enumerate(block_transpose(pairs, field_ref.shape[3] // len(pairs))):
        chunk_ref[b] = chunk.astype(BF)
    store_steps(chunk_ref, send_refs)


def pairs_kernel(field_ref, pairs_ref):
    for p, pair in enumerate(pairs_of(field_ref)):
        pairs_ref[p] = pair.astype(BF)


def joined(value):
    chans = value.shape[1] // 2
    return value[:, :chans].astype(F32) + value[:, chans:].astype(F32)


def parted(value):
    high = value.astype(BF).astype(F32)
    both = jnp.concatenate([high, value - high], axis=1)
    rest = jnp.zeros((EXTRA - both.shape[0], both.shape[1]), F32)
    return jnp.concatenate([both, rest], axis=0).astype(BF)


def transform_kernel(scale, parts_x, parts_y, line_ref, column_ref, *refs):
    recv_refs, send_ref, extra = refs[:parts_x], refs[parts_x], refs[parts_x + 1 :]
    rows = line_ref.shape[1] // parts_x
    own = [ref.at[k // (parts_x // 2)] for k, ref in enumerate(recv_refs)]
    if extra:
        total = joined(own[0][rows:, :])
        for ref in own[1:]:
            total = total + joined(ref[rows:, :])
        extra[0][...] = parted(total[: LANES // 2 // parts_x])
    data = jnp.concatenate([ref[:rows, :] for ref in own], axis=0)
    lines = dot(line_ref[...], data)
    half = lines.shape[0] // 2
    lines = lines[:half] + lines[half:]
    count = half // 2
    both = jnp.concatenate([lines[:count], lines[count:]], axis=1)
    depth = both.shape[1]
    high = both.astype(BF)
    low = (both - high.astype(F32)).astype(BF)
    modes = dot(split_rows(both), column_ref[:depth, :])
    modes = modes[:count] + modes[count:] + dot(high, column_ref[depth:, :])
    modes = modes * scale
    tall = count // parts_x
    for gx in range(parts_x):
        for gy in range(parts_y):
            send_ref[gx * parts_y + gy] = modes[
                gx * tall : (gx + 1) * tall, gy * LANES : (gy + 1) * LANES
            ].astype(BF)


def sum_parts(recv_ref, parts_y):
    parts = recv_ref.shape[0] // parts_y
    out = []
    for b in range(parts):
        total = recv_ref[b * parts_y].astype(F32)
        for gy in range(1, parts_y):
            total = total + recv_ref[b * parts_y + gy].astype(F32)
        out.append(total)
    return out


def lay_modes(scratch, send_ref, count_y, rows):
    chans = 64
    for m in range(0, rows, 2):
        parts = []
        for part in range(2):
            first = scratch[pl.ds(part * rows + m, count_y, stride=2 * rows), :chans]
            second = scratch[pl.ds(part * rows + m + 1, count_y, stride=2 * rows), :chans]
            parts.append(jnp.concatenate([first, second], axis=1))
        send_ref[:, m * chans : (m + 2) * chans] = jnp.concatenate(parts, axis=0).astype(send_ref.dtype)


def mix_kernel(forward, parts_y, recv_ref, weight_ref, *refs):
    send_ref, spec_ref, scratch = refs[-3:]
    if len(refs) == 4:
        send_ref[:, WIDE:] = refs[0][...]
    size_x, size_y, size_z, _, chans, _ = weight_ref.shape
    rows = size_x * size_z
    spectra = block_transpose(sum_parts(recv_ref, parts_y), chans // size_y)
    for ky in range(size_y):
        spec = spectra[ky]
        spec_ref[ky] = spec
        turned = pltpu.roll(spec, chans, 1)
        if forward:
            both = jnp.concatenate([spec, turned], axis=0)[:, :chans].T
            high = both.astype(BF)
            both = jnp.concatenate([high, (both - high.astype(F32)).astype(BF)], axis=1)
        else:
            first = lax.broadcasted_iota(jnp.int32, spec.shape, 1) < chans
            both = split_rows(jnp.concatenate([spec, jnp.where(first, turned, -turned)], axis=0))
        if forward:
            wide = [weight_ref[m // size_z, ky, m % size_z].reshape(2 * chans, chans) for m in range(rows)]
            wide = [jnp.concatenate(wide[m : m + 2], axis=1) for m in range(0, rows, 2)]
            mode = lax.broadcasted_iota(jnp.int32, both.shape, 1) % rows
            own = [jnp.where(mode == m, both, jnp.zeros_like(both)) for m in range(rows)]
            total = dot(jnp.concatenate(wide, axis=1), jnp.concatenate(own, axis=0))
            total = total.T
        else:
            stack = jnp.concatenate(
                [weight_ref[kx, ky].reshape(size_z * 2 * chans, chans) for kx in range(size_x)], axis=0
            )
            mode = lax.broadcasted_iota(jnp.int32, both.shape, 0) % rows
            own = [jnp.where(mode == m, both, jnp.zeros_like(both)) for m in range(rows)]
            total = dot(jnp.concatenate(own, axis=1), stack)
        total = total[: 2 * rows] + total[2 * rows :]
        if forward:
            real, imag = total[:rows], total[rows:]
            mixed = jnp.concatenate(
                [
                    real[:, :chans] - imag[:, chans:],
                    imag[:, :chans] + real[:, chans:],
                ],
                axis=0,
            )
        else:
            mixed = total
        scratch[ky * 2 * rows : (ky + 1) * 2 * rows, :chans] = mixed
    lay_modes(scratch, send_ref, size_y, rows)


def column_kernel(table_ref, *refs):
    steps = len(refs) - 2
    send_ref, scratch = refs[steps], refs[steps + 1]
    chans = 64
    if refs[0].shape[1] > WIDE:
        total = joined(refs[0][:, WIDE:])
        for s in range(1, steps):
            total = total + joined(refs[s][:, WIDE:])
        send_ref[:EXTRA, WIDE:] = parted(total[: EXTRA // 2])
        send_ref[EXTRA:, WIDE:] = jnp.zeros((send_ref.shape[0] - EXTRA, LANES), BF)
    data = jnp.concatenate([refs[s][:, :WIDE] for s in range(steps)], axis=0)
    lines = dot(table_ref[...], data)
    half = lines.shape[0] // 2
    lines = lines[:half] + lines[half:]
    size_y = half // 2
    count = WIDE // chans
    for m in range(0, count, 2):
        pair = lines[:, m * chans : (m + 2) * chans]
        scratch[m * half : (m + 1) * half, :] = pair
        scratch[(m + 1) * half : (m + 2) * half, :] = pltpu.roll(pair, chans, 1)
    for part in range(2):
        for y in range(size_y // 2):
            first = scratch[pl.ds(part * size_y + y, count, stride=half), :chans]
            second = scratch[pl.ds(part * size_y + y + size_y // 2, count, stride=half), :chans]
            send_ref[part * count : (part + 1) * count, y * 2 * chans : (y + 1) * 2 * chans] = (
                jnp.concatenate([first, second], axis=1).astype(BF)
            )


def cells_of(table_ref, recv_refs, scale):
    data = jnp.concatenate([ref[:, :WIDE] for ref in recv_refs], axis=0)
    cells = dot(table_ref[...], data)
    half = cells.shape[0] // 2
    return (cells[:half] + cells[half:]) * scale


def store_pair(out_ref, p, value):
    size_x, size_y, size_z, chans = out_ref.shape
    out_ref[:, p, :, :] = value[:, :chans].reshape(size_x, size_z, chans).astype(out_ref.dtype)
    out_ref[:, p + size_y // 2, :, :] = (
        value[:, chans:].reshape(size_x, size_z, chans).astype(out_ref.dtype)
    )


def point_kernel(scale, table_ref, *refs):
    recv_refs, refs = refs[: 2 * SIDES], refs[2 * SIDES :]
    conv_ref, field_ref, cot_ref, act_ref, slope_ref = refs[:5]
    send_refs, chunk_ref = refs[5:-1], refs[-1]
    cells = cells_of(table_ref, recv_refs, scale)
    count = field_ref.shape[0]
    slopes = []
    grad = jnp.zeros((LANES, LANES), F32)
    for p in range(count):
        field = field_ref[p]
        pre = cells[:, p * LANES : (p + 1) * LANES] + dot(field, conv_ref[...])
        cdf = normal_cdf(pre)
        store_pair(act_ref, p, pre * cdf)
        slope = cot_ref[p].astype(F32) * (cdf + pre * normal_pdf(pre))
        narrow = slope.astype(BF)
        slope_ref[p] = narrow
        slopes.append(narrow.astype(F32))
        grad = grad + dot(field, narrow, ((0,), (0,)))
    rows = slopes[0].shape[0]
    chans = LANES // 2
    grad = grad[:chans, :chans] + grad[chans:, chans:]
    block = chans // count
    for b, chunk in enumerate(block_transpose(slopes, block)):
        chunk_ref[b, :rows, :] = chunk.astype(BF)
        chunk_ref[b, rows:, :] = parted(grad[b * block : (b + 1) * block])
    store_steps(chunk_ref, send_refs)


def last_kernel(scale, table_ref, *refs):
    conv_ref, slope_ref, out_ref, grad_ref = refs[-4:]
    recv_refs = refs[:-4]
    block = grad_ref.shape[0] // len(recv_refs)
    me = lax.axis_index("gx")
    for step, ref in zip(steps_of(len(recv_refs)), recv_refs):
        total = joined(ref[:EXTRA, WIDE:])
        grad_ref[pl.ds(pl.multiple_of((me ^ step) * block, block), block), :] = total[:block] * scale
    cells = cells_of(table_ref, recv_refs, scale)
    for p in range(slope_ref.shape[0]):
        store_pair(out_ref, p, cells[:, p * LANES : (p + 1) * LANES] + dot(slope_ref[p], conv_ref[...]))


def outer_kernel(spec_ref, back_ref, out_ref, held_ref, sems):
    size_x, size_y, size_z, _, chans, _ = held_ref.shape
    rows = size_x * size_z
    first = lax.broadcasted_iota(jnp.int32, back_ref.shape[1:], 1) < chans
    mode = lax.broadcasted_iota(jnp.int32, (6 * rows, chans), 0) % rows
    copies = []
    for ky in range(size_y):
        back, spec = back_ref[ky], spec_ref[ky]
        turned = pltpu.roll(back, chans, 1)
        left = jnp.concatenate([back, jnp.where(first, turned, -turned)], axis=0).T
        right = jnp.concatenate([spec, pltpu.roll(spec, chans, 1)], axis=0)[:, :chans]
        left_high, right_high = left.astype(BF), right.astype(BF)
        left_low = (left - left_high.astype(F32)).astype(BF)
        right_low = (right - right_high.astype(F32)).astype(BF)
        lefts = jnp.concatenate([left_high, left_high, left_low], axis=1)
        rights = jnp.concatenate([right_high, right_low, right_high], axis=0)
        for m in range(rows):
            own = jnp.where(mode == m, rights, jnp.zeros_like(rights))
            held_ref[m // size_z, ky, m % size_z] = dot(lefts, own).reshape(2, chans, chans)
        copy = pltpu.make_async_copy(held_ref.at[:, ky], out_ref.at[:, ky], sems.at[ky])
        copy.start()
        copies.append(copy)
    for copy in copies:
        copy.wait()


def call(kernel, outs, *args, scratch=()):
    params = pltpu.CompilerParams(vmem_limit_bytes=16 * 2**20)
    return pl.pallas_call(kernel, out_shape=outs, scratch_shapes=list(scratch), compiler_params=params)(*args)


def bind(kernel, *static):
    def bound(*refs):
        return kernel(*static, *refs)

    return bound


def sds(shape, dtype):
    return jax.ShapeDtypeStruct(shape, dtype)


def fast(features, cotangent, spectral_weight, conv_weight, modes_x, modes_y, modes_z):
    rows_x, rows_y, size_z, chans = features.shape
    local_x, local_y, count_z = spectral_weight.shape[:3]
    parts_x, parts_y = lax.axis_size("gx"), lax.axis_size("gy")
    length_x, length_y = rows_x * parts_x, rows_y * parts_y
    block = chans // parts_x
    cells = rows_x * size_z
    modes = local_x * count_z
    half_y = rows_y // 2
    first = 1.0 / math.sqrt(length_x * length_y * size_z)
    second = 1.0 / math.sqrt(modes_x.shape[0] * modes_y.shape[0] * count_z)

    *send, field = call(
        spread_kernel,
        [sds((2, cells, LANES), BF)] * SIDES + [sds((half_y, cells, LANES), BF)],
        features,
        scratch=[pltpu.VMEM((parts_x, cells, LANES), BF)],
    )
    cot = call(pairs_kernel, sds((half_y, cells, LANES), BF), cotangent)
    outside = pl.BlockSpec(memory_space=pltpu.HBM)
    inside = pl.BlockSpec(memory_space=pltpu.VMEM)
    line_table, column_table, column_back, line_back, conv_pair, conv_turn = pl.pallas_call(
        bind(table_kernel, size_z),
        in_specs=[outside] * 5,
        out_shape=(
            sds((4 * modes_x.shape[0] * count_z, length_x * size_z), BF),
            sds((4 * LANES, 4 * LANES), BF),
            sds((4 * rows_y, 2 * modes_y.shape[0]), BF),
            sds((2 * cells, 2 * modes_x.shape[0] * count_z), BF),
            sds((LANES, LANES), BF),
            sds((LANES, LANES), BF),
        ),
        scratch_shapes=[
            pltpu.SMEM(modes_x.shape, jnp.int32),
            pltpu.SMEM(modes_y.shape, jnp.int32),
            pltpu.SMEM(modes_z.shape, jnp.int32),
            pltpu.VMEM(conv_weight.shape, BF),
            pltpu.SemaphoreType.DMA((4,)),
        ],
        compiler_params=pltpu.CompilerParams(vmem_limit_bytes=16 * 2**20),
    )(*(pltpu.with_memory_space_constraint(x, pltpu.HBM) for x in (modes_x, modes_y, modes_z, conv_weight, spectral_weight)))

    def cross(pieces, beside=None):
        pieces = pieces[:1] + [
            lax.ppermute(piece, "gx", [(i, i ^ 2 * t) for i in range(parts_x)])
            for t, piece in enumerate(pieces)
            if t
        ]
        if beside is not None:
            pieces[-1], beside = lax.optimization_barrier((pieces[-1], beside))
        swap = [(i, i ^ 1) for i in range(parts_x)]
        pieces = pieces + [lax.ppermute(piece, "gx", swap) for piece in pieces]
        return pieces, beside

    def to_modes(send, factor, extra, tables):
        outs = [sds((parts_x * parts_y, modes, LANES), BF)]
        if extra:
            outs.append(sds((EXTRA, LANES), BF))
        kernel = bind(transform_kernel, factor, parts_x, parts_y)
        pieces, ready = cross(send, None if extra else tables)
        tables = tables if ready is None else ready
        send, *rest = call(kernel, outs, *tables, *pieces)
        return lax.all_to_all(send, ("gx", "gy"), 0, 0, tiled=True), rest, tables

    def mix(recv, forward, rest):
        return call(
            bind(mix_kernel, forward, parts_y),
            (
                sds((2 * local_y, WIDE + len(rest) * LANES), BF),
                sds((local_y, modes, LANES), F32),
            ),
            recv,
            spectral_weight,
            *rest,
            scratch=[pltpu.VMEM((local_y * 2 * modes, LANES), F32)],
        )

    def to_lines(send, beside=None):
        pieces = [send]
        for step in range(1, parts_y):
            ring = [(i, (i + step) % parts_y) for i in range(parts_y)]
            pieces.append(lax.ppermute(send, "gy", ring))
        if beside is not None:
            pieces[-1], beside = lax.optimization_barrier((pieces[-1], beside))
        lines = call(
            column_kernel,
            sds((2 * modes, send.shape[1]), BF),
            column_back,
            *pieces,
            scratch=[pltpu.VMEM((modes * 2 * rows_y, LANES), F32)],
        )
        return cross([lines] * SIDES)[0], beside


    recv, _, tables = to_modes(send, first, False, (line_table, column_table))
    send, spec = mix(recv, True, [])
    pieces, _ = to_lines(send)
    activation, slope, *send = call(
        bind(point_kernel, second),
        (
            sds(features.shape, BF),
            sds((half_y, cells, LANES), BF),
        )
        + (sds((2, cells + EXTRA, LANES), BF),) * SIDES,
        line_back,
        *pieces,
        conv_pair,
        field,
        cot,
        scratch=[pltpu.VMEM((parts_x, cells + EXTRA, LANES), BF)],
    )
    recv, rest, _ = to_modes(send, second, True, tables)
    send, back = mix(recv, False, rest)
    grad_spectral = pl.pallas_call(
        outer_kernel,
        in_specs=[inside] * 2,
        out_specs=outside,
        out_shape=sds(spectral_weight.shape, F32),
        scratch_shapes=[pltpu.VMEM(spectral_weight.shape, F32), pltpu.SemaphoreType.DMA((local_y,))],
        compiler_params=pltpu.CompilerParams(vmem_limit_bytes=16 * 2**20),
    )(spec, back)
    pieces, grad_spectral = to_lines(send, grad_spectral)
    grad_features, grad_conv = call(
        bind(last_kernel, first),
        (sds(features.shape, BF), sds((chans, chans), F32)),
        line_back,
        *pieces,
        conv_turn,
        slope,
    )
    return activation, grad_features, grad_spectral, grad_conv


def phase_tables(freqs, places, length):
    product = freqs[:, None] * places[None, :] % length
    angles = product.astype(jnp.float32) * (2.0 * math.pi / length)
    return (jnp.cos(angles), jnp.sin(angles))


def plane_modes(values, factor, modes_z):
    size_x, size_y, size_z, chans = values.shape
    cos_z, sin_z = phase_tables(modes_z, jnp.arange(size_z, dtype=jnp.int32), size_z)
    wide = values.astype(jnp.float32)
    plane_real = (factor * jnp.einsum("xyzc,kz->xykc", wide, cos_z, precision=HIGH)).reshape(
        size_x, size_y, -1
    )
    plane_imag = (-factor * jnp.einsum("xyzc,kz->xykc", wide, sin_z, precision=HIGH)).reshape(
        size_x, size_y, -1
    )
    return (plane_real, plane_imag)


def line_modes(plane_real, plane_imag, freqs, places, length):
    cos_x, sin_x = phase_tables(freqs, places, length)
    line_real = jnp.einsum("kx,xyq->kyq", cos_x, plane_real, precision=HIGH) + jnp.einsum(
        "kx,xyq->kyq", sin_x, plane_imag, precision=HIGH
    )
    line_imag = jnp.einsum("kx,xyq->kyq", cos_x, plane_imag, precision=HIGH) - jnp.einsum(
        "kx,xyq->kyq", sin_x, plane_real, precision=HIGH
    )
    return jnp.stack([line_real, line_imag], axis=1)


def to_modes(values, factor, modes_x, modes_y, modes_z):
    rows_x, rows_y = (values.shape[0], values.shape[1])
    parts_x = lax.axis_size("gx")
    parts_y = lax.axis_size("gy")
    length_x = rows_x * parts_x
    length_y = rows_y * parts_y
    pencil = lax.all_to_all(values, "gx", split_axis=1, concat_axis=0, tiled=True)
    plane_real, plane_imag = plane_modes(pencil, factor, modes_z)
    whole = line_modes(
        plane_real, plane_imag, modes_x, jnp.arange(length_x, dtype=jnp.int32), length_x
    )
    spectrum = lax.all_to_all(whole, "gx", split_axis=0, concat_axis=2, tiled=True)
    places_y = lax.axis_index("gy") * rows_y + jnp.arange(rows_y, dtype=jnp.int32)
    cos_y, sin_y = phase_tables(modes_y, places_y, length_y)
    mode_real = jnp.einsum("ly,kyq->lkq", cos_y, spectrum[:, 0], precision=HIGH) + jnp.einsum(
        "ly,kyq->lkq", sin_y, spectrum[:, 1], precision=HIGH
    )
    mode_imag = jnp.einsum("ly,kyq->lkq", cos_y, spectrum[:, 1], precision=HIGH) - jnp.einsum(
        "ly,kyq->lkq", sin_y, spectrum[:, 0], precision=HIGH
    )
    return lax.psum_scatter(
        jnp.stack([mode_real, mode_imag], axis=2), "gy", scatter_dimension=0, tiled=True
    )


def to_cells(spectrum, factor, rows_x, rows_y, size_z, modes_x, modes_y, modes_z):
    length_x = rows_x * lax.axis_size("gx")
    length_y = rows_y * lax.axis_size("gy")
    places_y = lax.axis_index("gy") * rows_y + jnp.arange(rows_y, dtype=jnp.int32)
    places_x = lax.axis_index("gx") * rows_x + jnp.arange(rows_x, dtype=jnp.int32)
    piece = lax.all_gather(spectrum, "gy", axis=0, tiled=True)
    freqs = modes_y
    cos_y, sin_y = phase_tables(freqs, places_y, length_y)
    line_real = jnp.einsum("ly,lkq->kyq", cos_y, piece[:, :, 0], precision=HIGH) - jnp.einsum(
        "ly,lkq->kyq", sin_y, piece[:, :, 1], precision=HIGH
    )
    line_imag = jnp.einsum("ly,lkq->kyq", cos_y, piece[:, :, 1], precision=HIGH) + jnp.einsum(
        "ly,lkq->kyq", sin_y, piece[:, :, 0], precision=HIGH
    )
    line_real, line_imag = (line_real, line_imag)
    lines = jnp.stack([line_real, line_imag], axis=1)
    piece = lax.all_gather(lines, "gx", axis=0, tiled=True)
    freqs = modes_x
    cos_x, sin_x = phase_tables(freqs, places_x, length_x)
    plane_real = jnp.einsum("kx,kyq->xyq", cos_x, piece[:, 0], precision=HIGH) - jnp.einsum(
        "kx,kyq->xyq", sin_x, piece[:, 1], precision=HIGH
    )
    plane_imag = jnp.einsum("kx,kyq->xyq", cos_x, piece[:, 1], precision=HIGH) + jnp.einsum(
        "kx,kyq->xyq", sin_x, piece[:, 0], precision=HIGH
    )
    plane_real, plane_imag = (plane_real, plane_imag)
    count_z = modes_z.shape[0]
    plane_real = plane_real.reshape(rows_x, rows_y, count_z, -1)
    plane_imag = plane_imag.reshape(rows_x, rows_y, count_z, -1)
    cos_z, sin_z = phase_tables(modes_z, jnp.arange(size_z, dtype=jnp.int32), size_z)
    return factor * (
        jnp.einsum("xykc,kz->xyzc", plane_real, cos_z, precision=HIGH)
        - jnp.einsum("xykc,kz->xyzc", plane_imag, sin_z, precision=HIGH)
    )


def plain(features, cotangent, spectral_weight, conv_weight, modes_x, modes_y, modes_z):
    rows_x, rows_y, size_z, chans = features.shape
    count_x, count_y, count_z = (modes_x.shape[0], modes_y.shape[0], modes_z.shape[0])
    length_x = rows_x * lax.axis_size("gx")
    length_y = rows_y * lax.axis_size("gy")
    first = 1.0 / math.sqrt(length_x * length_y * size_z)
    second = 1.0 / math.sqrt(count_x * count_y * count_z)
    spectrum = to_modes(features, first, modes_x, modes_y, modes_z)
    local_y, local_x = (spectrum.shape[0], spectrum.shape[1])
    spec_real = spectrum[:, :, 0].reshape(local_y, local_x, count_z, chans)
    spec_imag = spectrum[:, :, 1].reshape(local_y, local_x, count_z, chans)
    weight = spectral_weight.astype(jnp.float32)
    real_w = weight[:, :, :, 0]
    imag_w = weight[:, :, :, 1]
    form = "abzoi,bazi->bazo"
    mixed_real = jnp.einsum(form, real_w, spec_real, precision=HIGH) - jnp.einsum(
        form, imag_w, spec_imag, precision=HIGH
    )
    mixed_imag = jnp.einsum(form, real_w, spec_imag, precision=HIGH) + jnp.einsum(
        form, imag_w, spec_real, precision=HIGH
    )
    mixed = jnp.stack(
        [mixed_real.reshape(local_y, local_x, -1), mixed_imag.reshape(local_y, local_x, -1)], axis=2
    )
    spectral = to_cells(mixed, second, rows_x, rows_y, size_z, modes_x, modes_y, modes_z)
    flat = features.reshape(-1, chans)
    conv = jnp.dot(flat, conv_weight, preferred_element_type=jnp.float32).reshape(spectral.shape)
    pre = spectral + conv
    cdf = normal_cdf(pre)
    activation = (pre * cdf).astype(jnp.bfloat16)
    slope = (cotangent.astype(jnp.float32) * (cdf + pre * normal_pdf(pre))).astype(jnp.bfloat16)
    back = to_modes(slope, second, modes_x, modes_y, modes_z)
    back_real = back[:, :, 0].reshape(local_y, local_x, count_z, chans)
    back_imag = back[:, :, 1].reshape(local_y, local_x, count_z, chans)
    outer = "bazo,bazi->abzoi"
    grad_real = jnp.einsum(outer, back_real, spec_real, precision=HIGH) + jnp.einsum(
        outer, back_imag, spec_imag, precision=HIGH
    )
    grad_imag = jnp.einsum(outer, back_imag, spec_real, precision=HIGH) - jnp.einsum(
        outer, back_real, spec_imag, precision=HIGH
    )
    grad_spectral = jnp.stack([grad_real, grad_imag], axis=3)
    adjoint = "abzoi,bazo->bazi"
    modes_real = jnp.einsum(adjoint, real_w, back_real, precision=HIGH) + jnp.einsum(
        adjoint, imag_w, back_imag, precision=HIGH
    )
    modes_imag = jnp.einsum(adjoint, real_w, back_imag, precision=HIGH) - jnp.einsum(
        adjoint, imag_w, back_real, precision=HIGH
    )
    back_modes = jnp.stack(
        [modes_real.reshape(local_y, local_x, -1), modes_imag.reshape(local_y, local_x, -1)], axis=2
    )
    spectral_back = to_cells(back_modes, first, rows_x, rows_y, size_z, modes_x, modes_y, modes_z)
    slope_flat = slope.reshape(-1, chans)
    conv_back = jnp.dot(slope_flat, conv_weight.T, preferred_element_type=jnp.float32).reshape(
        spectral.shape
    )
    grad_features = (spectral_back + conv_back).astype(jnp.bfloat16)
    local_conv = jnp.dot(flat.T, slope_flat, preferred_element_type=jnp.float32)
    grad_conv = first * lax.psum(local_conv, ("gx", "gy"))
    return (activation, grad_features, grad_spectral, grad_conv)


def fits(features, spectral_weight):
    rows_x, rows_y, size_z, chans = features.shape
    local_x, local_y, count_z = spectral_weight.shape[:3]
    parts_x, parts_y = lax.axis_size("gx"), lax.axis_size("gy")
    return (
        chans == 64
        and parts_x == 8
        and rows_y == 2 * parts_x
        and local_y == parts_x
        and rows_x * size_z == LANES
        and local_x * count_z == 2 * parts_x
        and parts_y == 4
        and all(n & (n - 1) == 0 for n in (rows_x * parts_x, rows_y * parts_y, size_z))
    )


def shards(features, cotangent, spectral_weight, *rest):
    run = fast if fits(features, spectral_weight) else plain
    return run(features, cotangent, spectral_weight, *rest)


def solution(mesh):
    placed = (
        P("gx", "gy", None, None),
        P("gx", "gy", None, None),
        P("gx", "gy", None, None, None, None),
        P(),
        P(),
        P(),
        P(),
    )
    return jax.shard_map(
        shards,
        mesh=mesh,
        in_specs=placed,
        out_specs=(
            P("gx", "gy", None, None),
            P("gx", "gy", None, None),
            P("gx", "gy", None, None, None, None),
            P(),
        ),
        check_vma=False,
    )
```

```python
import math

import jax
import jax.numpy as jnp
from jax import lax
from jax.experimental import pallas as pl
from jax.experimental.pallas import tpu as pltpu
from jax.sharding import PartitionSpec as P

HIGH = lax.Precision.HIGHEST
BF = jnp.bfloat16
F32 = jnp.float32
LANES = 128
EXTRA = 16
WIDE = 1024
SIDES = 4


def steps_of(parts):
    return list(range(0, parts, 2)) + list(range(1, parts, 2))


def cosine(turns, length):
    half = length // 2
    place = ((turns + length // 4) & (length - 1)) - half
    place = jnp.minimum(jnp.maximum(place, -half - place), half - place)
    angle = place.astype(F32) * (-2.0 * math.pi / length)
    square = angle * angle
    series = 1.0 / 362880.0 - square * (1.0 / 39916800.0)
    series = square * series - 1.0 / 5040.0
    series = square * series + 1.0 / 120.0
    series = square * series - 1.0 / 6.0
    return angle + angle * (square * series)


def pick(ref, index, places):
    out = jnp.zeros(index.shape, jnp.int32)
    for k, place in enumerate(places):
        out = jnp.where(index == k, ref[place], out)
    return out


def store_halves(ref, row, value):
    high = value.astype(BF)
    tall = ref.shape[0] // 2
    ref[row : row + value.shape[0]] = high
    ref[tall + row : tall + row + value.shape[0]] = (value - high.astype(F32)).astype(BF)


def grid_of(rows, cols):
    return (
        lax.broadcasted_iota(jnp.int32, (rows, cols), 0),
        lax.broadcasted_iota(jnp.int32, (rows, cols), 1),
    )


def table_kernel(size_z, *refs):
    sources, outs, places, sems = refs[:4], refs[5:11], refs[11:15], refs[15]
    line_ref, column_ref, cback_ref, lback_ref, pair_ref, turn_ref = outs
    copies = [
        pltpu.make_async_copy(source, place, sems.at[k])
        for k, (source, place) in enumerate(zip(sources, places))
    ]
    for copy in copies:
        copy.start()
    for copy in copies:
        copy.wait()
    mx_ref, my_ref, mz_ref, conv_ref = places
    parts_x, parts_y = lax.axis_size("gx"), lax.axis_size("gy")
    me_x, me_y = lax.axis_index("gx"), lax.axis_index("gy")
    count_x, count_y, count_z = mx_ref.shape[0], my_ref.shape[0], mz_ref.shape[0]
    local_x, local_y = count_x // parts_x, count_y // parts_y
    chans = conv_ref.shape[0]
    block = chans // parts_x
    length_x = line_ref.shape[1] // size_z
    whole = line_ref.shape[1]
    tile = 16

    rows_x = length_x // parts_x
    row, col = grid_of(tile, LANES)
    per = tile // count_z
    quarter = whole // 4
    base = pick(mz_ref, row % count_z, range(count_z)) * (col % size_z) * length_x
    inner = row // count_z
    offset = jnp.zeros(col.shape, jnp.int32)
    for k, step in enumerate(steps_of(parts_x)):
        offset = jnp.where(col == k, (me_x ^ step) * (rows_x * size_z), offset)
    modes = count_x * count_z
    for start in range(0, count_x, per):
        freq = pick(mx_ref, inner, range(start, start + per))
        turns = freq * (col // size_z * size_z) + base
        cos, sin = cosine(turns, whole), cosine(turns - quarter, whole)
        turns = freq * offset
        cos_step, sin_step = cosine(turns, whole), cosine(turns - quarter, whole)
        at = start * count_z
        for k in range(parts_x):
            cos_k = jnp.broadcast_to(cos_step[:, k : k + 1], cos.shape)
            sin_k = jnp.broadcast_to(sin_step[:, k : k + 1], cos.shape)
            columns = line_ref.at[:, k * LANES : (k + 1) * LANES]
            store_halves(columns, at, cos * cos_k - sin * sin_k)
            store_halves(columns, at + modes, -sin * cos_k - cos * sin_k)

    rows_y = column_ref.shape[0] // 4 // block
    length_y = rows_y * parts_y
    per = tile // block
    ky = col // block % local_y
    shift = col // (LANES // 2) * (length_y // 4)
    same = row % block == col % block
    low = col < LANES // 2
    inner = row // block + me_y * rows_y
    for gy in range(parts_y):
        freq = pick(my_ref, ky, range(gy * local_y, (gy + 1) * local_y))
        columns = column_ref.at[:, gy * LANES : (gy + 1) * LANES]
        for start in range(0, rows_y, per):
            value = jnp.where(same, cosine(freq * (inner + start) + shift, length_y), 0.0)
            store_halves(columns, start * block, value)
            turned = pltpu.roll(value, LANES // 2, 1)
            store_halves(columns, (rows_y + start) * block, jnp.where(low, -turned, turned))

    row, col = grid_of(2 * rows_y, cback_ref.shape[1])
    places = [
        (me_y + parts_y - step) % parts_y * local_y + k for step in range(parts_y) for k in range(local_y)
    ]
    freq = pick(my_ref, col // (2 * local_y) * local_y + col % local_y, places)
    shift = (col // local_y % 2 - row // rows_y) * (length_y // 4)
    store_halves(cback_ref, 0, cosine(freq * (row % rows_y + me_y * rows_y) + shift, length_y))

    row, col = grid_of(tile, lback_ref.shape[1])
    modes = local_x * count_z
    kx = col // (2 * modes) * local_x + col // count_z % local_x
    places = [(me_x ^ step) * local_x + k for step in steps_of(parts_x) for k in range(local_x)]
    freq = pick(mx_ref, kx, places) * size_z
    base = pick(mz_ref, col % count_z, range(count_z)) * (row % size_z) * length_x
    base = base + col // modes % 2 * (whole // 4)
    inner = row // size_z + me_x * rows_x
    per = tile // size_z
    for start in range(0, rows_x, per):
        store_halves(lback_ref, start * size_z, cosine(freq * (inner + start) + base, whole))

    conv = conv_ref[...].astype(F32)
    none = jnp.zeros_like(conv)
    for ref, value in ((pair_ref, conv), (turn_ref, conv.T)):
        ref[:chans] = jnp.concatenate([value, none], axis=1).astype(BF)
        ref[chans:] = jnp.concatenate([none, value], axis=1).astype(BF)


def dot(a, b, dims=((1,), (0,))):
    return lax.dot_general(a, b, (dims, ((), ())), preferred_element_type=F32)


def pairs_of(ref):
    size_x, size_y, size_z, chans = ref.shape
    out = []
    for y in range(size_y // 2):
        low = ref[:, y, :, :].astype(F32).reshape(size_x * size_z, chans)
        high = ref[:, y + size_y // 2, :, :].astype(F32).reshape(size_x * size_z, chans)
        out.append(jnp.concatenate([low, high], axis=1))
    return out


def block_transpose(arrays, block):
    count = len(arrays)
    arrays = list(arrays)
    lanes = arrays[0].shape[1]
    index = lax.broadcasted_iota(jnp.int32, arrays[0].shape, 1) // block % count
    step = 1
    while step < count:
        upper = (index & step) != 0
        for p in range(count):
            if p & step:
                continue
            a, b = arrays[p], arrays[p | step]
            arrays[p] = jnp.where(upper, pltpu.roll(b, step * block, 1), a)
            arrays[p | step] = jnp.where(upper, b, pltpu.roll(a, lanes - step * block, 1))
        step *= 2
    return arrays


def split_rows(value):
    high = value.astype(BF)
    return jnp.concatenate([high, (value - high.astype(F32)).astype(BF)], axis=0)


def normal_cdf(values):
    return 0.5 * (1.0 + lax.erf(values * (1.0 / math.sqrt(2.0))))


def normal_pdf(values):
    return jnp.exp(-0.5 * values * values) * (1.0 / math.sqrt(2.0 * math.pi))


def store_steps(chunk_ref, send_refs):
    me = lax.axis_index("gx")
    for t, ref in enumerate(send_refs):
        for r in range(2):
            ref[r] = chunk_ref[me ^ (2 * t + r)]


def spread_kernel(field_ref, *refs):
    send_refs, pairs_ref, chunk_ref = refs[:-2], refs[-2], refs[-1]
    pairs = pairs_of(field_ref)
    for p, pair in enumerate(pairs):
        pairs_ref[p] = pair.astype(BF)
    for b, chunk in enumerate(block_transpose(pairs, field_ref.shape[3] // len(pairs))):
        chunk_ref[b] = chunk.astype(BF)
    store_steps(chunk_ref, send_refs)


def ready_kernel(cot_ref, field_ref, conv_ref, pairs_ref, mapped_ref, turned_ref):
    for p, pair in enumerate(pairs_of(cot_ref)):
        pairs_ref[p] = pair.astype(BF)
        field = field_ref[p]
        mapped_ref[p] = dot(field, conv_ref[...])
        turned_ref[p] = field.astype(F32).T.astype(BF)


def joined(value):
    chans = value.shape[1] // 2
    return value[:, :chans].astype(F32) + value[:, chans:].astype(F32)


def parted(value):
    high = value.astype(BF).astype(F32)
    both = jnp.concatenate([high, value - high], axis=1)
    rest = jnp.zeros((EXTRA - both.shape[0], both.shape[1]), F32)
    return jnp.concatenate([both, rest], axis=0).astype(BF)


def transform_kernel(scale, parts_x, parts_y, line_ref, column_ref, *refs):
    recv_refs, send_ref, extra = refs[:parts_x], refs[parts_x], refs[parts_x + 1 :]
    rows = line_ref.shape[1] // parts_x
    own = [ref.at[k // (parts_x // 2)] for k, ref in enumerate(recv_refs)]
    if extra:
        total = joined(own[0][rows:, :])
        for ref in own[1:]:
            total = total + joined(ref[rows:, :])
        extra[0][...] = parted(total[: LANES // 2 // parts_x])
    data = jnp.concatenate([ref[:rows, :] for ref in own], axis=0)
    lines = dot(line_ref[...], data)
    half = lines.shape[0] // 2
    lines = lines[:half] + lines[half:]
    count = half // 2
    both = jnp.concatenate([lines[:count], lines[count:]], axis=1)
    depth = both.shape[1]
    high = both.astype(BF)
    low = (both - high.astype(F32)).astype(BF)
    modes = dot(split_rows(both), column_ref[:depth, :])
    modes = modes[:count] + modes[count:] + dot(high, column_ref[depth:, :])
    modes = modes * scale
    tall = count // parts_x
    for gx in range(parts_x):
        for gy in range(parts_y):
            send_ref[gx * parts_y + gy] = modes[
                gx * tall : (gx + 1) * tall, gy * LANES : (gy + 1) * LANES
            ].astype(BF)


def sum_parts(recv_ref, parts_y):
    parts = recv_ref.shape[0] // parts_y
    out = []
    for b in range(parts):
        total = recv_ref[b * parts_y].astype(F32)
        for gy in range(1, parts_y):
            total = total + recv_ref[b * parts_y + gy].astype(F32)
        out.append(total)
    return out


def lay_modes(scratch, send_ref, count_y, rows):
    chans = 64
    for m in range(0, rows, 2):
        parts = []
        for part in range(2):
            first = scratch[pl.ds(part * rows + m, count_y, stride=2 * rows), :chans]
            second = scratch[pl.ds(part * rows + m + 1, count_y, stride=2 * rows), :chans]
            parts.append(jnp.concatenate([first, second], axis=1))
        send_ref[:, m * chans : (m + 2) * chans] = jnp.concatenate(parts, axis=0).astype(send_ref.dtype)


def mix_kernel(forward, parts_y, recv_ref, weight_ref, *refs):
    send_ref, spec_ref, scratch = refs[-3:]
    if len(refs) == 4:
        send_ref[:, WIDE:] = refs[0][...]
    size_x, size_y, size_z, _, chans, _ = weight_ref.shape
    rows = size_x * size_z
    spectra = block_transpose(sum_parts(recv_ref, parts_y), chans // size_y)
    for ky in range(size_y):
        spec = spectra[ky]
        spec_ref[ky] = spec
        turned = pltpu.roll(spec, chans, 1)
        if forward:
            both = jnp.concatenate([spec, turned], axis=0)[:, :chans].T
            high = both.astype(BF)
            both = jnp.concatenate([high, (both - high.astype(F32)).astype(BF)], axis=1)
        else:
            first = lax.broadcasted_iota(jnp.int32, spec.shape, 1) < chans
            both = split_rows(jnp.concatenate([spec, jnp.where(first, turned, -turned)], axis=0))
        if forward:
            wide = [weight_ref[m // size_z, ky, m % size_z].reshape(2 * chans, chans) for m in range(rows)]
            wide = [jnp.concatenate(wide[m : m + 2], axis=1) for m in range(0, rows, 2)]
            mode = lax.broadcasted_iota(jnp.int32, both.shape, 1) % rows
            own = [jnp.where(mode == m, both, jnp.zeros_like(both)) for m in range(rows)]
            total = dot(jnp.concatenate(wide, axis=1), jnp.concatenate(own, axis=0))
            total = total.T
        else:
            stack = jnp.concatenate(
                [weight_ref[kx, ky].reshape(size_z * 2 * chans, chans) for kx in range(size_x)], axis=0
            )
            mode = lax.broadcasted_iota(jnp.int32, both.shape, 0) % rows
            own = [jnp.where(mode == m, both, jnp.zeros_like(both)) for m in range(rows)]
            total = dot(jnp.concatenate(own, axis=1), stack)
        total = total[: 2 * rows] + total[2 * rows :]
        if forward:
            real, imag = total[:rows], total[rows:]
            mixed = jnp.concatenate(
                [
                    real[:, :chans] - imag[:, chans:],
                    imag[:, :chans] + real[:, chans:],
                ],
                axis=0,
            )
        else:
            mixed = total
        scratch[ky * 2 * rows : (ky + 1) * 2 * rows, :chans] = mixed
    lay_modes(scratch, send_ref, size_y, rows)


def column_kernel(table_ref, *refs):
    steps = len(refs) - 2
    send_ref, scratch = refs[steps], refs[steps + 1]
    chans = 64
    if refs[0].shape[1] > WIDE:
        total = joined(refs[0][:, WIDE:])
        for s in range(1, steps):
            total = total + joined(refs[s][:, WIDE:])
        send_ref[:EXTRA, WIDE:] = parted(total[: EXTRA // 2])
        send_ref[EXTRA:, WIDE:] = jnp.zeros((send_ref.shape[0] - EXTRA, LANES), BF)
    data = jnp.concatenate([refs[s][:, :WIDE] for s in range(steps)], axis=0)
    lines = dot(table_ref[...], data)
    half = lines.shape[0] // 2
    lines = lines[:half] + lines[half:]
    size_y = half // 2
    count = WIDE // chans
    for m in range(0, count, 2):
        pair = lines[:, m * chans : (m + 2) * chans]
        scratch[m * half : (m + 1) * half, :] = pair
        scratch[(m + 1) * half : (m + 2) * half, :] = pltpu.roll(pair, chans, 1)
    for part in range(2):
        for y in range(size_y // 2):
            first = scratch[pl.ds(part * size_y + y, count, stride=half), :chans]
            second = scratch[pl.ds(part * size_y + y + size_y // 2, count, stride=half), :chans]
            send_ref[part * count : (part + 1) * count, y * 2 * chans : (y + 1) * 2 * chans] = (
                jnp.concatenate([first, second], axis=1).astype(BF)
            )


def cells_of(table_ref, recv_refs, scale):
    data = jnp.concatenate([ref[:, :WIDE] for ref in recv_refs], axis=0)
    cells = dot(table_ref[...], data)
    half = cells.shape[0] // 2
    return (cells[:half] + cells[half:]) * scale


def store_pair(out_ref, p, value):
    size_x, size_y, size_z, chans = out_ref.shape
    out_ref[:, p, :, :] = value[:, :chans].reshape(size_x, size_z, chans).astype(out_ref.dtype)
    out_ref[:, p + size_y // 2, :, :] = (
        value[:, chans:].reshape(size_x, size_z, chans).astype(out_ref.dtype)
    )


def point_kernel(scale, table_ref, *refs):
    recv_refs, refs = refs[: 2 * SIDES], refs[2 * SIDES :]
    conv_ref, field_ref, cot_ref, act_ref, slope_ref = refs[:5]
    send_refs, chunk_ref = refs[5:-1], refs[-1]
    cells = cells_of(table_ref, recv_refs, scale)
    count = field_ref.shape[0]
    slopes = []
    grad = jnp.zeros((LANES, LANES), F32)
    for p in range(count):
        field = field_ref[p]
        pre = cells[:, p * LANES : (p + 1) * LANES] + conv_ref[p]
        cdf = normal_cdf(pre)
        store_pair(act_ref, p, pre * cdf)
        slope = cot_ref[p].astype(F32) * (cdf + pre * normal_pdf(pre))
        narrow = slope.astype(BF)
        slope_ref[p] = narrow
        slopes.append(narrow.astype(F32))
        grad = grad + dot(field, narrow)
    rows = slopes[0].shape[0]
    chans = LANES // 2
    grad = grad[:chans, :chans] + grad[chans:, chans:]
    block = chans // count
    for b, chunk in enumerate(block_transpose(slopes, block)):
        chunk_ref[b, :rows, :] = chunk.astype(BF)
        chunk_ref[b, rows:, :] = parted(grad[b * block : (b + 1) * block])
    store_steps(chunk_ref, send_refs)


def last_kernel(scale, table_ref, *refs):
    conv_ref, slope_ref, out_ref, grad_ref = refs[-4:]
    recv_refs = refs[:-4]
    block = grad_ref.shape[0] // len(recv_refs)
    me = lax.axis_index("gx")
    for step, ref in zip(steps_of(len(recv_refs)), recv_refs):
        total = joined(ref[:EXTRA, WIDE:])
        grad_ref[pl.ds(pl.multiple_of((me ^ step) * block, block), block), :] = total[:block] * scale
    cells = cells_of(table_ref, recv_refs, scale)
    for p in range(slope_ref.shape[0]):
        store_pair(out_ref, p, cells[:, p * LANES : (p + 1) * LANES] + dot(slope_ref[p], conv_ref[...]))


def outer_kernel(spec_ref, back_ref, out_ref, held_ref, sems):
    size_x, size_y, size_z, _, chans, _ = held_ref.shape
    rows = size_x * size_z
    first = lax.broadcasted_iota(jnp.int32, back_ref.shape[1:], 1) < chans
    mode = lax.broadcasted_iota(jnp.int32, (6 * rows, chans), 0) % rows
    copies = []
    for ky in range(size_y):
        back, spec = back_ref[ky], spec_ref[ky]
        turned = pltpu.roll(back, chans, 1)
        left = jnp.concatenate([back, jnp.where(first, turned, -turned)], axis=0).T
        right = jnp.concatenate([spec, pltpu.roll(spec, chans, 1)], axis=0)[:, :chans]
        left_high, right_high = left.astype(BF), right.astype(BF)
        left_low = (left - left_high.astype(F32)).astype(BF)
        right_low = (right - right_high.astype(F32)).astype(BF)
        lefts = jnp.concatenate([left_high, left_high, left_low], axis=1)
        rights = jnp.concatenate([right_high, right_low, right_high], axis=0)
        for m in range(rows):
            own = jnp.where(mode == m, rights, jnp.zeros_like(rights))
            held_ref[m // size_z, ky, m % size_z] = dot(lefts, own).reshape(2, chans, chans)
        copy = pltpu.make_async_copy(held_ref.at[:, ky], out_ref.at[:, ky], sems.at[ky])
        copy.start()
        copies.append(copy)
    for copy in copies:
        copy.wait()


def call(kernel, outs, *args, scratch=()):
    params = pltpu.CompilerParams(vmem_limit_bytes=16 * 2**20)
    return pl.pallas_call(kernel, out_shape=outs, scratch_shapes=list(scratch), compiler_params=params)(*args)


def bind(kernel, *static):
    def bound(*refs):
        return kernel(*static, *refs)

    return bound


def sds(shape, dtype):
    return jax.ShapeDtypeStruct(shape, dtype)


def fast(features, cotangent, spectral_weight, conv_weight, modes_x, modes_y, modes_z):
    rows_x, rows_y, size_z, chans = features.shape
    local_x, local_y, count_z = spectral_weight.shape[:3]
    parts_x, parts_y = lax.axis_size("gx"), lax.axis_size("gy")
    length_x, length_y = rows_x * parts_x, rows_y * parts_y
    block = chans // parts_x
    cells = rows_x * size_z
    modes = local_x * count_z
    half_y = rows_y // 2
    first = 1.0 / math.sqrt(length_x * length_y * size_z)
    second = 1.0 / math.sqrt(modes_x.shape[0] * modes_y.shape[0] * count_z)

    *send, field = call(
        spread_kernel,
        [sds((2, cells, LANES), BF)] * SIDES + [sds((half_y, cells, LANES), BF)],
        features,
        scratch=[pltpu.VMEM((parts_x, cells, LANES), BF)],
    )
    outside = pl.BlockSpec(memory_space=pltpu.HBM)
    inside = pl.BlockSpec(memory_space=pltpu.VMEM)
    line_table, column_table, column_back, line_back, conv_pair, conv_turn = pl.pallas_call(
        bind(table_kernel, size_z),
        in_specs=[outside] * 5,
        out_shape=(
            sds((4 * modes_x.shape[0] * count_z, length_x * size_z), BF),
            sds((4 * LANES, 4 * LANES), BF),
            sds((4 * rows_y, 2 * modes_y.shape[0]), BF),
            sds((2 * cells, 2 * modes_x.shape[0] * count_z), BF),
            sds((LANES, LANES), BF),
            sds((LANES, LANES), BF),
        ),
        scratch_shapes=[
            pltpu.SMEM(modes_x.shape, jnp.int32),
            pltpu.SMEM(modes_y.shape, jnp.int32),
            pltpu.SMEM(modes_z.shape, jnp.int32),
            pltpu.VMEM(conv_weight.shape, BF),
            pltpu.SemaphoreType.DMA((4,)),
        ],
        compiler_params=pltpu.CompilerParams(vmem_limit_bytes=16 * 2**20),
    )(*(pltpu.with_memory_space_constraint(x, pltpu.HBM) for x in (modes_x, modes_y, modes_z, conv_weight, spectral_weight)))

    def cross(pieces, beside=None):
        pieces = pieces[:1] + [
            lax.ppermute(piece, "gx", [(i, i ^ 2 * t) for i in range(parts_x)])
            for t, piece in enumerate(pieces)
            if t
        ]
        if beside is not None:
            pieces[-1], beside = lax.optimization_barrier((pieces[-1], beside))
        swap = [(i, i ^ 1) for i in range(parts_x)]
        pieces = pieces + [lax.ppermute(piece, "gx", swap) for piece in pieces]
        return pieces, beside

    def to_modes(send, factor, extra, tables):
        outs = [sds((parts_x * parts_y, modes, LANES), BF)]
        if extra:
            outs.append(sds((EXTRA, LANES), BF))
        kernel = bind(transform_kernel, factor, parts_x, parts_y)
        pieces, ready = cross(send, None if extra else tables)
        tables = tables if ready is None else ready
        send, *rest = call(kernel, outs, *tables, *pieces)
        return lax.all_to_all(send, ("gx", "gy"), 0, 0, tiled=True), rest, tables

    def mix(recv, forward, rest):
        return call(
            bind(mix_kernel, forward, parts_y),
            (
                sds((2 * local_y, WIDE + len(rest) * LANES), BF),
                sds((local_y, modes, LANES), F32),
            ),
            recv,
            spectral_weight,
            *rest,
            scratch=[pltpu.VMEM((local_y * 2 * modes, LANES), F32)],
        )

    def to_lines(send, beside=None):
        pieces = [send]
        for step in range(1, parts_y):
            ring = [(i, (i + step) % parts_y) for i in range(parts_y)]
            pieces.append(lax.ppermute(send, "gy", ring))
        if beside is not None:
            pieces[-1], beside = lax.optimization_barrier((pieces[-1], beside))
        lines = call(
            column_kernel,
            sds((2 * modes, send.shape[1]), BF),
            column_back,
            *pieces,
            scratch=[pltpu.VMEM((modes * 2 * rows_y, LANES), F32)],
        )
        return cross([lines] * SIDES)[0], beside


    recv, _, tables = to_modes(send, first, False, (line_table, column_table))
    send, spec = mix(recv, True, [])
    pair_shape = (half_y, cells, LANES)
    ready = call(
        ready_kernel,
        (sds(pair_shape, BF), sds(pair_shape, F32), sds((half_y, LANES, cells), BF)),
        cotangent,
        field,
        conv_pair,
    )
    pieces, (cot, mapped, turned) = to_lines(send, ready)
    activation, slope, *send = call(
        bind(point_kernel, second),
        (
            sds(features.shape, BF),
            sds((half_y, cells, LANES), BF),
        )
        + (sds((2, cells + EXTRA, LANES), BF),) * SIDES,
        line_back,
        *pieces,
        mapped,
        turned,
        cot,
        scratch=[pltpu.VMEM((parts_x, cells + EXTRA, LANES), BF)],
    )
    recv, rest, _ = to_modes(send, second, True, tables)
    send, back = mix(recv, False, rest)
    grad_spectral = pl.pallas_call(
        outer_kernel,
        in_specs=[inside] * 2,
        out_specs=outside,
        out_shape=sds(spectral_weight.shape, F32),
        scratch_shapes=[pltpu.VMEM(spectral_weight.shape, F32), pltpu.SemaphoreType.DMA((local_y,))],
        compiler_params=pltpu.CompilerParams(vmem_limit_bytes=16 * 2**20),
    )(spec, back)
    pieces, grad_spectral = to_lines(send, grad_spectral)
    grad_features, grad_conv = call(
        bind(last_kernel, first),
        (sds(features.shape, BF), sds((chans, chans), F32)),
        line_back,
        *pieces,
        conv_turn,
        slope,
    )
    return activation, grad_features, grad_spectral, grad_conv


def phase_tables(freqs, places, length):
    product = freqs[:, None] * places[None, :] % length
    angles = product.astype(jnp.float32) * (2.0 * math.pi / length)
    return (jnp.cos(angles), jnp.sin(angles))


def plane_modes(values, factor, modes_z):
    size_x, size_y, size_z, chans = values.shape
    cos_z, sin_z = phase_tables(modes_z, jnp.arange(size_z, dtype=jnp.int32), size_z)
    wide = values.astype(jnp.float32)
    plane_real = (factor * jnp.einsum("xyzc,kz->xykc", wide, cos_z, precision=HIGH)).reshape(
        size_x, size_y, -1
    )
    plane_imag = (-factor * jnp.einsum("xyzc,kz->xykc", wide, sin_z, precision=HIGH)).reshape(
        size_x, size_y, -1
    )
    return (plane_real, plane_imag)


def line_modes(plane_real, plane_imag, freqs, places, length):
    cos_x, sin_x = phase_tables(freqs, places, length)
    line_real = jnp.einsum("kx,xyq->kyq", cos_x, plane_real, precision=HIGH) + jnp.einsum(
        "kx,xyq->kyq", sin_x, plane_imag, precision=HIGH
    )
    line_imag = jnp.einsum("kx,xyq->kyq", cos_x, plane_imag, precision=HIGH) - jnp.einsum(
        "kx,xyq->kyq", sin_x, plane_real, precision=HIGH
    )
    return jnp.stack([line_real, line_imag], axis=1)


def to_modes(values, factor, modes_x, modes_y, modes_z):
    rows_x, rows_y = (values.shape[0], values.shape[1])
    parts_x = lax.axis_size("gx")
    parts_y = lax.axis_size("gy")
    length_x = rows_x * parts_x
    length_y = rows_y * parts_y
    pencil = lax.all_to_all(values, "gx", split_axis=1, concat_axis=0, tiled=True)
    plane_real, plane_imag = plane_modes(pencil, factor, modes_z)
    whole = line_modes(
        plane_real, plane_imag, modes_x, jnp.arange(length_x, dtype=jnp.int32), length_x
    )
    spectrum = lax.all_to_all(whole, "gx", split_axis=0, concat_axis=2, tiled=True)
    places_y = lax.axis_index("gy") * rows_y + jnp.arange(rows_y, dtype=jnp.int32)
    cos_y, sin_y = phase_tables(modes_y, places_y, length_y)
    mode_real = jnp.einsum("ly,kyq->lkq", cos_y, spectrum[:, 0], precision=HIGH) + jnp.einsum(
        "ly,kyq->lkq", sin_y, spectrum[:, 1], precision=HIGH
    )
    mode_imag = jnp.einsum("ly,kyq->lkq", cos_y, spectrum[:, 1], precision=HIGH) - jnp.einsum(
        "ly,kyq->lkq", sin_y, spectrum[:, 0], precision=HIGH
    )
    return lax.psum_scatter(
        jnp.stack([mode_real, mode_imag], axis=2), "gy", scatter_dimension=0, tiled=True
    )


def to_cells(spectrum, factor, rows_x, rows_y, size_z, modes_x, modes_y, modes_z):
    length_x = rows_x * lax.axis_size("gx")
    length_y = rows_y * lax.axis_size("gy")
    places_y = lax.axis_index("gy") * rows_y + jnp.arange(rows_y, dtype=jnp.int32)
    places_x = lax.axis_index("gx") * rows_x + jnp.arange(rows_x, dtype=jnp.int32)
    piece = lax.all_gather(spectrum, "gy", axis=0, tiled=True)
    freqs = modes_y
    cos_y, sin_y = phase_tables(freqs, places_y, length_y)
    line_real = jnp.einsum("ly,lkq->kyq", cos_y, piece[:, :, 0], precision=HIGH) - jnp.einsum(
        "ly,lkq->kyq", sin_y, piece[:, :, 1], precision=HIGH
    )
    line_imag = jnp.einsum("ly,lkq->kyq", cos_y, piece[:, :, 1], precision=HIGH) + jnp.einsum(
        "ly,lkq->kyq", sin_y, piece[:, :, 0], precision=HIGH
    )
    line_real, line_imag = (line_real, line_imag)
    lines = jnp.stack([line_real, line_imag], axis=1)
    piece = lax.all_gather(lines, "gx", axis=0, tiled=True)
    freqs = modes_x
    cos_x, sin_x = phase_tables(freqs, places_x, length_x)
    plane_real = jnp.einsum("kx,kyq->xyq", cos_x, piece[:, 0], precision=HIGH) - jnp.einsum(
        "kx,kyq->xyq", sin_x, piece[:, 1], precision=HIGH
    )
    plane_imag = jnp.einsum("kx,kyq->xyq", cos_x, piece[:, 1], precision=HIGH) + jnp.einsum(
        "kx,kyq->xyq", sin_x, piece[:, 0], precision=HIGH
    )
    plane_real, plane_imag = (plane_real, plane_imag)
    count_z = modes_z.shape[0]
    plane_real = plane_real.reshape(rows_x, rows_y, count_z, -1)
    plane_imag = plane_imag.reshape(rows_x, rows_y, count_z, -1)
    cos_z, sin_z = phase_tables(modes_z, jnp.arange(size_z, dtype=jnp.int32), size_z)
    return factor * (
        jnp.einsum("xykc,kz->xyzc", plane_real, cos_z, precision=HIGH)
        - jnp.einsum("xykc,kz->xyzc", plane_imag, sin_z, precision=HIGH)
    )


def plain(features, cotangent, spectral_weight, conv_weight, modes_x, modes_y, modes_z):
    rows_x, rows_y, size_z, chans = features.shape
    count_x, count_y, count_z = (modes_x.shape[0], modes_y.shape[0], modes_z.shape[0])
    length_x = rows_x * lax.axis_size("gx")
    length_y = rows_y * lax.axis_size("gy")
    first = 1.0 / math.sqrt(length_x * length_y * size_z)
    second = 1.0 / math.sqrt(count_x * count_y * count_z)
    spectrum = to_modes(features, first, modes_x, modes_y, modes_z)
    local_y, local_x = (spectrum.shape[0], spectrum.shape[1])
    spec_real = spectrum[:, :, 0].reshape(local_y, local_x, count_z, chans)
    spec_imag = spectrum[:, :, 1].reshape(local_y, local_x, count_z, chans)
    weight = spectral_weight.astype(jnp.float32)
    real_w = weight[:, :, :, 0]
    imag_w = weight[:, :, :, 1]
    form = "abzoi,bazi->bazo"
    mixed_real = jnp.einsum(form, real_w, spec_real, precision=HIGH) - jnp.einsum(
        form, imag_w, spec_imag, precision=HIGH
    )
    mixed_imag = jnp.einsum(form, real_w, spec_imag, precision=HIGH) + jnp.einsum(
        form, imag_w, spec_real, precision=HIGH
    )
    mixed = jnp.stack(
        [mixed_real.reshape(local_y, local_x, -1), mixed_imag.reshape(local_y, local_x, -1)], axis=2
    )
    spectral = to_cells(mixed, second, rows_x, rows_y, size_z, modes_x, modes_y, modes_z)
    flat = features.reshape(-1, chans)
    conv = jnp.dot(flat, conv_weight, preferred_element_type=jnp.float32).reshape(spectral.shape)
    pre = spectral + conv
    cdf = normal_cdf(pre)
    activation = (pre * cdf).astype(jnp.bfloat16)
    slope = (cotangent.astype(jnp.float32) * (cdf + pre * normal_pdf(pre))).astype(jnp.bfloat16)
    back = to_modes(slope, second, modes_x, modes_y, modes_z)
    back_real = back[:, :, 0].reshape(local_y, local_x, count_z, chans)
    back_imag = back[:, :, 1].reshape(local_y, local_x, count_z, chans)
    outer = "bazo,bazi->abzoi"
    grad_real = jnp.einsum(outer, back_real, spec_real, precision=HIGH) + jnp.einsum(
        outer, back_imag, spec_imag, precision=HIGH
    )
    grad_imag = jnp.einsum(outer, back_imag, spec_real, precision=HIGH) - jnp.einsum(
        outer, back_real, spec_imag, precision=HIGH
    )
    grad_spectral = jnp.stack([grad_real, grad_imag], axis=3)
    adjoint = "abzoi,bazo->bazi"
    modes_real = jnp.einsum(adjoint, real_w, back_real, precision=HIGH) + jnp.einsum(
        adjoint, imag_w, back_imag, precision=HIGH
    )
    modes_imag = jnp.einsum(adjoint, real_w, back_imag, precision=HIGH) - jnp.einsum(
        adjoint, imag_w, back_real, precision=HIGH
    )
    back_modes = jnp.stack(
        [modes_real.reshape(local_y, local_x, -1), modes_imag.reshape(local_y, local_x, -1)], axis=2
    )
    spectral_back = to_cells(back_modes, first, rows_x, rows_y, size_z, modes_x, modes_y, modes_z)
    slope_flat = slope.reshape(-1, chans)
    conv_back = jnp.dot(slope_flat, conv_weight.T, preferred_element_type=jnp.float32).reshape(
        spectral.shape
    )
    grad_features = (spectral_back + conv_back).astype(jnp.bfloat16)
    local_conv = jnp.dot(flat.T, slope_flat, preferred_element_type=jnp.float32)
    grad_conv = first * lax.psum(local_conv, ("gx", "gy"))
    return (activation, grad_features, grad_spectral, grad_conv)


def fits(features, spectral_weight):
    rows_x, rows_y, size_z, chans = features.shape
    local_x, local_y, count_z = spectral_weight.shape[:3]
    parts_x, parts_y = lax.axis_size("gx"), lax.axis_size("gy")
    return (
        chans == 64
        and parts_x == 8
        and rows_y == 2 * parts_x
        and local_y == parts_x
        and rows_x * size_z == LANES
        and local_x * count_z == 2 * parts_x
        and parts_y == 4
        and all(n & (n - 1) == 0 for n in (rows_x * parts_x, rows_y * parts_y, size_z))
    )


def shards(features, cotangent, spectral_weight, *rest):
    run = fast if fits(features, spectral_weight) else plain
    return run(features, cotangent, spectral_weight, *rest)


def solution(mesh):
    placed = (
        P("gx", "gy", None, None),
        P("gx", "gy", None, None),
        P("gx", "gy", None, None, None, None),
        P(),
        P(),
        P(),
        P(),
    )
    return jax.shard_map(
        shards,
        mesh=mesh,
        in_specs=placed,
        out_specs=(
            P("gx", "gy", None, None),
            P("gx", "gy", None, None),
            P("gx", "gy", None, None, None, None),
            P(),
        ),
        check_vma=False,
    )
```

```python
import math

import jax
import jax.numpy as jnp
from jax import lax
from jax.experimental import pallas as pl
from jax.experimental.pallas import tpu as pltpu
from jax.sharding import PartitionSpec as P

HIGH = lax.Precision.HIGHEST
BF = jnp.bfloat16
F32 = jnp.float32
LANES = 128
EXTRA = 16
WIDE = 1024
SIDES = 4


def steps_of(parts):
    return list(range(0, parts, 2)) + list(range(1, parts, 2))


def cosine(turns, length):
    half = length // 2
    place = ((turns + length // 4) & (length - 1)) - half
    place = jnp.minimum(jnp.maximum(place, -half - place), half - place)
    angle = place.astype(F32) * (-2.0 * math.pi / length)
    square = angle * angle
    series = 1.0 / 362880.0 - square * (1.0 / 39916800.0)
    series = square * series - 1.0 / 5040.0
    series = square * series + 1.0 / 120.0
    series = square * series - 1.0 / 6.0
    return angle + angle * (square * series)


def pick(ref, index, places):
    out = jnp.zeros(index.shape, jnp.int32)
    for k, place in enumerate(places):
        out = jnp.where(index == k, ref[place], out)
    return out


def store_halves(ref, row, value):
    high = value.astype(BF)
    tall = ref.shape[0] // 2
    ref[row : row + value.shape[0]] = high
    ref[tall + row : tall + row + value.shape[0]] = (value - high.astype(F32)).astype(BF)


def grid_of(rows, cols):
    return (
        lax.broadcasted_iota(jnp.int32, (rows, cols), 0),
        lax.broadcasted_iota(jnp.int32, (rows, cols), 1),
    )


def table_kernel(size_z, *refs):
    sources, outs, places, sems = refs[:4], refs[5:11], refs[11:15], refs[15]
    line_ref, column_ref, cback_ref, lback_ref, pair_ref, turn_ref = outs
    copies = [
        pltpu.make_async_copy(source, place, sems.at[k])
        for k, (source, place) in enumerate(zip(sources, places))
    ]
    for copy in copies:
        copy.start()
    for copy in copies:
        copy.wait()
    mx_ref, my_ref, mz_ref, conv_ref = places
    parts_x, parts_y = lax.axis_size("gx"), lax.axis_size("gy")
    me_x, me_y = lax.axis_index("gx"), lax.axis_index("gy")
    count_x, count_y, count_z = mx_ref.shape[0], my_ref.shape[0], mz_ref.shape[0]
    local_x, local_y = count_x // parts_x, count_y // parts_y
    chans = conv_ref.shape[0]
    block = chans // parts_x
    length_x = line_ref.shape[1] // size_z
    whole = line_ref.shape[1]
    tile = 16

    rows_x = length_x // parts_x
    row, col = grid_of(tile, LANES)
    per = tile // count_z
    quarter = whole // 4
    base = pick(mz_ref, row % count_z, range(count_z)) * (col % size_z) * length_x
    inner = row // count_z
    offset = jnp.zeros(col.shape, jnp.int32)
    for k, step in enumerate(steps_of(parts_x)):
        offset = jnp.where(col == k, (me_x ^ step) * (rows_x * size_z), offset)
    modes = count_x * count_z
    for start in range(0, count_x, per):
        freq = pick(mx_ref, inner, range(start, start + per))
        turns = freq * (col // size_z * size_z) + base
        cos, sin = cosine(turns, whole), cosine(turns - quarter, whole)
        turns = freq * offset
        cos_step, sin_step = cosine(turns, whole), cosine(turns - quarter, whole)
        at = start * count_z
        for k in range(parts_x):
            cos_k = jnp.broadcast_to(cos_step[:, k : k + 1], cos.shape)
            sin_k = jnp.broadcast_to(sin_step[:, k : k + 1], cos.shape)
            columns = line_ref.at[:, k * LANES : (k + 1) * LANES]
            store_halves(columns, at, cos * cos_k - sin * sin_k)
            store_halves(columns, at + modes, -sin * cos_k - cos * sin_k)

    rows_y = column_ref.shape[0] // 4 // block
    length_y = rows_y * parts_y
    per = tile // block
    ky = col // block % local_y
    shift = col // (LANES // 2) * (length_y // 4)
    same = row % block == col % block
    low = col < LANES // 2
    inner = row // block + me_y * rows_y
    for gy in range(parts_y):
        freq = pick(my_ref, ky, range(gy * local_y, (gy + 1) * local_y))
        columns = column_ref.at[:, gy * LANES : (gy + 1) * LANES]
        for start in range(0, rows_y, per):
            value = jnp.where(same, cosine(freq * (inner + start) + shift, length_y), 0.0)
            store_halves(columns, start * block, value)
            turned = pltpu.roll(value, LANES // 2, 1)
            store_halves(columns, (rows_y + start) * block, jnp.where(low, -turned, turned))

    row, col = grid_of(2 * rows_y, cback_ref.shape[1])
    places = [
        (me_y + parts_y - step) % parts_y * local_y + k for step in range(parts_y) for k in range(local_y)
    ]
    freq = pick(my_ref, col // (2 * local_y) * local_y + col % local_y, places)
    shift = (col // local_y % 2 - row // rows_y) * (length_y // 4)
    store_halves(cback_ref, 0, cosine(freq * (row % rows_y + me_y * rows_y) + shift, length_y))

    row, col = grid_of(tile, lback_ref.shape[1])
    modes = local_x * count_z
    kx = col // (2 * modes) * local_x + col // count_z % local_x
    places = [(me_x ^ step) * local_x + k for step in steps_of(parts_x) for k in range(local_x)]
    freq = pick(mx_ref, kx, places) * size_z
    base = pick(mz_ref, col % count_z, range(count_z)) * (row % size_z) * length_x
    base = base + col // modes % 2 * (whole // 4)
    inner = row // size_z + me_x * rows_x
    per = tile // size_z
    for start in range(0, rows_x, per):
        store_halves(lback_ref, start * size_z, cosine(freq * (inner + start) + base, whole))

    conv = conv_ref[...].astype(F32)
    none = jnp.zeros_like(conv)
    for ref, value in ((pair_ref, conv), (turn_ref, conv.T)):
        ref[:chans] = jnp.concatenate([value, none], axis=1).astype(BF)
        ref[chans:] = jnp.concatenate([none, value], axis=1).astype(BF)


def dot(a, b, dims=((1,), (0,))):
    return lax.dot_general(a, b, (dims, ((), ())), preferred_element_type=F32)


def pairs_of(ref):
    size_x, size_y, size_z, chans = ref.shape
    out = []
    for y in range(size_y // 2):
        low = ref[:, y, :, :].astype(F32).reshape(size_x * size_z, chans)
        high = ref[:, y + size_y // 2, :, :].astype(F32).reshape(size_x * size_z, chans)
        out.append(jnp.concatenate([low, high], axis=1))
    return out


def block_transpose(arrays, block):
    count = len(arrays)
    arrays = list(arrays)
    lanes = arrays[0].shape[1]
    index = lax.broadcasted_iota(jnp.int32, arrays[0].shape, 1) // block % count
    step = 1
    while step < count:
        upper = (index & step) != 0
        for p in range(count):
            if p & step:
                continue
            a, b = arrays[p], arrays[p | step]
            arrays[p] = jnp.where(upper, pltpu.roll(b, step * block, 1), a)
            arrays[p | step] = jnp.where(upper, b, pltpu.roll(a, lanes - step * block, 1))
        step *= 2
    return arrays


def split_rows(value):
    high = value.astype(BF)
    return jnp.concatenate([high, (value - high.astype(F32)).astype(BF)], axis=0)


def normal_cdf(values):
    return 0.5 * (1.0 + lax.erf(values * (1.0 / math.sqrt(2.0))))


def normal_pdf(values):
    return jnp.exp(-0.5 * values * values) * (1.0 / math.sqrt(2.0 * math.pi))


def store_steps(chunk_ref, send_refs):
    me = lax.axis_index("gx")
    for t, ref in enumerate(send_refs):
        for r in range(2):
            ref[r] = chunk_ref[me ^ (2 * t + r)]


def spread_kernel(field_ref, *refs):
    send_refs, pairs_ref, chunk_ref = refs[:-2], refs[-2], refs[-1]
    pairs = pairs_of(field_ref)
    for p, pair in enumerate(pairs):
        pairs_ref[p] = pair.astype(BF)
    for b, chunk in enumerate(block_transpose(pairs, field_ref.shape[3] // len(pairs))):
        chunk_ref[b] = chunk.astype(BF)
    store_steps(chunk_ref, send_refs)


def ready_kernel(cot_ref, field_ref, conv_ref, pairs_ref, mapped_ref, turned_ref):
    for p, pair in enumerate(pairs_of(cot_ref)):
        pairs_ref[p] = pair.astype(BF)
        field = field_ref[p]
        mapped_ref[p] = dot(field, conv_ref[...])
        turned_ref[p] = field.astype(F32).T.astype(BF)


def joined(value):
    chans = value.shape[1] // 2
    return value[:, :chans].astype(F32) + value[:, chans:].astype(F32)


def parted(value):
    high = value.astype(BF).astype(F32)
    both = jnp.concatenate([high, value - high], axis=1)
    rest = jnp.zeros((EXTRA - both.shape[0], both.shape[1]), F32)
    return jnp.concatenate([both, rest], axis=0).astype(BF)


def transform_kernel(scale, parts_x, parts_y, line_ref, column_ref, *refs):
    recv_refs, send_ref, extra = refs[:parts_x], refs[parts_x], refs[parts_x + 1 :]
    rows = line_ref.shape[1] // parts_x
    own = [ref.at[k // (parts_x // 2)] for k, ref in enumerate(recv_refs)]
    if extra:
        total = joined(own[0][rows:, :])
        for ref in own[1:]:
            total = total + joined(ref[rows:, :])
        extra[0][...] = parted(total[: LANES // 2 // parts_x])
    data = jnp.concatenate([ref[:rows, :] for ref in own], axis=0)
    half = line_ref.shape[0] // 2
    table = jnp.concatenate([line_ref[:half, :], line_ref[half:, :]], axis=1)
    lines = dot(table, jnp.concatenate([data, data], axis=0))
    count = half // 2
    both = jnp.concatenate([lines[:count], lines[count:]], axis=1)
    depth = both.shape[1]
    high = both.astype(BF)
    low = (both - high.astype(F32)).astype(BF)
    modes = dot(split_rows(both), column_ref[:depth, :])
    modes = modes[:count] + modes[count:] + dot(high, column_ref[depth:, :])
    modes = modes * scale
    tall = count // parts_x
    for gx in range(parts_x):
        for gy in range(parts_y):
            send_ref[gx * parts_y + gy] = modes[
                gx * tall : (gx + 1) * tall, gy * LANES : (gy + 1) * LANES
            ].astype(BF)


def sum_parts(recv_ref, parts_y):
    parts = recv_ref.shape[0] // parts_y
    out = []
    for b in range(parts):
        total = recv_ref[b * parts_y].astype(F32)
        for gy in range(1, parts_y):
            total = total + recv_ref[b * parts_y + gy].astype(F32)
        out.append(total)
    return out


def lay_modes(scratch, send_ref, count_y, rows):
    chans = 64
    for m in range(0, rows, 2):
        parts = []
        for part in range(2):
            first = scratch[pl.ds(part * rows + m, count_y, stride=2 * rows), :chans]
            second = scratch[pl.ds(part * rows + m + 1, count_y, stride=2 * rows), :chans]
            parts.append(jnp.concatenate([first, second], axis=1))
        send_ref[:, m * chans : (m + 2) * chans] = jnp.concatenate(parts, axis=0).astype(send_ref.dtype)


def mix_kernel(forward, parts_y, recv_ref, weight_ref, *refs):
    send_ref, spec_ref, scratch = refs[-3:]
    if len(refs) == 4:
        send_ref[:, WIDE:] = refs[0][...]
    size_x, size_y, size_z, _, chans, _ = weight_ref.shape
    rows = size_x * size_z
    spectra = block_transpose(sum_parts(recv_ref, parts_y), chans // size_y)
    for ky, spec in enumerate(spectra):
        spec_ref[ky] = spec
    if forward:
        group = LANES // (2 * rows)
        for start in range(0, size_y, group):
            both = []
            for spec in spectra[start : start + group]:
                both += [spec, pltpu.roll(spec, chans, 1)]
            both = jnp.concatenate(both, axis=0)[:, :chans].T
            high = both.astype(BF)
            both = jnp.concatenate([high, (both - high.astype(F32)).astype(BF)], axis=1)
            lane = lax.broadcasted_iota(jnp.int32, both.shape, 1) % LANES
            mode = lane // (2 * rows) * rows + lane % rows
            own = [jnp.where(mode == m, both, jnp.zeros_like(both)) for m in range(group * rows)]
            wide = [
                weight_ref[m // size_z, start + ky, m % size_z].reshape(2 * chans, chans)
                for ky in range(group)
                for m in range(rows)
            ]
            wide = [jnp.concatenate(wide[m : m + 2], axis=1) for m in range(0, len(wide), 2)]
            total = dot(jnp.concatenate(wide, axis=1), jnp.concatenate(own, axis=0))
            total = (total[:, :LANES] + total[:, LANES:]).T
            for ky in range(group):
                at = ky * 2 * rows
                real, imag = total[at : at + rows], total[at + rows : at + 2 * rows]
                at += start * 2 * rows
                scratch[at : at + rows, :chans] = real[:, :chans] - imag[:, chans:]
                scratch[at + rows : at + 2 * rows, :chans] = imag[:, :chans] + real[:, chans:]
    else:
        first = lax.broadcasted_iota(jnp.int32, spectra[0].shape, 1) < chans
        for ky, spec in enumerate(spectra):
            turned = pltpu.roll(spec, chans, 1)
            both = split_rows(jnp.concatenate([spec, jnp.where(first, turned, -turned)], axis=0))
            stack = jnp.concatenate(
                [weight_ref[kx, ky].reshape(size_z * 2 * chans, chans) for kx in range(size_x)], axis=0
            )
            mode = lax.broadcasted_iota(jnp.int32, both.shape, 0) % rows
            own = [jnp.where(mode == m, both, jnp.zeros_like(both)) for m in range(rows)]
            total = dot(jnp.concatenate(own, axis=1), stack)
            scratch[ky * 2 * rows : (ky + 1) * 2 * rows, :chans] = total[: 2 * rows] + total[2 * rows :]
    lay_modes(scratch, send_ref, size_y, rows)


def column_kernel(table_ref, *refs):
    steps = len(refs) - 2
    send_ref, scratch = refs[steps], refs[steps + 1]
    chans = 64
    if refs[0].shape[1] > WIDE:
        total = joined(refs[0][:, WIDE:])
        for s in range(1, steps):
            total = total + joined(refs[s][:, WIDE:])
        send_ref[:EXTRA, WIDE:] = parted(total[: EXTRA // 2])
        send_ref[EXTRA:, WIDE:] = jnp.zeros((send_ref.shape[0] - EXTRA, LANES), BF)
    data = jnp.concatenate([refs[s][:, :WIDE] for s in range(steps)], axis=0)
    lines = dot(table_ref[...], data)
    half = lines.shape[0] // 2
    lines = lines[:half] + lines[half:]
    size_y = half // 2
    count = WIDE // chans
    for m in range(0, count, 2):
        pair = lines[:, m * chans : (m + 2) * chans]
        scratch[m * half : (m + 1) * half, :] = pair
        scratch[(m + 1) * half : (m + 2) * half, :] = pltpu.roll(pair, chans, 1)
    for part in range(2):
        for y in range(size_y // 2):
            first = scratch[pl.ds(part * size_y + y, count, stride=half), :chans]
            second = scratch[pl.ds(part * size_y + y + size_y // 2, count, stride=half), :chans]
            send_ref[part * count : (part + 1) * count, y * 2 * chans : (y + 1) * 2 * chans] = (
                jnp.concatenate([first, second], axis=1).astype(BF)
            )


def cells_of(table_ref, recv_refs, scale):
    data = jnp.concatenate([ref[:, :WIDE] for ref in recv_refs], axis=0)
    cells = dot(table_ref[...], data)
    half = cells.shape[0] // 2
    return (cells[:half] + cells[half:]) * scale


def store_pair(out_ref, p, value):
    size_x, size_y, size_z, chans = out_ref.shape
    out_ref[:, p, :, :] = value[:, :chans].reshape(size_x, size_z, chans).astype(out_ref.dtype)
    out_ref[:, p + size_y // 2, :, :] = (
        value[:, chans:].reshape(size_x, size_z, chans).astype(out_ref.dtype)
    )


def point_kernel(scale, table_ref, *refs):
    recv_refs, refs = refs[: 2 * SIDES], refs[2 * SIDES :]
    conv_ref, field_ref, cot_ref, act_ref, slope_ref = refs[:5]
    send_refs, chunk_ref = refs[5:-1], refs[-1]
    cells = cells_of(table_ref, recv_refs, scale)
    count = field_ref.shape[0]
    slopes = []
    grad = jnp.zeros((LANES, LANES), F32)
    for p in range(count):
        field = field_ref[p]
        pre = cells[:, p * LANES : (p + 1) * LANES] + conv_ref[p]
        cdf = normal_cdf(pre)
        store_pair(act_ref, p, pre * cdf)
        slope = cot_ref[p].astype(F32) * (cdf + pre * normal_pdf(pre))
        narrow = slope.astype(BF)
        slope_ref[p] = narrow
        slopes.append(narrow.astype(F32))
        grad = grad + dot(field, narrow)
    rows = slopes[0].shape[0]
    chans = LANES // 2
    grad = grad[:chans, :chans] + grad[chans:, chans:]
    block = chans // count
    for b, chunk in enumerate(block_transpose(slopes, block)):
        chunk_ref[b, :rows, :] = chunk.astype(BF)
        chunk_ref[b, rows:, :] = parted(grad[b * block : (b + 1) * block])
    store_steps(chunk_ref, send_refs)


def last_kernel(scale, table_ref, *refs):
    conv_ref, slope_ref, out_ref, grad_ref = refs[-4:]
    recv_refs = refs[:-4]
    block = grad_ref.shape[0] // len(recv_refs)
    me = lax.axis_index("gx")
    for step, ref in zip(steps_of(len(recv_refs)), recv_refs):
        total = joined(ref[:EXTRA, WIDE:])
        grad_ref[pl.ds(pl.multiple_of((me ^ step) * block, block), block), :] = total[:block] * scale
    cells = cells_of(table_ref, recv_refs, scale)
    for p in range(slope_ref.shape[0]):
        store_pair(out_ref, p, cells[:, p * LANES : (p + 1) * LANES] + dot(slope_ref[p], conv_ref[...]))


def outer_kernel(spec_ref, back_ref, out_ref, held_ref, sems):
    size_x, size_y, size_z, _, chans, _ = held_ref.shape
    rows = size_x * size_z
    first = lax.broadcasted_iota(jnp.int32, back_ref.shape[1:], 1) < chans
    mode = lax.broadcasted_iota(jnp.int32, (6 * rows, chans), 0) % rows
    copies = []
    for ky in range(size_y):
        back, spec = back_ref[ky], spec_ref[ky]
        turned = pltpu.roll(back, chans, 1)
        left = jnp.concatenate([back, jnp.where(first, turned, -turned)], axis=0).T
        right = jnp.concatenate([spec, pltpu.roll(spec, chans, 1)], axis=0)[:, :chans]
        left_high, right_high = left.astype(BF), right.astype(BF)
        left_low = (left - left_high.astype(F32)).astype(BF)
        right_low = (right - right_high.astype(F32)).astype(BF)
        lefts = jnp.concatenate([left_high, left_high, left_low], axis=1)
        rights = jnp.concatenate([right_high, right_low, right_high], axis=0)
        for m in range(rows):
            own = jnp.where(mode == m, rights, jnp.zeros_like(rights))
            held_ref[m // size_z, ky, m % size_z] = dot(lefts, own).reshape(2, chans, chans)
        copy = pltpu.make_async_copy(held_ref.at[:, ky], out_ref.at[:, ky], sems.at[ky])
        copy.start()
        copies.append(copy)
    for copy in copies:
        copy.wait()


def call(kernel, outs, *args, scratch=()):
    params = pltpu.CompilerParams(vmem_limit_bytes=16 * 2**20)
    return pl.pallas_call(kernel, out_shape=outs, scratch_shapes=list(scratch), compiler_params=params)(*args)


def bind(kernel, *static):
    def bound(*refs):
        return kernel(*static, *refs)

    return bound


def sds(shape, dtype):
    return jax.ShapeDtypeStruct(shape, dtype)


def fast(features, cotangent, spectral_weight, conv_weight, modes_x, modes_y, modes_z):
    rows_x, rows_y, size_z, chans = features.shape
    local_x, local_y, count_z = spectral_weight.shape[:3]
    parts_x, parts_y = lax.axis_size("gx"), lax.axis_size("gy")
    length_x, length_y = rows_x * parts_x, rows_y * parts_y
    block = chans // parts_x
    cells = rows_x * size_z
    modes = local_x * count_z
    half_y = rows_y // 2
    first = 1.0 / math.sqrt(length_x * length_y * size_z)
    second = 1.0 / math.sqrt(modes_x.shape[0] * modes_y.shape[0] * count_z)

    *send, field = call(
        spread_kernel,
        [sds((2, cells, LANES), BF)] * SIDES + [sds((half_y, cells, LANES), BF)],
        features,
        scratch=[pltpu.VMEM((parts_x, cells, LANES), BF)],
    )
    outside = pl.BlockSpec(memory_space=pltpu.HBM)
    inside = pl.BlockSpec(memory_space=pltpu.VMEM)
    line_table, column_table, column_back, line_back, conv_pair, conv_turn = pl.pallas_call(
        bind(table_kernel, size_z),
        in_specs=[outside] * 5,
        out_shape=(
            sds((4 * modes_x.shape[0] * count_z, length_x * size_z), BF),
            sds((4 * LANES, 4 * LANES), BF),
            sds((4 * rows_y, 2 * modes_y.shape[0]), BF),
            sds((2 * cells, 2 * modes_x.shape[0] * count_z), BF),
            sds((LANES, LANES), BF),
            sds((LANES, LANES), BF),
        ),
        scratch_shapes=[
            pltpu.SMEM(modes_x.shape, jnp.int32),
            pltpu.SMEM(modes_y.shape, jnp.int32),
            pltpu.SMEM(modes_z.shape, jnp.int32),
            pltpu.VMEM(conv_weight.shape, BF),
            pltpu.SemaphoreType.DMA((4,)),
        ],
        compiler_params=pltpu.CompilerParams(vmem_limit_bytes=16 * 2**20),
    )(*(pltpu.with_memory_space_constraint(x, pltpu.HBM) for x in (modes_x, modes_y, modes_z, conv_weight, spectral_weight)))

    def cross(pieces, beside=None):
        pieces = pieces[:1] + [
            lax.ppermute(piece, "gx", [(i, i ^ 2 * t) for i in range(parts_x)])
            for t, piece in enumerate(pieces)
            if t
        ]
        if beside is not None:
            pieces[-1], beside = lax.optimization_barrier((pieces[-1], beside))
        swap = [(i, i ^ 1) for i in range(parts_x)]
        pieces = pieces + [lax.ppermute(piece, "gx", swap) for piece in pieces]
        return pieces, beside

    def to_modes(send, factor, extra, tables):
        outs = [sds((parts_x * parts_y, modes, LANES), BF)]
        if extra:
            outs.append(sds((EXTRA, LANES), BF))
        kernel = bind(transform_kernel, factor, parts_x, parts_y)
        pieces, ready = cross(send, None if extra else tables)
        tables = tables if ready is None else ready
        send, *rest = call(kernel, outs, *tables, *pieces)
        return lax.all_to_all(send, ("gx", "gy"), 0, 0, tiled=True), rest, tables

    def mix(recv, forward, rest):
        return call(
            bind(mix_kernel, forward, parts_y),
            (
                sds((2 * local_y, WIDE + len(rest) * LANES), BF),
                sds((local_y, modes, LANES), F32),
            ),
            recv,
            spectral_weight,
            *rest,
            scratch=[pltpu.VMEM((local_y * 2 * modes, LANES), F32)],
        )

    def to_lines(send, beside=None):
        pieces = [send]
        for step in range(1, parts_y):
            ring = [(i, (i + step) % parts_y) for i in range(parts_y)]
            pieces.append(lax.ppermute(send, "gy", ring))
        if beside is not None:
            pieces[-1], beside = lax.optimization_barrier((pieces[-1], beside))
        lines = call(
            column_kernel,
            sds((2 * modes, send.shape[1]), BF),
            column_back,
            *pieces,
            scratch=[pltpu.VMEM((modes * 2 * rows_y, LANES), F32)],
        )
        return cross([lines] * SIDES)[0], beside


    recv, _, tables = to_modes(send, first, False, (line_table, column_table))
    send, spec = mix(recv, True, [])
    pair_shape = (half_y, cells, LANES)
    ready = call(
        ready_kernel,
        (sds(pair_shape, BF), sds(pair_shape, F32), sds((half_y, LANES, cells), BF)),
        cotangent,
        field,
        conv_pair,
    )
    pieces, (cot, mapped, turned) = to_lines(send, ready)
    activation, slope, *send = call(
        bind(point_kernel, second),
        (
            sds(features.shape, BF),
            sds((half_y, cells, LANES), BF),
        )
        + (sds((2, cells + EXTRA, LANES), BF),) * SIDES,
        line_back,
        *pieces,
        mapped,
        turned,
        cot,
        scratch=[pltpu.VMEM((parts_x, cells + EXTRA, LANES), BF)],
    )
    recv, rest, _ = to_modes(send, second, True, tables)
    send, back = mix(recv, False, rest)
    grad_spectral = pl.pallas_call(
        outer_kernel,
        in_specs=[inside] * 2,
        out_specs=outside,
        out_shape=sds(spectral_weight.shape, F32),
        scratch_shapes=[pltpu.VMEM(spectral_weight.shape, F32), pltpu.SemaphoreType.DMA((local_y,))],
        compiler_params=pltpu.CompilerParams(vmem_limit_bytes=16 * 2**20),
    )(spec, back)
    pieces, grad_spectral = to_lines(send, grad_spectral)
    grad_features, grad_conv = call(
        bind(last_kernel, first),
        (sds(features.shape, BF), sds((chans, chans), F32)),
        line_back,
        *pieces,
        conv_turn,
        slope,
    )
    return activation, grad_features, grad_spectral, grad_conv


def phase_tables(freqs, places, length):
    product = freqs[:, None] * places[None, :] % length
    angles = product.astype(jnp.float32) * (2.0 * math.pi / length)
    return (jnp.cos(angles), jnp.sin(angles))


def plane_modes(values, factor, modes_z):
    size_x, size_y, size_z, chans = values.shape
    cos_z, sin_z = phase_tables(modes_z, jnp.arange(size_z, dtype=jnp.int32), size_z)
    wide = values.astype(jnp.float32)
    plane_real = (factor * jnp.einsum("xyzc,kz->xykc", wide, cos_z, precision=HIGH)).reshape(
        size_x, size_y, -1
    )
    plane_imag = (-factor * jnp.einsum("xyzc,kz->xykc", wide, sin_z, precision=HIGH)).reshape(
        size_x, size_y, -1
    )
    return (plane_real, plane_imag)


def line_modes(plane_real, plane_imag, freqs, places, length):
    cos_x, sin_x = phase_tables(freqs, places, length)
    line_real = jnp.einsum("kx,xyq->kyq", cos_x, plane_real, precision=HIGH) + jnp.einsum(
        "kx,xyq->kyq", sin_x, plane_imag, precision=HIGH
    )
    line_imag = jnp.einsum("kx,xyq->kyq", cos_x, plane_imag, precision=HIGH) - jnp.einsum(
        "kx,xyq->kyq", sin_x, plane_real, precision=HIGH
    )
    return jnp.stack([line_real, line_imag], axis=1)


def to_modes(values, factor, modes_x, modes_y, modes_z):
    rows_x, rows_y = (values.shape[0], values.shape[1])
    parts_x = lax.axis_size("gx")
    parts_y = lax.axis_size("gy")
    length_x = rows_x * parts_x
    length_y = rows_y * parts_y
    pencil = lax.all_to_all(values, "gx", split_axis=1, concat_axis=0, tiled=True)
    plane_real, plane_imag = plane_modes(pencil, factor, modes_z)
    whole = line_modes(
        plane_real, plane_imag, modes_x, jnp.arange(length_x, dtype=jnp.int32), length_x
    )
    spectrum = lax.all_to_all(whole, "gx", split_axis=0, concat_axis=2, tiled=True)
    places_y = lax.axis_index("gy") * rows_y + jnp.arange(rows_y, dtype=jnp.int32)
    cos_y, sin_y = phase_tables(modes_y, places_y, length_y)
    mode_real = jnp.einsum("ly,kyq->lkq", cos_y, spectrum[:, 0], precision=HIGH) + jnp.einsum(
        "ly,kyq->lkq", sin_y, spectrum[:, 1], precision=HIGH
    )
    mode_imag = jnp.einsum("ly,kyq->lkq", cos_y, spectrum[:, 1], precision=HIGH) - jnp.einsum(
        "ly,kyq->lkq", sin_y, spectrum[:, 0], precision=HIGH
    )
    return lax.psum_scatter(
        jnp.stack([mode_real, mode_imag], axis=2), "gy", scatter_dimension=0, tiled=True
    )


def to_cells(spectrum, factor, rows_x, rows_y, size_z, modes_x, modes_y, modes_z):
    length_x = rows_x * lax.axis_size("gx")
    length_y = rows_y * lax.axis_size("gy")
    places_y = lax.axis_index("gy") * rows_y + jnp.arange(rows_y, dtype=jnp.int32)
    places_x = lax.axis_index("gx") * rows_x + jnp.arange(rows_x, dtype=jnp.int32)
    piece = lax.all_gather(spectrum, "gy", axis=0, tiled=True)
    freqs = modes_y
    cos_y, sin_y = phase_tables(freqs, places_y, length_y)
    line_real = jnp.einsum("ly,lkq->kyq", cos_y, piece[:, :, 0], precision=HIGH) - jnp.einsum(
        "ly,lkq->kyq", sin_y, piece[:, :, 1], precision=HIGH
    )
    line_imag = jnp.einsum("ly,lkq->kyq", cos_y, piece[:, :, 1], precision=HIGH) + jnp.einsum(
        "ly,lkq->kyq", sin_y, piece[:, :, 0], precision=HIGH
    )
    line_real, line_imag = (line_real, line_imag)
    lines = jnp.stack([line_real, line_imag], axis=1)
    piece = lax.all_gather(lines, "gx", axis=0, tiled=True)
    freqs = modes_x
    cos_x, sin_x = phase_tables(freqs, places_x, length_x)
    plane_real = jnp.einsum("kx,kyq->xyq", cos_x, piece[:, 0], precision=HIGH) - jnp.einsum(
        "kx,kyq->xyq", sin_x, piece[:, 1], precision=HIGH
    )
    plane_imag = jnp.einsum("kx,kyq->xyq", cos_x, piece[:, 1], precision=HIGH) + jnp.einsum(
        "kx,kyq->xyq", sin_x, piece[:, 0], precision=HIGH
    )
    plane_real, plane_imag = (plane_real, plane_imag)
    count_z = modes_z.shape[0]
    plane_real = plane_real.reshape(rows_x, rows_y, count_z, -1)
    plane_imag = plane_imag.reshape(rows_x, rows_y, count_z, -1)
    cos_z, sin_z = phase_tables(modes_z, jnp.arange(size_z, dtype=jnp.int32), size_z)
    return factor * (
        jnp.einsum("xykc,kz->xyzc", plane_real, cos_z, precision=HIGH)
        - jnp.einsum("xykc,kz->xyzc", plane_imag, sin_z, precision=HIGH)
    )


def plain(features, cotangent, spectral_weight, conv_weight, modes_x, modes_y, modes_z):
    rows_x, rows_y, size_z, chans = features.shape
    count_x, count_y, count_z = (modes_x.shape[0], modes_y.shape[0], modes_z.shape[0])
    length_x = rows_x * lax.axis_size("gx")
    length_y = rows_y * lax.axis_size("gy")
    first = 1.0 / math.sqrt(length_x * length_y * size_z)
    second = 1.0 / math.sqrt(count_x * count_y * count_z)
    spectrum = to_modes(features, first, modes_x, modes_y, modes_z)
    local_y, local_x = (spectrum.shape[0], spectrum.shape[1])
    spec_real = spectrum[:, :, 0].reshape(local_y, local_x, count_z, chans)
    spec_imag = spectrum[:, :, 1].reshape(local_y, local_x, count_z, chans)
    weight = spectral_weight.astype(jnp.float32)
    real_w = weight[:, :, :, 0]
    imag_w = weight[:, :, :, 1]
    form = "abzoi,bazi->bazo"
    mixed_real = jnp.einsum(form, real_w, spec_real, precision=HIGH) - jnp.einsum(
        form, imag_w, spec_imag, precision=HIGH
    )
    mixed_imag = jnp.einsum(form, real_w, spec_imag, precision=HIGH) + jnp.einsum(
        form, imag_w, spec_real, precision=HIGH
    )
    mixed = jnp.stack(
        [mixed_real.reshape(local_y, local_x, -1), mixed_imag.reshape(local_y, local_x, -1)], axis=2
    )
    spectral = to_cells(mixed, second, rows_x, rows_y, size_z, modes_x, modes_y, modes_z)
    flat = features.reshape(-1, chans)
    conv = jnp.dot(flat, conv_weight, preferred_element_type=jnp.float32).reshape(spectral.shape)
    pre = spectral + conv
    cdf = normal_cdf(pre)
    activation = (pre * cdf).astype(jnp.bfloat16)
    slope = (cotangent.astype(jnp.float32) * (cdf + pre * normal_pdf(pre))).astype(jnp.bfloat16)
    back = to_modes(slope, second, modes_x, modes_y, modes_z)
    back_real = back[:, :, 0].reshape(local_y, local_x, count_z, chans)
    back_imag = back[:, :, 1].reshape(local_y, local_x, count_z, chans)
    outer = "bazo,bazi->abzoi"
    grad_real = jnp.einsum(outer, back_real, spec_real, precision=HIGH) + jnp.einsum(
        outer, back_imag, spec_imag, precision=HIGH
    )
    grad_imag = jnp.einsum(outer, back_imag, spec_real, precision=HIGH) - jnp.einsum(
        outer, back_real, spec_imag, precision=HIGH
    )
    grad_spectral = jnp.stack([grad_real, grad_imag], axis=3)
    adjoint = "abzoi,bazo->bazi"
    modes_real = jnp.einsum(adjoint, real_w, back_real, precision=HIGH) + jnp.einsum(
        adjoint, imag_w, back_imag, precision=HIGH
    )
    modes_imag = jnp.einsum(adjoint, real_w, back_imag, precision=HIGH) - jnp.einsum(
        adjoint, imag_w, back_real, precision=HIGH
    )
    back_modes = jnp.stack(
        [modes_real.reshape(local_y, local_x, -1), modes_imag.reshape(local_y, local_x, -1)], axis=2
    )
    spectral_back = to_cells(back_modes, first, rows_x, rows_y, size_z, modes_x, modes_y, modes_z)
    slope_flat = slope.reshape(-1, chans)
    conv_back = jnp.dot(slope_flat, conv_weight.T, preferred_element_type=jnp.float32).reshape(
        spectral.shape
    )
    grad_features = (spectral_back + conv_back).astype(jnp.bfloat16)
    local_conv = jnp.dot(flat.T, slope_flat, preferred_element_type=jnp.float32)
    grad_conv = first * lax.psum(local_conv, ("gx", "gy"))
    return (activation, grad_features, grad_spectral, grad_conv)


def fits(features, spectral_weight):
    rows_x, rows_y, size_z, chans = features.shape
    local_x, local_y, count_z = spectral_weight.shape[:3]
    parts_x, parts_y = lax.axis_size("gx"), lax.axis_size("gy")
    return (
        chans == 64
        and parts_x == 8
        and rows_y == 2 * parts_x
        and local_y == parts_x
        and rows_x * size_z == LANES
        and local_x * count_z == 2 * parts_x
        and parts_y == 4
        and all(n & (n - 1) == 0 for n in (rows_x * parts_x, rows_y * parts_y, size_z))
    )


def shards(features, cotangent, spectral_weight, *rest):
    run = fast if fits(features, spectral_weight) else plain
    return run(features, cotangent, spectral_weight, *rest)


def solution(mesh):
    placed = (
        P("gx", "gy", None, None),
        P("gx", "gy", None, None),
        P("gx", "gy", None, None, None, None),
        P(),
        P(),
        P(),
        P(),
    )
    return jax.shard_map(
        shards,
        mesh=mesh,
        in_specs=placed,
        out_specs=(
            P("gx", "gy", None, None),
            P("gx", "gy", None, None),
            P("gx", "gy", None, None, None, None),
            P(),
        ),
        check_vma=False,
    )
```

```python
import math

import jax
import jax.numpy as jnp
from jax import lax
from jax.experimental import pallas as pl
from jax.experimental.pallas import tpu as pltpu
from jax.sharding import PartitionSpec as P

HIGH = lax.Precision.HIGHEST
BF = jnp.bfloat16
F32 = jnp.float32
LANES = 128
EXTRA = 16
WIDE = 1024
SIDES = 4


def steps_of(parts):
    return list(range(0, parts, 2)) + list(range(1, parts, 2))


def cosine(turns, length):
    half = length // 2
    place = ((turns + length // 4) & (length - 1)) - half
    place = jnp.minimum(jnp.maximum(place, -half - place), half - place)
    angle = place.astype(F32) * (-2.0 * math.pi / length)
    square = angle * angle
    series = 1.0 / 362880.0 - square * (1.0 / 39916800.0)
    series = square * series - 1.0 / 5040.0
    series = square * series + 1.0 / 120.0
    series = square * series - 1.0 / 6.0
    return angle + angle * (square * series)


def pick(ref, index, places):
    out = jnp.zeros(index.shape, jnp.int32)
    for k, place in enumerate(places):
        out = jnp.where(index == k, ref[place], out)
    return out


def store_halves(ref, row, value):
    high = value.astype(BF)
    tall = ref.shape[0] // 2
    ref[row : row + value.shape[0]] = high
    ref[tall + row : tall + row + value.shape[0]] = (value - high.astype(F32)).astype(BF)


def grid_of(rows, cols):
    return (
        lax.broadcasted_iota(jnp.int32, (rows, cols), 0),
        lax.broadcasted_iota(jnp.int32, (rows, cols), 1),
    )


def table_kernel(size_z, *refs):
    sources, outs, places, sems = refs[:4], refs[5:11], refs[11:15], refs[15]
    line_ref, column_ref, cback_ref, lback_ref, pair_ref, turn_ref = outs
    copies = [
        pltpu.make_async_copy(source, place, sems.at[k])
        for k, (source, place) in enumerate(zip(sources, places))
    ]
    for copy in copies:
        copy.start()
    for copy in copies:
        copy.wait()
    mx_ref, my_ref, mz_ref, conv_ref = places
    parts_x, parts_y = lax.axis_size("gx"), lax.axis_size("gy")
    me_x, me_y = lax.axis_index("gx"), lax.axis_index("gy")
    count_x, count_y, count_z = mx_ref.shape[0], my_ref.shape[0], mz_ref.shape[0]
    local_x, local_y = count_x // parts_x, count_y // parts_y
    chans = conv_ref.shape[0]
    block = chans // parts_x
    length_x = line_ref.shape[1] // size_z
    whole = line_ref.shape[1]
    tile = 16

    rows_x = length_x // parts_x
    row, col = grid_of(tile, LANES)
    per = tile // count_z
    quarter = whole // 4
    base = pick(mz_ref, row % count_z, range(count_z)) * (col % size_z) * length_x
    inner = row // count_z
    offset = jnp.zeros(col.shape, jnp.int32)
    for k, step in enumerate(steps_of(parts_x)):
        offset = jnp.where(col == k, (me_x ^ step) * (rows_x * size_z), offset)
    modes = count_x * count_z
    for start in range(0, count_x, per):
        freq = pick(mx_ref, inner, range(start, start + per))
        turns = freq * (col // size_z * size_z) + base
        cos, sin = cosine(turns, whole), cosine(turns - quarter, whole)
        turns = freq * offset
        cos_step, sin_step = cosine(turns, whole), cosine(turns - quarter, whole)
        at = start * count_z
        for k in range(parts_x):
            cos_k = jnp.broadcast_to(cos_step[:, k : k + 1], cos.shape)
            sin_k = jnp.broadcast_to(sin_step[:, k : k + 1], cos.shape)
            columns = line_ref.at[:, k * LANES : (k + 1) * LANES]
            store_halves(columns, at, cos * cos_k - sin * sin_k)
            store_halves(columns, at + modes, -sin * cos_k - cos * sin_k)

    rows_y = column_ref.shape[0] // 4 // block
    length_y = rows_y * parts_y
    per = tile // block
    ky = col // block % local_y
    shift = col // (LANES // 2) * (length_y // 4)
    same = row % block == col % block
    low = col < LANES // 2
    inner = row // block + me_y * rows_y
    for gy in range(parts_y):
        freq = pick(my_ref, ky, range(gy * local_y, (gy + 1) * local_y))
        columns = column_ref.at[:, gy * LANES : (gy + 1) * LANES]
        for start in range(0, rows_y, per):
            value = jnp.where(same, cosine(freq * (inner + start) + shift, length_y), 0.0)
            store_halves(columns, start * block, value)
            turned = pltpu.roll(value, LANES // 2, 1)
            store_halves(columns, (rows_y + start) * block, jnp.where(low, -turned, turned))

    row, col = grid_of(2 * rows_y, cback_ref.shape[1])
    places = [
        (me_y + parts_y - step) % parts_y * local_y + k for step in range(parts_y) for k in range(local_y)
    ]
    freq = pick(my_ref, col // (2 * local_y) * local_y + col % local_y, places)
    shift = (col // local_y % 2 - row // rows_y) * (length_y // 4)
    store_halves(cback_ref, 0, cosine(freq * (row % rows_y + me_y * rows_y) + shift, length_y))

    row, col = grid_of(tile, lback_ref.shape[1])
    modes = local_x * count_z
    kx = col // (2 * modes) * local_x + col // count_z % local_x
    places = [(me_x ^ step) * local_x + k for step in steps_of(parts_x) for k in range(local_x)]
    freq = pick(mx_ref, kx, places) * size_z
    base = pick(mz_ref, col % count_z, range(count_z)) * (row % size_z) * length_x
    base = base + col // modes % 2 * (whole // 4)
    inner = row // size_z + me_x * rows_x
    per = tile // size_z
    for start in range(0, rows_x, per):
        store_halves(lback_ref, start * size_z, cosine(freq * (inner + start) + base, whole))

    conv = conv_ref[...].astype(F32)
    none = jnp.zeros_like(conv)
    for ref, value in ((pair_ref, conv), (turn_ref, conv.T)):
        ref[:chans] = jnp.concatenate([value, none], axis=1).astype(BF)
        ref[chans:] = jnp.concatenate([none, value], axis=1).astype(BF)


def dot(a, b, dims=((1,), (0,))):
    return lax.dot_general(a, b, (dims, ((), ())), preferred_element_type=F32)


def pairs_of(ref):
    size_x, size_y, size_z, chans = ref.shape
    out = []
    for y in range(size_y // 2):
        low = ref[:, y, :, :].astype(F32).reshape(size_x * size_z, chans)
        high = ref[:, y + size_y // 2, :, :].astype(F32).reshape(size_x * size_z, chans)
        out.append(jnp.concatenate([low, high], axis=1))
    return out


def block_transpose(arrays, block):
    count = len(arrays)
    arrays = list(arrays)
    lanes = arrays[0].shape[1]
    index = lax.broadcasted_iota(jnp.int32, arrays[0].shape, 1) // block % count
    step = 1
    while step < count:
        upper = (index & step) != 0
        for p in range(count):
            if p & step:
                continue
            a, b = arrays[p], arrays[p | step]
            arrays[p] = jnp.where(upper, pltpu.roll(b, step * block, 1), a)
            arrays[p | step] = jnp.where(upper, b, pltpu.roll(a, lanes - step * block, 1))
        step *= 2
    return arrays


def split_rows(value):
    high = value.astype(BF)
    return jnp.concatenate([high, (value - high.astype(F32)).astype(BF)], axis=0)


def normal_cdf(values):
    return 0.5 * (1.0 + lax.erf(values * (1.0 / math.sqrt(2.0))))


def normal_pdf(values):
    return jnp.exp(-0.5 * values * values) * (1.0 / math.sqrt(2.0 * math.pi))


def store_steps(chunk_ref, send_refs):
    me = lax.axis_index("gx")
    for t, ref in enumerate(send_refs):
        for r in range(2):
            ref[r] = chunk_ref[me ^ (2 * t + r)]


def spread_kernel(field_ref, *refs):
    send_refs, pairs_ref, chunk_ref = refs[:-2], refs[-2], refs[-1]
    pairs = pairs_of(field_ref)
    for p, pair in enumerate(pairs):
        pairs_ref[p] = pair.astype(BF)
    for b, chunk in enumerate(block_transpose(pairs, field_ref.shape[3] // len(pairs))):
        chunk_ref[b] = chunk.astype(BF)
    store_steps(chunk_ref, send_refs)


def ready_kernel(cot_ref, field_ref, conv_ref, pairs_ref, mapped_ref, turned_ref):
    for p, pair in enumerate(pairs_of(cot_ref)):
        pairs_ref[p] = pair.astype(BF)
        field = field_ref[p]
        mapped_ref[p] = dot(field, conv_ref[...])
        turned_ref[p] = field.astype(F32).T.astype(BF)


def joined(value):
    chans = value.shape[1] // 2
    return value[:, :chans].astype(F32) + value[:, chans:].astype(F32)


def parted(value):
    high = value.astype(BF).astype(F32)
    both = jnp.concatenate([high, value - high], axis=1)
    rest = jnp.zeros((EXTRA - both.shape[0], both.shape[1]), F32)
    return jnp.concatenate([both, rest], axis=0).astype(BF)


def transform_kernel(scale, parts_x, parts_y, line_ref, column_ref, *refs):
    recv_refs, send_ref, extra = refs[:parts_x], refs[parts_x], refs[parts_x + 1 :]
    rows = line_ref.shape[1] // parts_x
    own = [ref.at[k // (parts_x // 2)] for k, ref in enumerate(recv_refs)]
    if extra:
        total = joined(own[0][rows:, :])
        for ref in own[1:]:
            total = total + joined(ref[rows:, :])
        extra[0][...] = parted(total[: LANES // 2 // parts_x])
    data = jnp.concatenate([ref[:rows, :] for ref in own], axis=0)
    half = line_ref.shape[0] // 2
    table = jnp.concatenate([line_ref[:half, :], line_ref[half:, :]], axis=1)
    lines = dot(table, jnp.concatenate([data, data], axis=0))
    count = half // 2
    both = jnp.concatenate([lines[:count], lines[count:]], axis=1)
    depth = both.shape[1]
    high = both.astype(BF)
    low = (both - high.astype(F32)).astype(BF)
    modes = dot(split_rows(both), column_ref[:depth, :])
    modes = modes[:count] + modes[count:] + dot(high, column_ref[depth:, :])
    modes = modes * scale
    tall = count // parts_x
    for gx in range(parts_x):
        for gy in range(parts_y):
            send_ref[gx * parts_y + gy] = modes[
                gx * tall : (gx + 1) * tall, gy * LANES : (gy + 1) * LANES
            ].astype(BF)


def sum_parts(recv_ref, parts_y):
    parts = recv_ref.shape[0] // parts_y
    out = []
    for b in range(parts):
        total = recv_ref[b * parts_y].astype(F32)
        for gy in range(1, parts_y):
            total = total + recv_ref[b * parts_y + gy].astype(F32)
        out.append(total)
    return out


def lay_modes(scratch, send_ref, count_y, rows):
    chans = 64
    for m in range(0, rows, 2):
        parts = []
        for part in range(2):
            first = scratch[pl.ds(part * rows + m, count_y, stride=2 * rows), :chans]
            second = scratch[pl.ds(part * rows + m + 1, count_y, stride=2 * rows), :chans]
            parts.append(jnp.concatenate([first, second], axis=1))
        send_ref[:, m * chans : (m + 2) * chans] = jnp.concatenate(parts, axis=0).astype(send_ref.dtype)


def mix_kernel(forward, parts_y, recv_ref, weight_ref, *refs):
    send_ref, spec_ref, scratch = refs[-3:]
    if len(refs) == 4:
        send_ref[:, WIDE:] = refs[0][...]
    size_x, size_y, size_z, _, chans, _ = weight_ref.shape
    rows = size_x * size_z
    spectra = block_transpose(sum_parts(recv_ref, parts_y), chans // size_y)
    for ky, spec in enumerate(spectra):
        spec_ref[ky] = spec
    if forward:
        group = LANES // (2 * rows)
        for start in range(0, size_y, group):
            both = []
            for spec in spectra[start : start + group]:
                both += [spec, pltpu.roll(spec, chans, 1)]
            both = jnp.concatenate(both, axis=0)[:, :chans].T
            high = both.astype(BF)
            both = jnp.concatenate([high, (both - high.astype(F32)).astype(BF)], axis=1)
            lane = lax.broadcasted_iota(jnp.int32, both.shape, 1) % LANES
            mode = lane // (2 * rows) * rows + lane % rows
            own = [jnp.where(mode == m, both, jnp.zeros_like(both)) for m in range(group * rows)]
            wide = [
                weight_ref[m // size_z, start + ky, m % size_z].reshape(2 * chans, chans)
                for ky in range(group)
                for m in range(rows)
            ]
            wide = [jnp.concatenate(wide[m : m + 2], axis=1) for m in range(0, len(wide), 2)]
            total = dot(jnp.concatenate(wide, axis=1), jnp.concatenate(own, axis=0))
            total = (total[:, :LANES] + total[:, LANES:]).T
            for ky in range(group):
                at = ky * 2 * rows
                real, imag = total[at : at + rows], total[at + rows : at + 2 * rows]
                at += start * 2 * rows
                scratch[at : at + rows, :chans] = real[:, :chans] - imag[:, chans:]
                scratch[at + rows : at + 2 * rows, :chans] = imag[:, :chans] + real[:, chans:]
    else:
        first = lax.broadcasted_iota(jnp.int32, spectra[0].shape, 1) < chans
        for ky, spec in enumerate(spectra):
            turned = pltpu.roll(spec, chans, 1)
            both = split_rows(jnp.concatenate([spec, jnp.where(first, turned, -turned)], axis=0))
            stack = jnp.concatenate(
                [weight_ref[kx, ky].reshape(size_z * 2 * chans, chans) for kx in range(size_x)], axis=0
            )
            mode = lax.broadcasted_iota(jnp.int32, both.shape, 0) % rows
            own = [jnp.where(mode == m, both, jnp.zeros_like(both)) for m in range(rows)]
            total = dot(jnp.concatenate(own, axis=1), stack)
            scratch[ky * 2 * rows : (ky + 1) * 2 * rows, :chans] = total[: 2 * rows] + total[2 * rows :]
    lay_modes(scratch, send_ref, size_y, rows)


def column_kernel(table_ref, *refs):
    steps = len(refs) - 2
    send_ref, scratch = refs[steps], refs[steps + 1]
    chans = 64
    if refs[0].shape[1] > WIDE:
        total = joined(refs[0][:, WIDE:])
        for s in range(1, steps):
            total = total + joined(refs[s][:, WIDE:])
        send_ref[:EXTRA, WIDE:] = parted(total[: EXTRA // 2])
        send_ref[EXTRA:, WIDE:] = jnp.zeros((send_ref.shape[0] - EXTRA, LANES), BF)
    data = jnp.concatenate([refs[s][:, :WIDE] for s in range(steps)], axis=0)
    lines = dot(table_ref[...], data)
    half = lines.shape[0] // 2
    lines = lines[:half] + lines[half:]
    size_y = half // 2
    count = WIDE // chans
    for m in range(0, count, 2):
        pair = lines[:, m * chans : (m + 2) * chans]
        scratch[m * half : (m + 1) * half, :] = pair
        scratch[(m + 1) * half : (m + 2) * half, :] = pltpu.roll(pair, chans, 1)
    for part in range(2):
        for y in range(size_y // 2):
            first = scratch[pl.ds(part * size_y + y, count, stride=half), :chans]
            second = scratch[pl.ds(part * size_y + y + size_y // 2, count, stride=half), :chans]
            send_ref[part * count : (part + 1) * count, y * 2 * chans : (y + 1) * 2 * chans] = (
                jnp.concatenate([first, second], axis=1).astype(BF)
            )


def cells_of(table_ref, recv_refs, scale):
    data = jnp.concatenate([ref[:, :WIDE] for ref in recv_refs], axis=0)
    cells = dot(table_ref[...], data)
    half = cells.shape[0] // 2
    return (cells[:half] + cells[half:]) * scale


def store_pair(out_ref, p, value):
    size_x, size_y, size_z, chans = out_ref.shape
    out_ref[:, p, :, :] = value[:, :chans].reshape(size_x, size_z, chans).astype(out_ref.dtype)
    out_ref[:, p + size_y // 2, :, :] = (
        value[:, chans:].reshape(size_x, size_z, chans).astype(out_ref.dtype)
    )


def point_kernel(scale, table_ref, *refs):
    recv_refs, refs = refs[: 2 * SIDES], refs[2 * SIDES :]
    conv_ref, field_ref, cot_ref, act_ref, slope_ref = refs[:5]
    send_refs, chunk_ref = refs[5:-1], refs[-1]
    cells = cells_of(table_ref, recv_refs, scale)
    count = field_ref.shape[0]
    slopes = []
    grad = jnp.zeros((LANES, LANES), F32)
    for p in range(count):
        field = field_ref[p]
        pre = cells[:, p * LANES : (p + 1) * LANES] + conv_ref[p]
        cdf = normal_cdf(pre)
        act_ref[p] = (pre * cdf).astype(BF)
        slope = cot_ref[p].astype(F32) * (cdf + pre * normal_pdf(pre))
        narrow = slope.astype(BF)
        slope_ref[p] = narrow
        slopes.append(narrow.astype(F32))
        grad = grad + dot(field, narrow)
    rows = slopes[0].shape[0]
    chans = LANES // 2
    grad = grad[:chans, :chans] + grad[chans:, chans:]
    block = chans // count
    for b, chunk in enumerate(block_transpose(slopes, block)):
        chunk_ref[b, :rows, :] = chunk.astype(BF)
        chunk_ref[b, rows:, :] = parted(grad[b * block : (b + 1) * block])
    store_steps(chunk_ref, send_refs)


def unpair_kernel(pairs_ref, out_ref):
    for p in range(pairs_ref.shape[0]):
        store_pair(out_ref, p, pairs_ref[p].astype(F32))


def last_kernel(scale, table_ref, *refs):
    conv_ref, slope_ref, out_ref, grad_ref = refs[-4:]
    recv_refs = refs[:-4]
    block = grad_ref.shape[0] // len(recv_refs)
    me = lax.axis_index("gx")
    for step, ref in zip(steps_of(len(recv_refs)), recv_refs):
        total = joined(ref[:EXTRA, WIDE:])
        grad_ref[pl.ds(pl.multiple_of((me ^ step) * block, block), block), :] = total[:block] * scale
    cells = cells_of(table_ref, recv_refs, scale)
    for p in range(slope_ref.shape[0]):
        store_pair(out_ref, p, cells[:, p * LANES : (p + 1) * LANES] + dot(slope_ref[p], conv_ref[...]))


def outer_kernel(spec_ref, back_ref, out_ref, held_ref, sems):
    size_x, size_y, size_z, _, chans, _ = held_ref.shape
    rows = size_x * size_z
    first = lax.broadcasted_iota(jnp.int32, back_ref.shape[1:], 1) < chans
    mode = lax.broadcasted_iota(jnp.int32, (6 * rows, chans), 0) % rows
    copies = []
    for ky in range(size_y):
        back, spec = back_ref[ky], spec_ref[ky]
        turned = pltpu.roll(back, chans, 1)
        left = jnp.concatenate([back, jnp.where(first, turned, -turned)], axis=0).T
        right = jnp.concatenate([spec, pltpu.roll(spec, chans, 1)], axis=0)[:, :chans]
        left_high, right_high = left.astype(BF), right.astype(BF)
        left_low = (left - left_high.astype(F32)).astype(BF)
        right_low = (right - right_high.astype(F32)).astype(BF)
        lefts = jnp.concatenate([left_high, left_high, left_low], axis=1)
        rights = jnp.concatenate([right_high, right_low, right_high], axis=0)
        for m in range(rows):
            own = jnp.where(mode == m, rights, jnp.zeros_like(rights))
            held_ref[m // size_z, ky, m % size_z] = dot(lefts, own).reshape(2, chans, chans)
        copy = pltpu.make_async_copy(held_ref.at[:, ky], out_ref.at[:, ky], sems.at[ky])
        copy.start()
        copies.append(copy)
    for copy in copies:
        copy.wait()


def call(kernel, outs, *args, scratch=()):
    params = pltpu.CompilerParams(vmem_limit_bytes=16 * 2**20)
    return pl.pallas_call(kernel, out_shape=outs, scratch_shapes=list(scratch), compiler_params=params)(*args)


def bind(kernel, *static):
    def bound(*refs):
        return kernel(*static, *refs)

    return bound


def sds(shape, dtype):
    return jax.ShapeDtypeStruct(shape, dtype)


def fast(features, cotangent, spectral_weight, conv_weight, modes_x, modes_y, modes_z):
    rows_x, rows_y, size_z, chans = features.shape
    local_x, local_y, count_z = spectral_weight.shape[:3]
    parts_x, parts_y = lax.axis_size("gx"), lax.axis_size("gy")
    length_x, length_y = rows_x * parts_x, rows_y * parts_y
    block = chans // parts_x
    cells = rows_x * size_z
    modes = local_x * count_z
    half_y = rows_y // 2
    first = 1.0 / math.sqrt(length_x * length_y * size_z)
    second = 1.0 / math.sqrt(modes_x.shape[0] * modes_y.shape[0] * count_z)

    *send, field = call(
        spread_kernel,
        [sds((2, cells, LANES), BF)] * SIDES + [sds((half_y, cells, LANES), BF)],
        features,
        scratch=[pltpu.VMEM((parts_x, cells, LANES), BF)],
    )
    outside = pl.BlockSpec(memory_space=pltpu.HBM)
    inside = pl.BlockSpec(memory_space=pltpu.VMEM)
    line_table, column_table, column_back, line_back, conv_pair, conv_turn = pl.pallas_call(
        bind(table_kernel, size_z),
        in_specs=[outside] * 5,
        out_shape=(
            sds((4 * modes_x.shape[0] * count_z, length_x * size_z), BF),
            sds((4 * LANES, 4 * LANES), BF),
            sds((4 * rows_y, 2 * modes_y.shape[0]), BF),
            sds((2 * cells, 2 * modes_x.shape[0] * count_z), BF),
            sds((LANES, LANES), BF),
            sds((LANES, LANES), BF),
        ),
        scratch_shapes=[
            pltpu.SMEM(modes_x.shape, jnp.int32),
            pltpu.SMEM(modes_y.shape, jnp.int32),
            pltpu.SMEM(modes_z.shape, jnp.int32),
            pltpu.VMEM(conv_weight.shape, BF),
            pltpu.SemaphoreType.DMA((4,)),
        ],
        compiler_params=pltpu.CompilerParams(vmem_limit_bytes=16 * 2**20),
    )(*(pltpu.with_memory_space_constraint(x, pltpu.HBM) for x in (modes_x, modes_y, modes_z, conv_weight, spectral_weight)))

    def cross(pieces, beside=None):
        pieces = pieces[:1] + [
            lax.ppermute(piece, "gx", [(i, i ^ 2 * t) for i in range(parts_x)])
            for t, piece in enumerate(pieces)
            if t
        ]
        if beside is not None:
            pieces[-1], beside = lax.optimization_barrier((pieces[-1], beside))
        swap = [(i, i ^ 1) for i in range(parts_x)]
        pieces = pieces + [lax.ppermute(piece, "gx", swap) for piece in pieces]
        return pieces, beside

    def to_modes(send, factor, extra, tables):
        outs = [sds((parts_x * parts_y, modes, LANES), BF)]
        if extra:
            outs.append(sds((EXTRA, LANES), BF))
        kernel = bind(transform_kernel, factor, parts_x, parts_y)
        pieces, ready = cross(send, tables)
        tables = ready
        send, *rest = call(kernel, outs, *tables[:2], *pieces)
        return lax.all_to_all(send, ("gx", "gy"), 0, 0, tiled=True), rest, tables

    def mix(recv, forward, rest):
        return call(
            bind(mix_kernel, forward, parts_y),
            (
                sds((2 * local_y, WIDE + len(rest) * LANES), BF),
                sds((local_y, modes, LANES), F32),
            ),
            recv,
            spectral_weight,
            *rest,
            scratch=[pltpu.VMEM((local_y * 2 * modes, LANES), F32)],
        )

    def to_lines(send, beside=None):
        pieces = [send]
        for step in range(1, parts_y):
            ring = [(i, (i + step) % parts_y) for i in range(parts_y)]
            pieces.append(lax.ppermute(send, "gy", ring))
        if beside is not None:
            pieces[-1], beside = lax.optimization_barrier((pieces[-1], beside))
        lines = call(
            column_kernel,
            sds((2 * modes, send.shape[1]), BF),
            column_back,
            *pieces,
            scratch=[pltpu.VMEM((modes * 2 * rows_y, LANES), F32)],
        )
        return cross([lines] * SIDES)[0], beside


    recv, _, tables = to_modes(send, first, False, (line_table, column_table))
    send, spec = mix(recv, True, [])
    pair_shape = (half_y, cells, LANES)
    ready = call(
        ready_kernel,
        (sds(pair_shape, BF), sds(pair_shape, F32), sds((half_y, LANES, cells), BF)),
        cotangent,
        field,
        conv_pair,
    )
    pieces, (cot, mapped, turned) = to_lines(send, ready)
    activation, slope, *send = call(
        bind(point_kernel, second),
        (
            sds(pair_shape, BF),
            sds(pair_shape, BF),
        )
        + (sds((2, cells + EXTRA, LANES), BF),) * SIDES,
        line_back,
        *pieces,
        mapped,
        turned,
        cot,
        scratch=[pltpu.VMEM((parts_x, cells + EXTRA, LANES), BF)],
    )
    activation = call(unpair_kernel, sds(features.shape, BF), activation)
    recv, rest, (_, _, activation) = to_modes(send, second, True, (*tables, activation))
    send, back = mix(recv, False, rest)
    grad_spectral = pl.pallas_call(
        outer_kernel,
        in_specs=[inside] * 2,
        out_specs=outside,
        out_shape=sds(spectral_weight.shape, F32),
        scratch_shapes=[pltpu.VMEM(spectral_weight.shape, F32), pltpu.SemaphoreType.DMA((local_y,))],
        compiler_params=pltpu.CompilerParams(vmem_limit_bytes=16 * 2**20),
    )(spec, back)
    pieces, grad_spectral = to_lines(send, grad_spectral)
    grad_features, grad_conv = call(
        bind(last_kernel, first),
        (sds(features.shape, BF), sds((chans, chans), F32)),
        line_back,
        *pieces,
        conv_turn,
        slope,
    )
    return activation, grad_features, grad_spectral, grad_conv


def phase_tables(freqs, places, length):
    product = freqs[:, None] * places[None, :] % length
    angles = product.astype(jnp.float32) * (2.0 * math.pi / length)
    return (jnp.cos(angles), jnp.sin(angles))


def plane_modes(values, factor, modes_z):
    size_x, size_y, size_z, chans = values.shape
    cos_z, sin_z = phase_tables(modes_z, jnp.arange(size_z, dtype=jnp.int32), size_z)
    wide = values.astype(jnp.float32)
    plane_real = (factor * jnp.einsum("xyzc,kz->xykc", wide, cos_z, precision=HIGH)).reshape(
        size_x, size_y, -1
    )
    plane_imag = (-factor * jnp.einsum("xyzc,kz->xykc", wide, sin_z, precision=HIGH)).reshape(
        size_x, size_y, -1
    )
    return (plane_real, plane_imag)


def line_modes(plane_real, plane_imag, freqs, places, length):
    cos_x, sin_x = phase_tables(freqs, places, length)
    line_real = jnp.einsum("kx,xyq->kyq", cos_x, plane_real, precision=HIGH) + jnp.einsum(
        "kx,xyq->kyq", sin_x, plane_imag, precision=HIGH
    )
    line_imag = jnp.einsum("kx,xyq->kyq", cos_x, plane_imag, precision=HIGH) - jnp.einsum(
        "kx,xyq->kyq", sin_x, plane_real, precision=HIGH
    )
    return jnp.stack([line_real, line_imag], axis=1)


def to_modes(values, factor, modes_x, modes_y, modes_z):
    rows_x, rows_y = (values.shape[0], values.shape[1])
    parts_x = lax.axis_size("gx")
    parts_y = lax.axis_size("gy")
    length_x = rows_x * parts_x
    length_y = rows_y * parts_y
    pencil = lax.all_to_all(values, "gx", split_axis=1, concat_axis=0, tiled=True)
    plane_real, plane_imag = plane_modes(pencil, factor, modes_z)
    whole = line_modes(
        plane_real, plane_imag, modes_x, jnp.arange(length_x, dtype=jnp.int32), length_x
    )
    spectrum = lax.all_to_all(whole, "gx", split_axis=0, concat_axis=2, tiled=True)
    places_y = lax.axis_index("gy") * rows_y + jnp.arange(rows_y, dtype=jnp.int32)
    cos_y, sin_y = phase_tables(modes_y, places_y, length_y)
    mode_real = jnp.einsum("ly,kyq->lkq", cos_y, spectrum[:, 0], precision=HIGH) + jnp.einsum(
        "ly,kyq->lkq", sin_y, spectrum[:, 1], precision=HIGH
    )
    mode_imag = jnp.einsum("ly,kyq->lkq", cos_y, spectrum[:, 1], precision=HIGH) - jnp.einsum(
        "ly,kyq->lkq", sin_y, spectrum[:, 0], precision=HIGH
    )
    return lax.psum_scatter(
        jnp.stack([mode_real, mode_imag], axis=2), "gy", scatter_dimension=0, tiled=True
    )


def to_cells(spectrum, factor, rows_x, rows_y, size_z, modes_x, modes_y, modes_z):
    length_x = rows_x * lax.axis_size("gx")
    length_y = rows_y * lax.axis_size("gy")
    places_y = lax.axis_index("gy") * rows_y + jnp.arange(rows_y, dtype=jnp.int32)
    places_x = lax.axis_index("gx") * rows_x + jnp.arange(rows_x, dtype=jnp.int32)
    piece = lax.all_gather(spectrum, "gy", axis=0, tiled=True)
    freqs = modes_y
    cos_y, sin_y = phase_tables(freqs, places_y, length_y)
    line_real = jnp.einsum("ly,lkq->kyq", cos_y, piece[:, :, 0], precision=HIGH) - jnp.einsum(
        "ly,lkq->kyq", sin_y, piece[:, :, 1], precision=HIGH
    )
    line_imag = jnp.einsum("ly,lkq->kyq", cos_y, piece[:, :, 1], precision=HIGH) + jnp.einsum(
        "ly,lkq->kyq", sin_y, piece[:, :, 0], precision=HIGH
    )
    line_real, line_imag = (line_real, line_imag)
    lines = jnp.stack([line_real, line_imag], axis=1)
    piece = lax.all_gather(lines, "gx", axis=0, tiled=True)
    freqs = modes_x
    cos_x, sin_x = phase_tables(freqs, places_x, length_x)
    plane_real = jnp.einsum("kx,kyq->xyq", cos_x, piece[:, 0], precision=HIGH) - jnp.einsum(
        "kx,kyq->xyq", sin_x, piece[:, 1], precision=HIGH
    )
    plane_imag = jnp.einsum("kx,kyq->xyq", cos_x, piece[:, 1], precision=HIGH) + jnp.einsum(
        "kx,kyq->xyq", sin_x, piece[:, 0], precision=HIGH
    )
    plane_real, plane_imag = (plane_real, plane_imag)
    count_z = modes_z.shape[0]
    plane_real = plane_real.reshape(rows_x, rows_y, count_z, -1)
    plane_imag = plane_imag.reshape(rows_x, rows_y, count_z, -1)
    cos_z, sin_z = phase_tables(modes_z, jnp.arange(size_z, dtype=jnp.int32), size_z)
    return factor * (
        jnp.einsum("xykc,kz->xyzc", plane_real, cos_z, precision=HIGH)
        - jnp.einsum("xykc,kz->xyzc", plane_imag, sin_z, precision=HIGH)
    )


def plain(features, cotangent, spectral_weight, conv_weight, modes_x, modes_y, modes_z):
    rows_x, rows_y, size_z, chans = features.shape
    count_x, count_y, count_z = (modes_x.shape[0], modes_y.shape[0], modes_z.shape[0])
    length_x = rows_x * lax.axis_size("gx")
    length_y = rows_y * lax.axis_size("gy")
    first = 1.0 / math.sqrt(length_x * length_y * size_z)
    second = 1.0 / math.sqrt(count_x * count_y * count_z)
    spectrum = to_modes(features, first, modes_x, modes_y, modes_z)
    local_y, local_x = (spectrum.shape[0], spectrum.shape[1])
    spec_real = spectrum[:, :, 0].reshape(local_y, local_x, count_z, chans)
    spec_imag = spectrum[:, :, 1].reshape(local_y, local_x, count_z, chans)
    weight = spectral_weight.astype(jnp.float32)
    real_w = weight[:, :, :, 0]
    imag_w = weight[:, :, :, 1]
    form = "abzoi,bazi->bazo"
    mixed_real = jnp.einsum(form, real_w, spec_real, precision=HIGH) - jnp.einsum(
        form, imag_w, spec_imag, precision=HIGH
    )
    mixed_imag = jnp.einsum(form, real_w, spec_imag, precision=HIGH) + jnp.einsum(
        form, imag_w, spec_real, precision=HIGH
    )
    mixed = jnp.stack(
        [mixed_real.reshape(local_y, local_x, -1), mixed_imag.reshape(local_y, local_x, -1)], axis=2
    )
    spectral = to_cells(mixed, second, rows_x, rows_y, size_z, modes_x, modes_y, modes_z)
    flat = features.reshape(-1, chans)
    conv = jnp.dot(flat, conv_weight, preferred_element_type=jnp.float32).reshape(spectral.shape)
    pre = spectral + conv
    cdf = normal_cdf(pre)
    activation = (pre * cdf).astype(jnp.bfloat16)
    slope = (cotangent.astype(jnp.float32) * (cdf + pre * normal_pdf(pre))).astype(jnp.bfloat16)
    back = to_modes(slope, second, modes_x, modes_y, modes_z)
    back_real = back[:, :, 0].reshape(local_y, local_x, count_z, chans)
    back_imag = back[:, :, 1].reshape(local_y, local_x, count_z, chans)
    outer = "bazo,bazi->abzoi"
    grad_real = jnp.einsum(outer, back_real, spec_real, precision=HIGH) + jnp.einsum(
        outer, back_imag, spec_imag, precision=HIGH
    )
    grad_imag = jnp.einsum(outer, back_imag, spec_real, precision=HIGH) - jnp.einsum(
        outer, back_real, spec_imag, precision=HIGH
    )
    grad_spectral = jnp.stack([grad_real, grad_imag], axis=3)
    adjoint = "abzoi,bazo->bazi"
    modes_real = jnp.einsum(adjoint, real_w, back_real, precision=HIGH) + jnp.einsum(
        adjoint, imag_w, back_imag, precision=HIGH
    )
    modes_imag = jnp.einsum(adjoint, real_w, back_imag, precision=HIGH) - jnp.einsum(
        adjoint, imag_w, back_real, precision=HIGH
    )
    back_modes = jnp.stack(
        [modes_real.reshape(local_y, local_x, -1), modes_imag.reshape(local_y, local_x, -1)], axis=2
    )
    spectral_back = to_cells(back_modes, first, rows_x, rows_y, size_z, modes_x, modes_y, modes_z)
    slope_flat = slope.reshape(-1, chans)
    conv_back = jnp.dot(slope_flat, conv_weight.T, preferred_element_type=jnp.float32).reshape(
        spectral.shape
    )
    grad_features = (spectral_back + conv_back).astype(jnp.bfloat16)
    local_conv = jnp.dot(flat.T, slope_flat, preferred_element_type=jnp.float32)
    grad_conv = first * lax.psum(local_conv, ("gx", "gy"))
    return (activation, grad_features, grad_spectral, grad_conv)


def fits(features, spectral_weight):
    rows_x, rows_y, size_z, chans = features.shape
    local_x, local_y, count_z = spectral_weight.shape[:3]
    parts_x, parts_y = lax.axis_size("gx"), lax.axis_size("gy")
    return (
        chans == 64
        and parts_x == 8
        and rows_y == 2 * parts_x
        and local_y == parts_x
        and rows_x * size_z == LANES
        and local_x * count_z == 2 * parts_x
        and parts_y == 4
        and all(n & (n - 1) == 0 for n in (rows_x * parts_x, rows_y * parts_y, size_z))
    )


def shards(features, cotangent, spectral_weight, *rest):
    run = fast if fits(features, spectral_weight) else plain
    return run(features, cotangent, spectral_weight, *rest)


def solution(mesh):
    placed = (
        P("gx", "gy", None, None),
        P("gx", "gy", None, None),
        P("gx", "gy", None, None, None, None),
        P(),
        P(),
        P(),
        P(),
    )
    return jax.shard_map(
        shards,
        mesh=mesh,
        in_specs=placed,
        out_specs=(
            P("gx", "gy", None, None),
            P("gx", "gy", None, None),
            P("gx", "gy", None, None, None, None),
            P(),
        ),
        check_vma=False,
    )
```

```python
import math

import jax
import jax.numpy as jnp
from jax import lax
from jax.experimental import pallas as pl
from jax.experimental.pallas import tpu as pltpu
from jax.sharding import PartitionSpec as P

HIGH = lax.Precision.HIGHEST
BF = jnp.bfloat16
F32 = jnp.float32
LANES = 128
EXTRA = 16
WIDE = 1024
SIDES = 4


def steps_of(parts):
    return list(range(0, parts, 2)) + list(range(1, parts, 2))


def cosine(turns, length):
    half = length // 2
    place = ((turns + length // 4) & (length - 1)) - half
    place = jnp.minimum(jnp.maximum(place, -half - place), half - place)
    angle = place.astype(F32) * (-2.0 * math.pi / length)
    square = angle * angle
    series = 1.0 / 362880.0 - square * (1.0 / 39916800.0)
    series = square * series - 1.0 / 5040.0
    series = square * series + 1.0 / 120.0
    series = square * series - 1.0 / 6.0
    return angle + angle * (square * series)


def pick(ref, index, places):
    out = jnp.zeros(index.shape, jnp.int32)
    for k, place in enumerate(places):
        out = jnp.where(index == k, ref[place], out)
    return out


def store_halves(ref, row, value):
    high = value.astype(BF)
    tall = ref.shape[0] // 2
    ref[row : row + value.shape[0]] = high
    ref[tall + row : tall + row + value.shape[0]] = (value - high.astype(F32)).astype(BF)


def grid_of(rows, cols):
    return (
        lax.broadcasted_iota(jnp.int32, (rows, cols), 0),
        lax.broadcasted_iota(jnp.int32, (rows, cols), 1),
    )


def table_kernel(size_z, *refs):
    sources, outs, places, sems = refs[:4], refs[5:11], refs[11:15], refs[15]
    line_ref, column_ref, cback_ref, lback_ref, pair_ref, turn_ref = outs
    copies = [
        pltpu.make_async_copy(source, place, sems.at[k])
        for k, (source, place) in enumerate(zip(sources, places))
    ]
    for copy in copies:
        copy.start()
    for copy in copies:
        copy.wait()
    mx_ref, my_ref, mz_ref, conv_ref = places
    parts_x, parts_y = lax.axis_size("gx"), lax.axis_size("gy")
    me_x, me_y = lax.axis_index("gx"), lax.axis_index("gy")
    count_x, count_y, count_z = mx_ref.shape[0], my_ref.shape[0], mz_ref.shape[0]
    local_x, local_y = count_x // parts_x, count_y // parts_y
    chans = conv_ref.shape[0]
    block = chans // parts_x
    length_x = line_ref.shape[1] // size_z
    whole = line_ref.shape[1]
    tile = 16

    rows_x = length_x // parts_x
    row, col = grid_of(tile, LANES)
    per = tile // count_z
    quarter = whole // 4
    base = pick(mz_ref, row % count_z, range(count_z)) * (col % size_z) * length_x
    inner = row // count_z
    offset = jnp.zeros(col.shape, jnp.int32)
    for k, step in enumerate(steps_of(parts_x)):
        offset = jnp.where(col == k, (me_x ^ step) * (rows_x * size_z), offset)
    modes = count_x * count_z
    for start in range(0, count_x, per):
        freq = pick(mx_ref, inner, range(start, start + per))
        turns = freq * (col // size_z * size_z) + base
        cos, sin = cosine(turns, whole), cosine(turns - quarter, whole)
        turns = freq * offset
        cos_step, sin_step = cosine(turns, whole), cosine(turns - quarter, whole)
        at = start * count_z
        for k in range(parts_x):
            cos_k = jnp.broadcast_to(cos_step[:, k : k + 1], cos.shape)
            sin_k = jnp.broadcast_to(sin_step[:, k : k + 1], cos.shape)
            columns = line_ref.at[:, k * LANES : (k + 1) * LANES]
            store_halves(columns, at, cos * cos_k - sin * sin_k)
            store_halves(columns, at + modes, -sin * cos_k - cos * sin_k)

    rows_y = column_ref.shape[0] // 4 // block
    length_y = rows_y * parts_y
    per = tile // block
    ky = col // block % local_y
    shift = col // (LANES // 2) * (length_y // 4)
    same = row % block == col % block
    low = col < LANES // 2
    inner = row // block + me_y * rows_y
    for gy in range(parts_y):
        freq = pick(my_ref, ky, range(gy * local_y, (gy + 1) * local_y))
        columns = column_ref.at[:, gy * LANES : (gy + 1) * LANES]
        for start in range(0, rows_y, per):
            value = jnp.where(same, cosine(freq * (inner + start) + shift, length_y), 0.0)
            store_halves(columns, start * block, value)
            turned = pltpu.roll(value, LANES // 2, 1)
            store_halves(columns, (rows_y + start) * block, jnp.where(low, -turned, turned))

    row, col = grid_of(2 * rows_y, cback_ref.shape[1])
    places = [
        (me_y + parts_y - step) % parts_y * local_y + k for step in range(parts_y) for k in range(local_y)
    ]
    freq = pick(my_ref, col // (2 * local_y) * local_y + col % local_y, places)
    shift = (col // local_y % 2 - row // rows_y) * (length_y // 4)
    store_halves(cback_ref, 0, cosine(freq * (row % rows_y + me_y * rows_y) + shift, length_y))

    row, col = grid_of(tile, lback_ref.shape[1])
    modes = local_x * count_z
    kx = col // (2 * modes) * local_x + col // count_z % local_x
    places = [(me_x ^ step) * local_x + k for step in steps_of(parts_x) for k in range(local_x)]
    freq = pick(mx_ref, kx, places) * size_z
    base = pick(mz_ref, col % count_z, range(count_z)) * (row % size_z) * length_x
    base = base + col // modes % 2 * (whole // 4)
    inner = row // size_z + me_x * rows_x
    per = tile // size_z
    for start in range(0, rows_x, per):
        store_halves(lback_ref, start * size_z, cosine(freq * (inner + start) + base, whole))

    conv = conv_ref[...].astype(F32)
    none = jnp.zeros_like(conv)
    for ref, value in ((pair_ref, conv), (turn_ref, conv.T)):
        ref[:chans] = jnp.concatenate([value, none], axis=1).astype(BF)
        ref[chans:] = jnp.concatenate([none, value], axis=1).astype(BF)


def dot(a, b, dims=((1,), (0,))):
    return lax.dot_general(a, b, (dims, ((), ())), preferred_element_type=F32)


def pairs_of(ref):
    size_x, size_y, size_z, chans = ref.shape
    out = []
    for y in range(size_y // 2):
        low = ref[:, y, :, :].astype(F32).reshape(size_x * size_z, chans)
        high = ref[:, y + size_y // 2, :, :].astype(F32).reshape(size_x * size_z, chans)
        out.append(jnp.concatenate([low, high], axis=1))
    return out


def block_transpose(arrays, block):
    count = len(arrays)
    arrays = list(arrays)
    lanes = arrays[0].shape[1]
    index = lax.broadcasted_iota(jnp.int32, arrays[0].shape, 1) // block % count
    step = 1
    while step < count:
        upper = (index & step) != 0
        for p in range(count):
            if p & step:
                continue
            a, b = arrays[p], arrays[p | step]
            arrays[p] = jnp.where(upper, pltpu.roll(b, step * block, 1), a)
            arrays[p | step] = jnp.where(upper, b, pltpu.roll(a, lanes - step * block, 1))
        step *= 2
    return arrays


def split_rows(value):
    high = value.astype(BF)
    return jnp.concatenate([high, (value - high.astype(F32)).astype(BF)], axis=0)


def normal_cdf(values):
    return 0.5 * (1.0 + lax.erf(values * (1.0 / math.sqrt(2.0))))


def normal_pdf(values):
    return jnp.exp(-0.5 * values * values) * (1.0 / math.sqrt(2.0 * math.pi))


def store_steps(chunk_ref, send_refs):
    me = lax.axis_index("gx")
    for t, ref in enumerate(send_refs):
        for r in range(2):
            ref[r] = chunk_ref[me ^ (2 * t + r)]


def spread_kernel(field_ref, *refs):
    send_refs, pairs_ref, chunk_ref = refs[:-2], refs[-2], refs[-1]
    pairs = pairs_of(field_ref)
    for p, pair in enumerate(pairs):
        pairs_ref[p] = pair.astype(BF)
    for b, chunk in enumerate(block_transpose(pairs, field_ref.shape[3] // len(pairs))):
        chunk_ref[b] = chunk.astype(BF)
    store_steps(chunk_ref, send_refs)


def ready_kernel(cot_ref, field_ref, conv_ref, pairs_ref, mapped_ref, turned_ref):
    for p, pair in enumerate(pairs_of(cot_ref)):
        pairs_ref[p] = pair.astype(BF)
        field = field_ref[p]
        mapped_ref[p] = dot(field, conv_ref[...])
        turned_ref[p] = field.astype(F32).T.astype(BF)


def joined(value):
    chans = value.shape[1] // 2
    return value[:, :chans].astype(F32) + value[:, chans:].astype(F32)


def parted(value):
    high = value.astype(BF).astype(F32)
    both = jnp.concatenate([high, value - high], axis=1)
    rest = jnp.zeros((EXTRA - both.shape[0], both.shape[1]), F32)
    return jnp.concatenate([both, rest], axis=0).astype(BF)


def transform_kernel(scale, parts_x, parts_y, line_ref, column_ref, *refs):
    recv_refs, send_ref, extra = refs[:parts_x], refs[parts_x], refs[parts_x + 1 :]
    rows = line_ref.shape[1] // parts_x
    own = [ref.at[k // (parts_x // 2)] for k, ref in enumerate(recv_refs)]
    if extra:
        total = joined(own[0][rows:, :])
        for ref in own[1:]:
            total = total + joined(ref[rows:, :])
        extra[0][...] = parted(total[: LANES // 2 // parts_x])
    data = jnp.concatenate([ref[:rows, :] for ref in own], axis=0)
    half = line_ref.shape[0] // 2
    table = jnp.concatenate([line_ref[:half, :], line_ref[half:, :]], axis=1)
    lines = dot(table, jnp.concatenate([data, data], axis=0))
    count = half // 2
    both = jnp.concatenate([lines[:count], lines[count:]], axis=1)
    depth = both.shape[1]
    high = both.astype(BF)
    low = (both - high.astype(F32)).astype(BF)
    modes = dot(split_rows(both), column_ref[:depth, :])
    modes = modes[:count] + modes[count:] + dot(high, column_ref[depth:, :])
    modes = modes * scale
    tall = count // parts_x
    for gx in range(parts_x):
        for gy in range(parts_y):
            send_ref[gx * parts_y + gy] = modes[
                gx * tall : (gx + 1) * tall, gy * LANES : (gy + 1) * LANES
            ].astype(BF)


def sum_parts(recv_ref, parts_y):
    parts = recv_ref.shape[0] // parts_y
    out = []
    for b in range(parts):
        total = recv_ref[b * parts_y].astype(F32)
        for gy in range(1, parts_y):
            total = total + recv_ref[b * parts_y + gy].astype(F32)
        out.append(total)
    return out


def lay_modes(scratch, send_ref, count_y, rows):
    chans = 64
    for m in range(0, rows, 2):
        parts = []
        for part in range(2):
            first = scratch[pl.ds(part * rows + m, count_y, stride=2 * rows), :chans]
            second = scratch[pl.ds(part * rows + m + 1, count_y, stride=2 * rows), :chans]
            parts.append(jnp.concatenate([first, second], axis=1))
        send_ref[:, m * chans : (m + 2) * chans] = jnp.concatenate(parts, axis=0).astype(send_ref.dtype)


def mix_kernel(forward, parts_y, recv_ref, weight_ref, *refs):
    send_ref, spec_ref, scratch = refs[-3:]
    if len(refs) == 4:
        send_ref[:, WIDE:] = refs[0][...]
    size_x, size_y, size_z, _, chans, _ = weight_ref.shape
    rows = size_x * size_z
    spectra = block_transpose(sum_parts(recv_ref, parts_y), chans // size_y)
    for ky, spec in enumerate(spectra):
        spec_ref[ky] = spec
    if forward:
        group = LANES // (2 * rows)
        for start in range(0, size_y, group):
            both = []
            for spec in spectra[start : start + group]:
                both += [spec, pltpu.roll(spec, chans, 1)]
            both = jnp.concatenate(both, axis=0)[:, :chans].T
            high = both.astype(BF)
            both = jnp.concatenate([high, (both - high.astype(F32)).astype(BF)], axis=1)
            lane = lax.broadcasted_iota(jnp.int32, both.shape, 1) % LANES
            mode = lane // (2 * rows) * rows + lane % rows
            own = [jnp.where(mode == m, both, jnp.zeros_like(both)) for m in range(group * rows)]
            wide = [
                weight_ref[m // size_z, start + ky, m % size_z].reshape(2 * chans, chans)
                for ky in range(group)
                for m in range(rows)
            ]
            wide = [jnp.concatenate(wide[m : m + 2], axis=1) for m in range(0, len(wide), 2)]
            total = dot(jnp.concatenate(wide, axis=1), jnp.concatenate(own, axis=0))
            total = (total[:, :LANES] + total[:, LANES:]).T
            for ky in range(group):
                at = ky * 2 * rows
                real, imag = total[at : at + rows], total[at + rows : at + 2 * rows]
                at += start * 2 * rows
                scratch[at : at + rows, :chans] = real[:, :chans] - imag[:, chans:]
                scratch[at + rows : at + 2 * rows, :chans] = imag[:, :chans] + real[:, chans:]
    else:
        first = lax.broadcasted_iota(jnp.int32, spectra[0].shape, 1) < chans
        for ky, spec in enumerate(spectra):
            turned = pltpu.roll(spec, chans, 1)
            both = split_rows(jnp.concatenate([spec, jnp.where(first, turned, -turned)], axis=0))
            stack = jnp.concatenate(
                [weight_ref[kx, ky].reshape(size_z * 2 * chans, chans) for kx in range(size_x)], axis=0
            )
            mode = lax.broadcasted_iota(jnp.int32, both.shape, 0) % rows
            own = [jnp.where(mode == m, both, jnp.zeros_like(both)) for m in range(rows)]
            total = dot(jnp.concatenate(own, axis=1), stack)
            scratch[ky * 2 * rows : (ky + 1) * 2 * rows, :chans] = total[: 2 * rows] + total[2 * rows :]
    lay_modes(scratch, send_ref, size_y, rows)


def column_kernel(table_ref, *refs):
    steps = len(refs) - 2
    send_ref, scratch = refs[steps], refs[steps + 1]
    chans = 64
    if refs[0].shape[1] > WIDE:
        total = joined(refs[0][:, WIDE:])
        for s in range(1, steps):
            total = total + joined(refs[s][:, WIDE:])
        send_ref[:EXTRA, WIDE:] = parted(total[: EXTRA // 2])
        send_ref[EXTRA:, WIDE:] = jnp.zeros((send_ref.shape[0] - EXTRA, LANES), BF)
    data = jnp.concatenate([refs[s][:, :WIDE] for s in range(steps)], axis=0)
    lines = dot(table_ref[...], data)
    half = lines.shape[0] // 2
    lines = lines[:half] + lines[half:]
    size_y = half // 2
    count = WIDE // chans
    for m in range(0, count, 2):
        pair = lines[:, m * chans : (m + 2) * chans]
        scratch[m * half : (m + 1) * half, :] = pair
        scratch[(m + 1) * half : (m + 2) * half, :] = pltpu.roll(pair, chans, 1)
    for part in range(2):
        for y in range(size_y // 2):
            first = scratch[pl.ds(part * size_y + y, count, stride=half), :chans]
            second = scratch[pl.ds(part * size_y + y + size_y // 2, count, stride=half), :chans]
            send_ref[part * count : (part + 1) * count, y * 2 * chans : (y + 1) * 2 * chans] = (
                jnp.concatenate([first, second], axis=1).astype(BF)
            )


def cells_of(table_ref, recv_refs, scale):
    data = jnp.concatenate([ref[:, :WIDE] for ref in recv_refs], axis=0)
    cells = dot(table_ref[...], data)
    half = cells.shape[0] // 2
    return (cells[:half] + cells[half:]) * scale


def store_pair(out_ref, p, value):
    size_x, size_y, size_z, chans = out_ref.shape
    out_ref[:, p, :, :] = value[:, :chans].reshape(size_x, size_z, chans).astype(out_ref.dtype)
    out_ref[:, p + size_y // 2, :, :] = (
        value[:, chans:].reshape(size_x, size_z, chans).astype(out_ref.dtype)
    )


def point_kernel(scale, table_ref, *refs):
    recv_refs, refs = refs[: 2 * SIDES], refs[2 * SIDES :]
    conv_ref, field_ref, cot_ref, act_ref, slope_ref = refs[:5]
    send_refs, chunk_ref = refs[5:-1], refs[-1]
    cells = cells_of(table_ref, recv_refs, scale)
    count = field_ref.shape[0]
    slopes = []
    grad = jnp.zeros((LANES, LANES), F32)
    for p in range(count):
        field = field_ref[p]
        pre = cells[:, p * LANES : (p + 1) * LANES] + conv_ref[p]
        cdf = normal_cdf(pre)
        act_ref[p] = (pre * cdf).astype(BF)
        slope = cot_ref[p].astype(F32) * (cdf + pre * normal_pdf(pre))
        narrow = slope.astype(BF)
        slope_ref[p] = narrow
        slopes.append(narrow.astype(F32))
        grad = grad + dot(field, narrow)
    rows = slopes[0].shape[0]
    chans = LANES // 2
    grad = grad[:chans, :chans] + grad[chans:, chans:]
    block = chans // count
    for b, chunk in enumerate(block_transpose(slopes, block)):
        chunk_ref[b, :rows, :] = chunk.astype(BF)
        chunk_ref[b, rows:, :] = parted(grad[b * block : (b + 1) * block])
    store_steps(chunk_ref, send_refs)


def unpair_kernel(pairs_ref, slope_ref, conv_ref, out_ref, turned_ref):
    for p in range(pairs_ref.shape[0]):
        turned_ref[p] = dot(slope_ref[p], conv_ref[...])
        store_pair(out_ref, p, pairs_ref[p].astype(F32))


def last_kernel(scale, table_ref, *refs):
    slope_ref, out_ref, grad_ref = refs[-3:]
    recv_refs = refs[:-3]
    block = grad_ref.shape[0] // len(recv_refs)
    me = lax.axis_index("gx")
    for step, ref in zip(steps_of(len(recv_refs)), recv_refs):
        total = joined(ref[:EXTRA, WIDE:])
        grad_ref[pl.ds(pl.multiple_of((me ^ step) * block, block), block), :] = total[:block] * scale
    cells = cells_of(table_ref, recv_refs, scale)
    for p in range(slope_ref.shape[0]):
        store_pair(out_ref, p, cells[:, p * LANES : (p + 1) * LANES] + slope_ref[p])


def outer_kernel(spec_ref, back_ref, out_ref, held_ref, sems):
    size_x, size_y, size_z, _, chans, _ = held_ref.shape
    rows = size_x * size_z
    first = lax.broadcasted_iota(jnp.int32, back_ref.shape[1:], 1) < chans
    mode = lax.broadcasted_iota(jnp.int32, (6 * rows, chans), 0) % rows
    copies = []
    for ky in range(size_y):
        back, spec = back_ref[ky], spec_ref[ky]
        turned = pltpu.roll(back, chans, 1)
        left = jnp.concatenate([back, jnp.where(first, turned, -turned)], axis=0).T
        right = jnp.concatenate([spec, pltpu.roll(spec, chans, 1)], axis=0)[:, :chans]
        left_high, right_high = left.astype(BF), right.astype(BF)
        left_low = (left - left_high.astype(F32)).astype(BF)
        right_low = (right - right_high.astype(F32)).astype(BF)
        lefts = jnp.concatenate([left_high, left_high, left_low], axis=1)
        rights = jnp.concatenate([right_high, right_low, right_high], axis=0)
        for m in range(rows):
            own = jnp.where(mode == m, rights, jnp.zeros_like(rights))
            held_ref[m // size_z, ky, m % size_z] = dot(lefts, own).reshape(2, chans, chans)
        copy = pltpu.make_async_copy(held_ref.at[:, ky], out_ref.at[:, ky], sems.at[ky])
        copy.start()
        copies.append(copy)
    for copy in copies:
        copy.wait()


def call(kernel, outs, *args, scratch=()):
    params = pltpu.CompilerParams(vmem_limit_bytes=16 * 2**20)
    return pl.pallas_call(kernel, out_shape=outs, scratch_shapes=list(scratch), compiler_params=params)(*args)


def bind(kernel, *static):
    def bound(*refs):
        return kernel(*static, *refs)

    return bound


def sds(shape, dtype):
    return jax.ShapeDtypeStruct(shape, dtype)


def fast(features, cotangent, spectral_weight, conv_weight, modes_x, modes_y, modes_z):
    rows_x, rows_y, size_z, chans = features.shape
    local_x, local_y, count_z = spectral_weight.shape[:3]
    parts_x, parts_y = lax.axis_size("gx"), lax.axis_size("gy")
    length_x, length_y = rows_x * parts_x, rows_y * parts_y
    block = chans // parts_x
    cells = rows_x * size_z
    modes = local_x * count_z
    half_y = rows_y // 2
    first = 1.0 / math.sqrt(length_x * length_y * size_z)
    second = 1.0 / math.sqrt(modes_x.shape[0] * modes_y.shape[0] * count_z)

    *send, field = call(
        spread_kernel,
        [sds((2, cells, LANES), BF)] * SIDES + [sds((half_y, cells, LANES), BF)],
        features,
        scratch=[pltpu.VMEM((parts_x, cells, LANES), BF)],
    )
    outside = pl.BlockSpec(memory_space=pltpu.HBM)
    inside = pl.BlockSpec(memory_space=pltpu.VMEM)
    line_table, column_table, column_back, line_back, conv_pair, conv_turn = pl.pallas_call(
        bind(table_kernel, size_z),
        in_specs=[outside] * 5,
        out_shape=(
            sds((4 * modes_x.shape[0] * count_z, length_x * size_z), BF),
            sds((4 * LANES, 4 * LANES), BF),
            sds((4 * rows_y, 2 * modes_y.shape[0]), BF),
            sds((2 * cells, 2 * modes_x.shape[0] * count_z), BF),
            sds((LANES, LANES), BF),
            sds((LANES, LANES), BF),
        ),
        scratch_shapes=[
            pltpu.SMEM(modes_x.shape, jnp.int32),
            pltpu.SMEM(modes_y.shape, jnp.int32),
            pltpu.SMEM(modes_z.shape, jnp.int32),
            pltpu.VMEM(conv_weight.shape, BF),
            pltpu.SemaphoreType.DMA((4,)),
        ],
        compiler_params=pltpu.CompilerParams(vmem_limit_bytes=16 * 2**20),
    )(*(pltpu.with_memory_space_constraint(x, pltpu.HBM) for x in (modes_x, modes_y, modes_z, conv_weight, spectral_weight)))

    def cross(pieces, beside=None):
        pieces = pieces[:1] + [
            lax.ppermute(piece, "gx", [(i, i ^ 2 * t) for i in range(parts_x)])
            for t, piece in enumerate(pieces)
            if t
        ]
        if beside is not None:
            pieces[-1], beside = lax.optimization_barrier((pieces[-1], beside))
        swap = [(i, i ^ 1) for i in range(parts_x)]
        pieces = pieces + [lax.ppermute(piece, "gx", swap) for piece in pieces]
        return pieces, beside

    def to_modes(send, factor, extra, tables):
        outs = [sds((parts_x * parts_y, modes, LANES), BF)]
        if extra:
            outs.append(sds((EXTRA, LANES), BF))
        kernel = bind(transform_kernel, factor, parts_x, parts_y)
        pieces, ready = cross(send, tables)
        tables = ready
        send, *rest = call(kernel, outs, *tables[:2], *pieces)
        return lax.all_to_all(send, ("gx", "gy"), 0, 0, tiled=True), rest, tables

    def mix(recv, forward, rest):
        return call(
            bind(mix_kernel, forward, parts_y),
            (
                sds((2 * local_y, WIDE + len(rest) * LANES), BF),
                sds((local_y, modes, LANES), F32),
            ),
            recv,
            spectral_weight,
            *rest,
            scratch=[pltpu.VMEM((local_y * 2 * modes, LANES), F32)],
        )

    def to_lines(send, beside=None):
        pieces = [send]
        for step in range(1, parts_y):
            ring = [(i, (i + step) % parts_y) for i in range(parts_y)]
            pieces.append(lax.ppermute(send, "gy", ring))
        if beside is not None:
            pieces[-1], beside = lax.optimization_barrier((pieces[-1], beside))
        lines = call(
            column_kernel,
            sds((2 * modes, send.shape[1]), BF),
            column_back,
            *pieces,
            scratch=[pltpu.VMEM((modes * 2 * rows_y, LANES), F32)],
        )
        return cross([lines] * SIDES)[0], beside


    recv, _, tables = to_modes(send, first, False, (line_table, column_table))
    send, spec = mix(recv, True, [])
    pair_shape = (half_y, cells, LANES)
    ready = call(
        ready_kernel,
        (sds(pair_shape, BF), sds(pair_shape, F32), sds((half_y, LANES, cells), BF)),
        cotangent,
        field,
        conv_pair,
    )
    pieces, (cot, mapped, turned) = to_lines(send, ready)
    activation, slope, *send = call(
        bind(point_kernel, second),
        (
            sds(pair_shape, BF),
            sds(pair_shape, BF),
        )
        + (sds((2, cells + EXTRA, LANES), BF),) * SIDES,
        line_back,
        *pieces,
        mapped,
        turned,
        cot,
        scratch=[pltpu.VMEM((parts_x, cells + EXTRA, LANES), BF)],
    )
    laid = call(
        unpair_kernel, (sds(features.shape, BF), sds(pair_shape, F32)), activation, slope, conv_turn
    )
    recv, rest, (_, _, (activation, turned)) = to_modes(send, second, True, (*tables, tuple(laid)))
    send, back = mix(recv, False, rest)
    grad_spectral = pl.pallas_call(
        outer_kernel,
        in_specs=[inside] * 2,
        out_specs=outside,
        out_shape=sds(spectral_weight.shape, F32),
        scratch_shapes=[pltpu.VMEM(spectral_weight.shape, F32), pltpu.SemaphoreType.DMA((local_y,))],
        compiler_params=pltpu.CompilerParams(vmem_limit_bytes=16 * 2**20),
    )(spec, back)
    pieces, grad_spectral = to_lines(send, grad_spectral)
    grad_features, grad_conv = call(
        bind(last_kernel, first),
        (sds(features.shape, BF), sds((chans, chans), F32)),
        line_back,
        *pieces,
        turned,
    )
    return activation, grad_features, grad_spectral, grad_conv


def phase_tables(freqs, places, length):
    product = freqs[:, None] * places[None, :] % length
    angles = product.astype(jnp.float32) * (2.0 * math.pi / length)
    return (jnp.cos(angles), jnp.sin(angles))


def plane_modes(values, factor, modes_z):
    size_x, size_y, size_z, chans = values.shape
    cos_z, sin_z = phase_tables(modes_z, jnp.arange(size_z, dtype=jnp.int32), size_z)
    wide = values.astype(jnp.float32)
    plane_real = (factor * jnp.einsum("xyzc,kz->xykc", wide, cos_z, precision=HIGH)).reshape(
        size_x, size_y, -1
    )
    plane_imag = (-factor * jnp.einsum("xyzc,kz->xykc", wide, sin_z, precision=HIGH)).reshape(
        size_x, size_y, -1
    )
    return (plane_real, plane_imag)


def line_modes(plane_real, plane_imag, freqs, places, length):
    cos_x, sin_x = phase_tables(freqs, places, length)
    line_real = jnp.einsum("kx,xyq->kyq", cos_x, plane_real, precision=HIGH) + jnp.einsum(
        "kx,xyq->kyq", sin_x, plane_imag, precision=HIGH
    )
    line_imag = jnp.einsum("kx,xyq->kyq", cos_x, plane_imag, precision=HIGH) - jnp.einsum(
        "kx,xyq->kyq", sin_x, plane_real, precision=HIGH
    )
    return jnp.stack([line_real, line_imag], axis=1)


def to_modes(values, factor, modes_x, modes_y, modes_z):
    rows_x, rows_y = (values.shape[0], values.shape[1])
    parts_x = lax.axis_size("gx")
    parts_y = lax.axis_size("gy")
    length_x = rows_x * parts_x
    length_y = rows_y * parts_y
    pencil = lax.all_to_all(values, "gx", split_axis=1, concat_axis=0, tiled=True)
    plane_real, plane_imag = plane_modes(pencil, factor, modes_z)
    whole = line_modes(
        plane_real, plane_imag, modes_x, jnp.arange(length_x, dtype=jnp.int32), length_x
    )
    spectrum = lax.all_to_all(whole, "gx", split_axis=0, concat_axis=2, tiled=True)
    places_y = lax.axis_index("gy") * rows_y + jnp.arange(rows_y, dtype=jnp.int32)
    cos_y, sin_y = phase_tables(modes_y, places_y, length_y)
    mode_real = jnp.einsum("ly,kyq->lkq", cos_y, spectrum[:, 0], precision=HIGH) + jnp.einsum(
        "ly,kyq->lkq", sin_y, spectrum[:, 1], precision=HIGH
    )
    mode_imag = jnp.einsum("ly,kyq->lkq", cos_y, spectrum[:, 1], precision=HIGH) - jnp.einsum(
        "ly,kyq->lkq", sin_y, spectrum[:, 0], precision=HIGH
    )
    return lax.psum_scatter(
        jnp.stack([mode_real, mode_imag], axis=2), "gy", scatter_dimension=0, tiled=True
    )


def to_cells(spectrum, factor, rows_x, rows_y, size_z, modes_x, modes_y, modes_z):
    length_x = rows_x * lax.axis_size("gx")
    length_y = rows_y * lax.axis_size("gy")
    places_y = lax.axis_index("gy") * rows_y + jnp.arange(rows_y, dtype=jnp.int32)
    places_x = lax.axis_index("gx") * rows_x + jnp.arange(rows_x, dtype=jnp.int32)
    piece = lax.all_gather(spectrum, "gy", axis=0, tiled=True)
    freqs = modes_y
    cos_y, sin_y = phase_tables(freqs, places_y, length_y)
    line_real = jnp.einsum("ly,lkq->kyq", cos_y, piece[:, :, 0], precision=HIGH) - jnp.einsum(
        "ly,lkq->kyq", sin_y, piece[:, :, 1], precision=HIGH
    )
    line_imag = jnp.einsum("ly,lkq->kyq", cos_y, piece[:, :, 1], precision=HIGH) + jnp.einsum(
        "ly,lkq->kyq", sin_y, piece[:, :, 0], precision=HIGH
    )
    line_real, line_imag = (line_real, line_imag)
    lines = jnp.stack([line_real, line_imag], axis=1)
    piece = lax.all_gather(lines, "gx", axis=0, tiled=True)
    freqs = modes_x
    cos_x, sin_x = phase_tables(freqs, places_x, length_x)
    plane_real = jnp.einsum("kx,kyq->xyq", cos_x, piece[:, 0], precision=HIGH) - jnp.einsum(
        "kx,kyq->xyq", sin_x, piece[:, 1], precision=HIGH
    )
    plane_imag = jnp.einsum("kx,kyq->xyq", cos_x, piece[:, 1], precision=HIGH) + jnp.einsum(
        "kx,kyq->xyq", sin_x, piece[:, 0], precision=HIGH
    )
    plane_real, plane_imag = (plane_real, plane_imag)
    count_z = modes_z.shape[0]
    plane_real = plane_real.reshape(rows_x, rows_y, count_z, -1)
    plane_imag = plane_imag.reshape(rows_x, rows_y, count_z, -1)
    cos_z, sin_z = phase_tables(modes_z, jnp.arange(size_z, dtype=jnp.int32), size_z)
    return factor * (
        jnp.einsum("xykc,kz->xyzc", plane_real, cos_z, precision=HIGH)
        - jnp.einsum("xykc,kz->xyzc", plane_imag, sin_z, precision=HIGH)
    )


def plain(features, cotangent, spectral_weight, conv_weight, modes_x, modes_y, modes_z):
    rows_x, rows_y, size_z, chans = features.shape
    count_x, count_y, count_z = (modes_x.shape[0], modes_y.shape[0], modes_z.shape[0])
    length_x = rows_x * lax.axis_size("gx")
    length_y = rows_y * lax.axis_size("gy")
    first = 1.0 / math.sqrt(length_x * length_y * size_z)
    second = 1.0 / math.sqrt(count_x * count_y * count_z)
    spectrum = to_modes(features, first, modes_x, modes_y, modes_z)
    local_y, local_x = (spectrum.shape[0], spectrum.shape[1])
    spec_real = spectrum[:, :, 0].reshape(local_y, local_x, count_z, chans)
    spec_imag = spectrum[:, :, 1].reshape(local_y, local_x, count_z, chans)
    weight = spectral_weight.astype(jnp.float32)
    real_w = weight[:, :, :, 0]
    imag_w = weight[:, :, :, 1]
    form = "abzoi,bazi->bazo"
    mixed_real = jnp.einsum(form, real_w, spec_real, precision=HIGH) - jnp.einsum(
        form, imag_w, spec_imag, precision=HIGH
    )
    mixed_imag = jnp.einsum(form, real_w, spec_imag, precision=HIGH) + jnp.einsum(
        form, imag_w, spec_real, precision=HIGH
    )
    mixed = jnp.stack(
        [mixed_real.reshape(local_y, local_x, -1), mixed_imag.reshape(local_y, local_x, -1)], axis=2
    )
    spectral = to_cells(mixed, second, rows_x, rows_y, size_z, modes_x, modes_y, modes_z)
    flat = features.reshape(-1, chans)
    conv = jnp.dot(flat, conv_weight, preferred_element_type=jnp.float32).reshape(spectral.shape)
    pre = spectral + conv
    cdf = normal_cdf(pre)
    activation = (pre * cdf).astype(jnp.bfloat16)
    slope = (cotangent.astype(jnp.float32) * (cdf + pre * normal_pdf(pre))).astype(jnp.bfloat16)
    back = to_modes(slope, second, modes_x, modes_y, modes_z)
    back_real = back[:, :, 0].reshape(local_y, local_x, count_z, chans)
    back_imag = back[:, :, 1].reshape(local_y, local_x, count_z, chans)
    outer = "bazo,bazi->abzoi"
    grad_real = jnp.einsum(outer, back_real, spec_real, precision=HIGH) + jnp.einsum(
        outer, back_imag, spec_imag, precision=HIGH
    )
    grad_imag = jnp.einsum(outer, back_imag, spec_real, precision=HIGH) - jnp.einsum(
        outer, back_real, spec_imag, precision=HIGH
    )
    grad_spectral = jnp.stack([grad_real, grad_imag], axis=3)
    adjoint = "abzoi,bazo->bazi"
    modes_real = jnp.einsum(adjoint, real_w, back_real, precision=HIGH) + jnp.einsum(
        adjoint, imag_w, back_imag, precision=HIGH
    )
    modes_imag = jnp.einsum(adjoint, real_w, back_imag, precision=HIGH) - jnp.einsum(
        adjoint, imag_w, back_real, precision=HIGH
    )
    back_modes = jnp.stack(
        [modes_real.reshape(local_y, local_x, -1), modes_imag.reshape(local_y, local_x, -1)], axis=2
    )
    spectral_back = to_cells(back_modes, first, rows_x, rows_y, size_z, modes_x, modes_y, modes_z)
    slope_flat = slope.reshape(-1, chans)
    conv_back = jnp.dot(slope_flat, conv_weight.T, preferred_element_type=jnp.float32).reshape(
        spectral.shape
    )
    grad_features = (spectral_back + conv_back).astype(jnp.bfloat16)
    local_conv = jnp.dot(flat.T, slope_flat, preferred_element_type=jnp.float32)
    grad_conv = first * lax.psum(local_conv, ("gx", "gy"))
    return (activation, grad_features, grad_spectral, grad_conv)


def fits(features, spectral_weight):
    rows_x, rows_y, size_z, chans = features.shape
    local_x, local_y, count_z = spectral_weight.shape[:3]
    parts_x, parts_y = lax.axis_size("gx"), lax.axis_size("gy")
    return (
        chans == 64
        and parts_x == 8
        and rows_y == 2 * parts_x
        and local_y == parts_x
        and rows_x * size_z == LANES
        and local_x * count_z == 2 * parts_x
        and parts_y == 4
        and all(n & (n - 1) == 0 for n in (rows_x * parts_x, rows_y * parts_y, size_z))
    )


def shards(features, cotangent, spectral_weight, *rest):
    run = fast if fits(features, spectral_weight) else plain
    return run(features, cotangent, spectral_weight, *rest)


def solution(mesh):
    placed = (
        P("gx", "gy", None, None),
        P("gx", "gy", None, None),
        P("gx", "gy", None, None, None, None),
        P(),
        P(),
        P(),
        P(),
    )
    return jax.shard_map(
        shards,
        mesh=mesh,
        in_specs=placed,
        out_specs=(
            P("gx", "gy", None, None),
            P("gx", "gy", None, None),
            P("gx", "gy", None, None, None, None),
            P(),
        ),
        check_vma=False,
    )
```
